32 devices in a mesh: batch: 8 (over z, y), grp: 4 (over x, core).
Axes of the slice: x: 2, y: 2, z: 4, core: 2. Of those that a mesh axis runs over, the one named last changes fastest.
Arguments:
- tokens: bfloat16 [8192, 768], P(('batch', 'grp')), may hold values from -6 to 6
- dest: int32 [8192, 1], P(('batch', 'grp')), may hold values from 0 to 7; in each aligned block of 256 rows (0 to 255, 256 to 511, ...) at most 64 rows name the same one
- seg_ids: int32 [32, 512], P(('batch', 'grp')), may hold values from 0 to 7, never falling along the last dimension, each value on 1 to 128 neighbouring positions
- cot_out: bfloat16 [8192, 768], P(('batch', 'grp')), may hold values from -6 to 6
- cot_align: bfloat16 [8192, 1024], P(('batch', 'grp')), may hold values from -6 to 6
- ln1_gain: bfloat16 [768], replicated, may hold values from 0.5 to 1.5
- ln1_bias: bfloat16 [768], replicated, may hold values from -1 to 1
- w_qkv: bfloat16 [768, 2304], replicated, may hold values from -0.21875 to 0.21875
- q_bias: bfloat16 [768], replicated, may hold values from -1 to 1
- v_bias: bfloat16 [768], replicated, may hold values from -1 to 1
- w_out: bfloat16 [768, 768], replicated, may hold values from -1.75 to 1.75
- out_bias: bfloat16 [768], replicated, may hold values from -1 to 1
- ln2_gain: bfloat16 [768], replicated, may hold values from 0.5 to 1.5
- ln2_bias: bfloat16 [768], replicated, may hold values from -1 to 1
- w_up: bfloat16 [768, 3072], replicated, may hold values from -0.21875 to 0.21875
- up_bias: bfloat16 [3072], replicated, may hold values from -1 to 1
- w_down: bfloat16 [3072, 768], replicated, may hold values from -0.109375 to 0.109375
- down_bias: bfloat16 [768], replicated, may hold values from -1 to 1
- ln3_gain: bfloat16 [768], replicated, may hold values from 0.5 to 1.5
- ln3_bias: bfloat16 [768], replicated, may hold values from -1 to 1
- w_align: bfloat16 [768, 1024], replicated, may hold values from -0.21875 to 0.21875
- align_bias: bfloat16 [1024], replicated, may hold values from -1 to 1
Outputs:
- out_tokens: bfloat16 [8192, 768], P(('batch', 'grp'))
- aligned_tokens: bfloat16 [8192, 1024], P(('batch', 'grp'))
- grad_tokens: bfloat16 [8192, 768], P(('batch', 'grp'))
- grad_ln1_gain: float32 [768], replicated
- grad_ln1_bias: float32 [768], replicated
- grad_w_qkv: float32 [768, 2304], P('batch', 'grp')
- grad_q_bias: float32 [768], replicated
- grad_v_bias: float32 [768], replicated
- grad_w_out: float32 [768, 768], P('batch', 'grp')
- grad_out_bias: float32 [768], replicated
- grad_ln2_gain: float32 [768], replicated
- grad_ln2_bias: float32 [768], replicated
- grad_w_up: float32 [768, 3072], P('batch', 'grp')
- grad_up_bias: float32 [3072], replicated
- grad_w_down: float32 [3072, 768], P('batch', 'grp')
- grad_down_bias: float32 [768], replicated
- grad_ln3_gain: float32 [768], replicated
- grad_ln3_bias: float32 [768], replicated
- grad_w_align: float32 [768, 1024], P('batch', 'grp')
- grad_align_bias: float32 [1024], replicated
The draws below stay inside these ranges and needn't reach their ends.
Inputs may be any that keep to these rules, and one draw needn't show every extreme that they name: `dest`: within the 256 rows of one device no destination is named by more than 64 rows, a bound that some block reaches. `seg_ids`: along each device's 512 slots the clip numbers never fall; each clip takes 1 to 128 slots and some clip exactly 128.
All inputs are finite; a program needn't handle non-finite values.
Results may differ from the reference program's by a relative error of at most 0.012.
Values may be sent and summed in bfloat16 or wider, within the bound.
No kernel may reach another device: no remote copies, remote signals or barrier semaphores. Data moves between devices by JAX's collectives and lax.ppermute only.
A program may use at most 192 MiB of HBM per device.

```python
import math
from functools import partial
import jax
import jax.numpy as jnp
import numpy as np
from jax import lax

D = 768
H = 12
FF = 3072
ALIGN = 1024
TOK_DEV = 256
CLIPS = 8
SEQ = 512
CAP = 64
CLIPMAX = 128
TOKENS = 8192
N_BATCH = 8
N_GRP = 4


def level_of(key, extent, cuts, smallest, top_value):
    def one(position, shards_of):
        steps = jax.random.uniform(jax.random.fold_in(jax.random.fold_in(key, 6), position), (shards_of,), jnp.float32, smallest / len(cuts), top_value / len(cuts))
        return jnp.repeat(jnp.exp(steps), extent[position] // shards_of).reshape((-1,) + (1,) * (len(extent) - position - 1))

    loudness = one(*cuts[0])
    for cut in cuts[1:]:
        loudness = loudness * one(*cut)
    return loudness


def length_profile(amount, total, bound, lean):
    portions = [(1 << 20) // math.isqrt(standing ** lean) + 1 for standing in range(2, amount + 1)]
    spare, counts = total - bound - (amount - 1), [1] * (amount - 1)
    while spare > 0:
        candidates = [i for i in range(amount - 1) if counts[i] < bound]
        pool, remaining = sum([portions[i] for i in candidates]), spare
        for i in candidates:
            addition = min(bound - counts[i], max(1, remaining * portions[i] // pool), spare)
            counts[i] = counts[i] + addition
            spare = spare - addition
    return np.array([bound] + counts)


def uneven(own_key, number_of, total, limit, slope):
    if number_of == 2:
        one = jax.random.randint(own_key, (), max(1, total - limit), min(limit, total - 1) + 1)
        return jnp.stack([one, total - one])
    lengths = jnp.asarray(length_profile(number_of, total, limit, slope), jnp.int32)
    twos = (number_of - 1) // 2
    donor, taker = lengths[1:1 + 2 * twos:2], lengths[2:2 + 2 * twos:2]
    margin = jnp.minimum(donor - 1, limit - taker)
    passed = jax.random.randint(jax.random.fold_in(own_key, 1), (twos,), 0, 1 << 20) % (margin + 1)
    lengths = lengths.at[1:1 + 2 * twos:2].set(donor - passed).at[2:2 + 2 * twos:2].set(taker + passed)
    return lengths[jax.random.permutation(jax.random.fold_in(own_key, 2), number_of)]


def routed_block(rng, own, number, rows, amount, top, most, skew):
    sequence = jax.random.permutation(rng, amount)
    crowded, usual = shares(amount, rows * top, most, skew, True), shares(amount, rows * top, most, skew, False)
    places = jnp.arange(amount)

    def named(sizes, turn):
        used = int((sizes > 0).sum())
        fixed = max(1, used // 4)
        passed = fixed + (places - fixed + turn * (used - fixed)) % max(1, amount - fixed)
        return jnp.zeros((amount,), jnp.int32).at[sequence[jnp.where(places < fixed, places, passed)]].set(jnp.asarray(sizes, jnp.int32))

    sizes = jnp.where(number % 4 == 0, named(crowded, number // 4), named(usual, number - number // 4 - 1))
    mixed = jax.random.permutation(jax.random.fold_in(own, 3), amount)
    giver, taker = mixed[0:amount // 2 * 2:2], mixed[1:amount // 2 * 2:2]
    margin = jnp.minimum(sizes[giver] - 1, most - sizes[taker]) // 2
    margin = jnp.where((giver == sequence[0]) | (taker == sequence[0]) | (sizes[taker] == 0), 0, jnp.maximum(margin, 0))
    passed = jax.random.randint(jax.random.fold_in(own, 4), (amount // 2,), 0, 1 << 20) % (margin + 1)
    sizes = sizes.at[giver].add(-passed).at[taker].add(passed)
    labels = jnp.searchsorted(jnp.cumsum(sizes), jnp.arange(rows * top), side="right").astype(jnp.int32)
    grid = labels.reshape(top, rows).T
    grid = grid[jax.random.permutation(jax.random.fold_in(own, 1), rows)]
    turn = jax.random.randint(jax.random.fold_in(own, 2), (rows, 1), 0, top)
    return jnp.take_along_axis(grid, (jnp.arange(top)[None, :] + turn) % top, axis=1)


def shares(count, total, reach, slope, full):
    weights = [(1 << 20) // math.isqrt(rank ** slope) + 1 for rank in range(1, count + 1)]
    largest = reach if full else min(reach, max(-(-total // count), total * weights[0] // sum(weights)))
    least = 1 if total - largest >= count - 1 else 0
    holding, rest = [largest] + [least] * (count - 1), total - largest - least * (count - 1)
    while rest > 0:
        movable = [i for i in range(1, count) if holding[i] < largest] or [i for i in range(1, count) if holding[i] < reach]
        whole, remaining = sum([weights[i] for i in movable]), rest
        for i in movable:
            addition = min(reach - holding[i], max(1, remaining * weights[i] // whole), rest)
            holding[i] = holding[i] + addition
            rest = rest - addition
    return np.array(holding)


def gaussian(own_key, dims, scale, most, cuts=(), kind=jnp.bfloat16):
    level = level_of(own_key, dims, cuts, -0.22, 0.18) if cuts else 1.0
    drawn = jax.random.normal(own_key, dims, jnp.float32) * scale * level
    return jnp.minimum(jnp.maximum(drawn, -most), most).astype(kind)


def setup_inputs(seed: int = 0) -> dict:
    streams_of = jax.random.split(jax.random.key(seed), 23)
    tokens = gaussian(streams_of[0], (TOKENS, D), 1.0, 6.0, ((0, 32),))
    dest_keys = jax.random.split(jax.random.fold_in(streams_of[1], 1), TOKENS // TOK_DEV)
    dest_turns = jax.random.permutation(jax.random.fold_in(streams_of[1], 3), TOKENS // TOK_DEV)
    dest = jax.vmap(lambda own, number: routed_block(jax.random.fold_in(streams_of[1], 2), own, number, TOK_DEV, N_BATCH, 1, CAP, 2))(dest_keys, dest_turns).reshape((TOKENS, 1))
    seg_ids = jax.vmap(lambda own: jnp.searchsorted(jnp.cumsum(uneven(own, CLIPS, SEQ, CLIPMAX, 2)), jnp.arange(SEQ), side="right"))(jax.random.split(streams_of[2], (N_BATCH * N_GRP))).reshape((N_BATCH * N_GRP, SEQ)).astype(jnp.int32)
    cot_out = gaussian(streams_of[3], (TOKENS, D), 1.0, 6.0, ((0, 32),))
    cot_align = gaussian(streams_of[4], (TOKENS, ALIGN), 1.0, 6.0, ((0, 32),))
    ln1_gain = jnp.clip(1.0 + 0.1 * jax.random.normal(streams_of[5], (D,), jnp.float32), 0.5, 1.5).astype(jnp.bfloat16)
    ln1_bias = gaussian(streams_of[6], (D,), 0.2, 1.0)
    w_qkv = gaussian(streams_of[7], (D, 3 * D), D ** -0.5, 0.21875)
    q_bias = gaussian(streams_of[8], (D,), 0.2, 1.0)
    v_bias = gaussian(streams_of[9], (D,), 0.2, 1.0)
    w_out = gaussian(streams_of[10], (D, D), (max(D // 64, 1)) ** -0.5, 1.75)
    out_bias = gaussian(streams_of[11], (D,), 0.2, 1.0)
    ln2_gain = jnp.clip(1.0 + 0.1 * jax.random.normal(streams_of[12], (D,), jnp.float32), 0.5, 1.5).astype(jnp.bfloat16)
    ln2_bias = gaussian(streams_of[13], (D,), 0.2, 1.0)
    w_up = gaussian(streams_of[14], (D, FF), D ** -0.5, 0.21875)
    up_bias = gaussian(streams_of[15], (FF,), 0.2, 1.0)
    w_down = gaussian(streams_of[16], (FF, D), FF ** -0.5, 0.109375)
    down_bias = gaussian(streams_of[17], (D,), 0.2, 1.0)
    ln3_gain = jnp.clip(1.0 + 0.1 * jax.random.normal(streams_of[18], (D,), jnp.float32), 0.5, 1.5).astype(jnp.bfloat16)
    ln3_bias = gaussian(streams_of[19], (D,), 0.2, 1.0)
    w_align = gaussian(streams_of[20], (D, ALIGN), D ** -0.5, 0.21875)
    align_bias = gaussian(streams_of[21], (ALIGN,), 0.2, 1.0)
    return {"tokens": tokens, "dest": dest, "seg_ids": seg_ids, "cot_out": cot_out, "cot_align": cot_align, "ln1_gain": ln1_gain, "ln1_bias": ln1_bias, "w_qkv": w_qkv, "q_bias": q_bias, "v_bias": v_bias, "w_out": w_out, "out_bias": out_bias, "ln2_gain": ln2_gain, "ln2_bias": ln2_bias, "w_up": w_up, "up_bias": up_bias, "w_down": w_down, "down_bias": down_bias, "ln3_gain": ln3_gain, "ln3_bias": ln3_bias, "w_align": w_align, "align_bias": align_bias}


@jax.custom_vjp
def low(v):
    return lax.optimization_barrier(v.astype(jnp.bfloat16)).astype(jnp.float32)

@jax.custom_vjp
def low_back(v):
    return v

def low_keep(v):
    return (low(v), None)

def low_pass(kept, grad):
    return (grad,)

def back_keep(v):
    return (v, None)

def back_low(kept, grad):
    return (low(grad),)
low.defvjp(low_keep, low_pass)
low_back.defvjp(back_keep, back_low)
layer_eps = 1e-06
masked_value = -1e+30

def precise_dot(left_side, right_side):
    return jnp.dot(left_side, right_side, precision=lax.Precision.HIGHEST, preferred_element_type=jnp.float32)

def normalize(values, gain_row, shift_row):
    average = lax.optimization_barrier(jnp.mean(values, axis=-1, keepdims=True))
    centered = values - average
    variance = lax.optimization_barrier(jnp.mean(centered * centered, axis=-1, keepdims=True))
    return centered * lax.rsqrt(variance + layer_eps) * gain_row + shift_row

def sequence_forward(weights, inputs, live_flags, segments):
    ln1_gain, ln1_bias, w_qkv, q_bias, v_bias, w_out, out_bias, ln2_gain, ln2_bias, w_up, up_bias, w_down, down_bias, ln3_gain, ln3_bias, w_align, align_bias = weights
    seq_rows = inputs.shape[0]
    head_size = D // H
    act_one = low(normalize(inputs, ln1_gain, ln1_bias))
    joined = precise_dot(act_one, w_qkv)
    queries = low(low_back(joined[:, :D] + q_bias)).reshape(seq_rows, H, head_size)
    key_rows = low(low_back(joined[:, D:2 * D])).reshape(seq_rows, H, head_size)
    value_rows = low(low_back(joined[:, 2 * D:] + v_bias)).reshape(seq_rows, H, head_size)
    raw_scores = jnp.einsum('qhd,khd->hqk', queries, key_rows, precision=lax.Precision.HIGHEST, preferred_element_type=jnp.float32) * head_size ** (-0.5)
    scores = low_back(raw_scores)
    positions = jnp.arange(seq_rows, dtype=jnp.int32)
    allowed = (segments[:, None] == segments[None, :]) & ((live_flags[None, :] > 0) | (positions[:, None] == positions[None, :]))
    masked = jnp.where(allowed[None], scores, masked_value)
    row_max = lax.optimization_barrier(jnp.max(masked, axis=-1, keepdims=True))
    powered = jnp.exp(masked - row_max)
    probs = low(powered / lax.optimization_barrier(jnp.sum(powered, axis=-1, keepdims=True)))
    context = jnp.einsum('hqk,khd->qhd', probs, value_rows, precision=lax.Precision.HIGHEST, preferred_element_type=jnp.float32).reshape(seq_rows, D)
    context = low(low_back(context))
    middle = inputs + low_back(precise_dot(context, w_out) + out_bias)
    act_two = low(normalize(middle, ln2_gain, ln2_bias))
    hidden_pre = low_back(precise_dot(act_two, w_up) + up_bias)
    hidden_act = low(jax.nn.gelu(hidden_pre, approximate=False))
    result = middle + low_back(precise_dot(hidden_act, w_down) + down_bias)
    act_three = low(normalize(result, ln3_gain, ln3_bias))
    aligned = precise_dot(act_three, w_align) + align_bias
    return (low(result), low(aligned))

def reference(tokens, dest, seg_ids, cot_out, cot_align, ln1_gain, ln1_bias, w_qkv, q_bias, v_bias, w_out, out_bias, ln2_gain, ln2_bias, w_up, up_bias, w_down, down_bias, ln3_gain, ln3_bias, w_align, align_bias):
    device_count = N_BATCH * N_GRP
    capacity = SEQ // N_BATCH
    targets = dest[:, 0].reshape(device_count, TOK_DEV)
    onehot = (targets[:, :, None] == jnp.arange(N_BATCH, dtype=jnp.int32)[None, None, :]).astype(jnp.int32)
    earlier = jnp.cumsum(onehot, axis=1) - onehot
    offset = lax.optimization_barrier(jnp.sum(earlier * onehot, axis=2)).astype(jnp.int32)
    sources = jnp.arange(device_count, dtype=jnp.int32)
    receiver = targets * N_GRP + (sources % N_GRP)[:, None]
    place_index = (receiver * SEQ + (sources // N_GRP)[:, None] * capacity + offset).reshape(-1).astype(jnp.int32)

    def spread(rows):
        empty = jnp.zeros((device_count * SEQ, rows.shape[1]), jnp.float32)
        return empty.at[place_index].set(rows.astype(jnp.float32)).reshape(device_count, SEQ, rows.shape[1])
    inbox = spread(tokens)
    inbox_grad = spread(cot_out)
    inbox_align = spread(cot_align)
    live_flags = jnp.zeros((device_count * SEQ,), jnp.int32).at[place_index].set(1).reshape(device_count, SEQ)
    weights = tuple((weight_arg.astype(jnp.float32) for weight_arg in (ln1_gain, ln1_bias, w_qkv, q_bias, v_bias, w_out, out_bias, ln2_gain, ln2_bias, w_up, up_bias, w_down, down_bias, ln3_gain, ln3_bias, w_align, align_bias)))
    group_size = math.gcd(max(1, 4096 // SEQ), device_count)
    steps_count = device_count // group_size

    def forward_all(inbox_rows, weight_set):

        def group_step(carry_value, pieces):
            rows, live_rows, segment_rows = pieces
            run_one = partial(sequence_forward, weight_set)
            return (carry_value, jax.vmap(run_one)(rows, live_rows, segment_rows))
        shaped = (inbox_rows.reshape(steps_count, group_size, SEQ, D), live_flags.reshape(steps_count, group_size, SEQ), seg_ids.reshape(steps_count, group_size, SEQ))
        unused, stacked = lax.scan(jax.checkpoint(group_step), jnp.float32(0.0), shaped)
        return (stacked[0].reshape(device_count, SEQ, D), stacked[1].reshape(device_count, SEQ, ALIGN))
    outputs, pull_back = jax.vjp(forward_all, inbox, weights)
    grad_inbox, grad_weights = pull_back((inbox_grad, inbox_align))
    out_tokens = outputs[0].reshape(-1, D)[place_index].astype(jnp.bfloat16)
    aligned_tokens = outputs[1].reshape(-1, ALIGN)[place_index].astype(jnp.bfloat16)
    grad_tokens = grad_inbox.reshape(-1, D)[place_index].astype(jnp.bfloat16)
    return (out_tokens, aligned_tokens, grad_tokens, grad_weights[0], grad_weights[1], grad_weights[2], grad_weights[3], grad_weights[4], grad_weights[5], grad_weights[6], grad_weights[7], grad_weights[8], grad_weights[9], grad_weights[10], grad_weights[11], grad_weights[12], grad_weights[13], grad_weights[14], grad_weights[15], grad_weights[16])
```

```python
import functools

import jax
import jax.numpy as jnp
from jax import lax
from jax.experimental import pallas as pl
from jax.experimental.pallas import tpu as pltpu
from jax.sharding import PartitionSpec as P

H = 12
CLIPMAX = 128
EPS = 1e-06
MASKED = -1e30
DEAD = 16.0
AXES = ("batch", "grp")
F32 = jnp.float32
BF16 = jnp.bfloat16
VMEM_BIG = 64_000_000


def dot(a, b):
    return jnp.dot(a, b, preferred_element_type=F32)


def dot_nt(a, b):
    return lax.dot_general(a, b, (((1,), (1,)), ((), ())), preferred_element_type=F32)


def dot_tn(a, b):
    return lax.dot_general(a, b, (((0,), (0,)), ((), ())), preferred_element_type=F32)


def iota(shape, axis):
    return lax.broadcasted_iota(jnp.int32, shape, axis)


def row_loop(total, step, body):
    def one(i, carry):
        body(pl.ds(pl.multiple_of(i * step, step), step))
        return carry

    lax.fori_loop(0, total // step, one, 0)


def norm_parts(v):
    centered = v - jnp.mean(v, axis=-1, keepdims=True)
    rstd = lax.rsqrt(jnp.mean(centered * centered, axis=-1, keepdims=True) + EPS)
    return centered * rstd, rstd


def norm_back(g_out, gain, hat, rstd):
    t = g_out * gain
    return rstd * (
        t - jnp.mean(t, axis=-1, keepdims=True) - hat * jnp.mean(t * hat, axis=-1, keepdims=True)
    )


def slot_column(dest_col, peers, capacity):
    rows = dest_col.shape[0]
    onehot = (dest_col == iota((rows, peers), 1)).astype(F32)
    before = (iota((rows, rows), 0) > iota((rows, rows), 1)).astype(BF16)
    earlier = dot(before, onehot.astype(BF16))
    offset = jnp.sum(earlier * onehot, axis=1, keepdims=True).astype(jnp.int32)
    return dest_col * capacity + offset


def slot_row(dest_row, peers, capacity):
    rows = dest_row.shape[1]
    onehot = (dest_row == iota((peers, rows), 0)).astype(F32)
    before = (iota((rows, rows), 0) < iota((rows, rows), 1)).astype(BF16)
    earlier = dot(onehot.astype(BF16), before)
    offset = jnp.sum(earlier * onehot, axis=0, keepdims=True).astype(jnp.int32)
    return dest_row * capacity + offset


def placing(dest_row, peers, capacity):
    rows = dest_row.shape[1]
    slots = peers * capacity
    return iota((slots, rows), 0) == slot_row(dest_row, peers, capacity)


def fetching(dest_col, peers, capacity):
    rows = dest_col.shape[0]
    slots = peers * capacity
    return (iota((rows, slots), 1) == slot_column(dest_col, peers, capacity)).astype(BF16)


def pack_kernel(peers, capacity, dest_row, tokens, out):
    place = placing(dest_row[...], peers, capacity)
    held = jnp.sum(place.astype(F32), axis=1, keepdims=True)
    rows = dot(place.astype(BF16), tokens[...])
    out[...] = jnp.where(held > 0.5, rows, DEAD).astype(BF16)


def windows(slots):
    block = CLIPMAX
    return [
        (n * block, max(0, (n - 1) * block), min(slots, (n + 2) * block))
        for n in range(slots // block)
    ]


def live_lanes(packed_ref):
    turned = jnp.transpose(packed_ref[:, 0:128].astype(F32))
    return turned[0:1, :] < DEAD * 0.5


def attention_kernel(
    packed, seg_row, seg_col, gain, shift, w_qkv, q_bias, v_bias, ctx, qkv, a1, lse, bias
):
    slots, width = packed.shape
    block = CLIPMAX
    live = live_lanes(packed)
    for n, (start, low, high) in enumerate(windows(slots)):
        rows, keys = (block, high - low), slice(low, high)
        same = seg_col[start : start + block, :] == seg_row[:, keys]
        own = (start + iota(rows, 0)) == (low + iota(rows, 1))
        usable = live[:, keys] | own
        bias[n, :, 0 : high - low] = jnp.where(same & usable, 0.0, MASKED)

    gain_f, shift_f = gain[...].astype(F32), shift[...].astype(F32)

    def norm_rows(r):
        x = packed[r, :].astype(F32)
        x = jnp.where(x[:, 0:1] < DEAD * 0.5, x, 0.0)
        hat, _ = norm_parts(x)
        a1[r, :] = (hat * gain_f + shift_f).astype(BF16)

    row_loop(slots, 32, norm_rows)

    piece = 256
    for part, part_bias in ((0, q_bias), (1, None), (2, v_bias)):
        for c in range(width // piece):
            cols = slice(part * width + c * piece, part * width + (c + 1) * piece)
            made = dot(a1[...], w_qkv[:, cols])
            if part_bias is not None:
                made = made + part_bias[:, c * piece : (c + 1) * piece].astype(F32)
            qkv[:, cols] = made.astype(BF16)

    lse[...] = jnp.zeros_like(lse)
    scale = jnp.asarray(64**-0.5, BF16)

    def pair(hp, carry):
        def lanes(part):
            return pl.ds(pl.multiple_of(part * width + hp * 128, 128), 128)

        first = iota((block, 128), 1) < 64
        for n, (start, low, high) in enumerate(windows(slots)):
            q = qkv[start : start + block, lanes(0)] * scale
            k = qkv[low:high, lanes(1)]
            v = qkv[low:high, lanes(2)]
            mask = bias[n, :, 0 : high - low]
            found = []
            logs = lse[start : start + block, :]
            for side in range(2):
                mine = first if side == 0 else ~first
                s = dot_nt(jnp.where(mine, q, jnp.zeros_like(q)), k) + mask
                top = jnp.max(s, axis=-1, keepdims=True)
                e = jnp.exp(s - top)
                total = jnp.sum(e, axis=-1, keepdims=True)
                p = (e / total).astype(BF16)
                found.append(dot(p, v))
                logs = jnp.where(
                    iota((block, 128), 1) == 2 * hp + side, top + jnp.log(total), logs
                )
            lse[start : start + block, :] = logs
            ctx[start : start + block, lanes(0)] = jnp.where(first, found[0], found[1]).astype(BF16)
        return carry

    lax.fori_loop(0, width // 128, pair, 0)


def attention_back_kernel(
    packed, g_ctx, qkv, a1, lse, seg_row, seg_col, gain, w_qkv,
    g_joined, g_rows, small, bias, lse_t, live_col, gk, gv, acc,
):
    slots, width = packed.shape
    block = CLIPMAX
    live = packed[:, 0:1].astype(F32) < DEAD * 0.5
    for n, (start, low, high) in enumerate(windows(slots)):
        shape, keys = (high - low, block), slice(low, high)
        same = seg_col[keys, :] == seg_row[:, start : start + block]
        own = (low + iota(shape, 0)) == (start + iota(shape, 1))
        usable = live[keys, :] | own
        bias[n, 0 : high - low, :] = jnp.where(same & usable, 0.0, MASKED)
    lse_t[...] = jnp.transpose(lse[...])
    scale = jnp.asarray(64**-0.5, BF16)

    def pair(hp, carry):
        def lanes(part):
            return pl.ds(pl.multiple_of(part * width + hp * 128, 128), 128)

        gk[...] = jnp.zeros_like(gk)
        gv[...] = jnp.zeros_like(gv)
        first = iota((block, 128), 1) < 64
        for n, (start, low, high) in enumerate(windows(slots)):
            here = slice(start, start + block)
            q = qkv[here, lanes(0)] * scale
            g = g_ctx[here, lanes(0)]
            k = qkv[low:high, lanes(1)]
            v = qkv[low:high, lanes(2)]
            mask = bias[n, 0 : high - low, :]
            zero = jnp.zeros_like(q)
            gq, sum_k, sum_v = None, None, None
            for side in range(2):
                mine = first if side == 0 else ~first
                q_own, g_own = jnp.where(mine, q, zero), jnp.where(mine, g, zero)
                s = dot_nt(k, q_own) + mask
                logs = jnp.where(iota((16, block), 0) == 2 * hp + side, lse_t[0:16, here], 0.0)
                p = jnp.exp(s - jnp.sum(logs, axis=0, keepdims=True))
                gp = dot_nt(v, g_own)
                inner = jnp.sum(gp * p, axis=0, keepdims=True)
                gs = (p * (gp - inner)).astype(BF16)
                part_v = dot(p.astype(BF16), g_own)
                part_k = dot(gs, q_own)
                part_q = dot_tn(gs, k)
                if side == 0:
                    gq, sum_k, sum_v = part_q, part_k, part_v
                else:
                    gq, sum_k, sum_v = jnp.where(first, gq, part_q), sum_k + part_k, sum_v + part_v
            gk[low:high, :] += sum_k
            gv[low:high, :] += sum_v
            g_joined[here, lanes(0)] = (gq * (64**-0.5)).astype(BF16)
        g_joined[:, lanes(1)] = gk[...].astype(BF16)
        g_joined[:, lanes(2)] = gv[...].astype(BF16)
        return carry

    lax.fori_loop(0, width // 128, pair, 0)

    acc[...] = dot_nt(g_joined[...], w_qkv[...])
    small[...] = jnp.zeros_like(small)
    gain_f = gain[...].astype(F32)

    def back_rows(r):
        x = packed[r, :].astype(F32)
        x = jnp.where(x[:, 0:1] < DEAD * 0.5, x, 0.0)
        hat, rstd = norm_parts(x)
        g_out = acc[r, :]
        small[0:1, :] += jnp.sum(g_out * hat, axis=0, keepdims=True)
        small[1:2, :] += jnp.sum(g_out, axis=0, keepdims=True)
        small[2:3, :] += jnp.sum(g_joined[r, 0:width].astype(F32), axis=0, keepdims=True)
        small[3:4, :] += jnp.sum(g_joined[r, 2 * width :].astype(F32), axis=0, keepdims=True)
        g_rows[r, :] = norm_back(g_out, gain_f, hat, rstd).astype(BF16)

    row_loop(slots, 32, back_rows)


def erfc_of(z):
    t = 1.0 / (1.0 + 0.5 * z)
    poly = 0.17087277
    for c in (
        -0.82215223, 1.48851587, -1.13520398, 0.27886807, -0.18628806,
        0.09678418, 0.37409196, 1.00002368, -1.26551223,
    ):
        poly = poly * t + c
    return t * jnp.exp(poly - z * z)


def rows_kernel(
    peers, capacity,
    arrived, tokens, dest_col, dest_row, cot_out, cot_align,
    w_out, out_bias, gain2, shift2, w_up, up_bias, w_down, down_bias, gain3, shift3, w_align, align_bias,
    y_out, al_out, g_packed, g_mid, a2, a3, ctx, hidden, gub, gyb, gmb, small,
    slope, mid, hat2, rstd2, acc,
):
    rows, width = tokens.shape
    wide = w_up.shape[1]
    piece = 256
    small[...] = jnp.zeros_like(small)

    ctx[...] = dot(fetching(dest_col[...], peers, capacity), arrived[...]).astype(BF16)
    acc[...] = dot(ctx[...], w_out[...])

    def to_mid(r):
        m = tokens[r, :].astype(F32) + acc[r, :] + out_bias[...].astype(F32)
        mid[r, :] = m
        hat, rstd = norm_parts(m)
        hat2[r, :] = hat
        rstd2[r, :] = jnp.broadcast_to(rstd, (rstd.shape[0], 128))
        a2[r, :] = (hat * gain2[...].astype(F32) + shift2[...].astype(F32)).astype(BF16)

    row_loop(rows, 32, to_mid)

    acc[...] = mid[...] + down_bias[...].astype(F32)

    def up(c, carry):
        cols = pl.ds(pl.multiple_of(c * piece, piece), piece)
        u = dot(a2[...], w_up[:, cols]) + up_bias[:, cols].astype(F32)
        tail = 0.5 * erfc_of(jnp.abs(u) * (0.5**0.5))
        below = jnp.where(u < 0.0, tail, 1.0 - tail)
        bell = jnp.exp(-0.5 * u * u) * 0.3989422804014327
        slope[:, cols] = below + u * bell
        made = (u * below).astype(BF16)
        hidden[:, cols] = made
        acc[...] += dot(made, w_down[cols, :])
        return carry

    lax.fori_loop(0, wide // piece, up, 0)

    def to_a3(r):
        y = acc[r, :]
        y_out[r, :] = y.astype(BF16)
        hat, rstd = norm_parts(y)
        a3[r, :] = (hat * gain3[...].astype(F32) + shift3[...].astype(F32)).astype(BF16)

    row_loop(rows, 32, to_a3)
    al_out[...] = (dot(a3[...], w_align[...]) + align_bias[...].astype(F32)).astype(BF16)
    mid[...] = dot_nt(cot_align[...], w_align[...])

    def back3(r):
        hat, rstd = norm_parts(acc[r, :])
        g_out = mid[r, :]
        gy = cot_out[r, :].astype(F32) + norm_back(g_out, gain3[...].astype(F32), hat, rstd)
        low = gy.astype(BF16)
        g_mid[r, :] = gy
        gyb[r, :] = low
        small[0:1, :] += jnp.sum(g_out * hat, axis=0, keepdims=True)
        small[1:2, :] += jnp.sum(g_out, axis=0, keepdims=True)
        small[2:3, :] += jnp.sum(low.astype(F32), axis=0, keepdims=True)
        for c in range(cot_align.shape[1] // piece):
            at = 10 * width + c * piece
            small[at // width : at // width + 1, at % width : at % width + piece] += jnp.sum(
                cot_align[r, c * piece : (c + 1) * piece].astype(F32), axis=0, keepdims=True
            )

    row_loop(rows, 32, back3)

    acc[...] = jnp.zeros_like(acc)
    for c in range(wide // piece):
        cols = slice(c * piece, (c + 1) * piece)
        low = (slope[:, cols] * dot_nt(gyb[...], w_down[cols, :])).astype(BF16)
        gub[:, cols] = low
        at = 6 * width + c * piece
        small[at // width : at // width + 1, at % width : at % width + piece] = jnp.sum(
            low.astype(F32), axis=0, keepdims=True
        )
        acc[...] += dot_nt(low, w_up[:, cols])

    def back2(r):
        hat, g_out = hat2[r, :], acc[r, :]
        gm = g_mid[r, :] + norm_back(g_out, gain2[...].astype(F32), hat, rstd2[r, 0:1])
        low = gm.astype(BF16)
        g_mid[r, :] = gm
        gmb[r, :] = low
        small[3:4, :] += jnp.sum(g_out * hat, axis=0, keepdims=True)
        small[4:5, :] += jnp.sum(g_out, axis=0, keepdims=True)
        small[5:6, :] += jnp.sum(low.astype(F32), axis=0, keepdims=True)

    row_loop(rows, 32, back2)
    g_ctx = dot_nt(gmb[...], w_out[...]).astype(BF16)
    place = placing(dest_row[...], peers, capacity).astype(BF16)
    g_packed[...] = dot(place, g_ctx).astype(BF16)


def last_kernel(peers, capacity, dest_col, g_mid, arrived, out):
    out[...] = (g_mid[...] + dot(fetching(dest_col[...], peers, capacity), arrived[...])).astype(
        BF16
    )


def turned_rows(order, lhs):
    count = order.shape[0]
    pick = (iota((count, count), 1) == order).astype(BF16)
    return dot_nt(pick, lhs).astype(BF16)


def spare_columns(ref, index, step, load):
    tile = pl.multiple_of((index * step) // 128 * 128, 128)
    part = ref[:, pl.ds(tile, load)].astype(F32)
    return jnp.where((index * step) % 128 == 64, pltpu.roll(part, load - 64, 1), part).astype(BF16)


def grad_a_kernel(ids, order, a2, a3, ctx, gub, da, gmb, keep, send, t2, t3, t1):
    step = pl.program_id(0)
    block = ids[1] ^ relative(step)

    @pl.when(step == 0)
    def _():
        t2[...] = turned_rows(order[...], a2[...])
        t3[...] = turned_rows(order[...], a3[...])
        t1[...] = turned_rows(order[...], ctx[...])

    own = spare_columns(gmb, block, gmb.shape[1] // 4, 256)

    def write(out):
        out[0, :, 0:768] = dot(t2[...], gub[...]).astype(BF16)
        out[0, :, 768:1024] = dot(t3[...], da[...]).astype(BF16)
        out[0, :, 1024:1280] = dot(t1[...], own).astype(BF16)

    pl.when(step < 2)(lambda: write(send))
    pl.when(step >= 2)(lambda: write(keep))


def relative(step):
    return jnp.where(step < 2, 1, 0) + 2 * (step % 2)


def grad_a(ids, order, a2, a3, ctx, gub, da, gmb):
    rows = a2.shape[0]
    whole = lambda shape: pl.BlockSpec(shape, lambda i, ids: (0, 0))
    column = lambda c: pl.BlockSpec((rows, c), lambda i, ids: (0, ids[1] ^ relative(i)))
    half = jax.ShapeDtypeStruct((2, 768, 1280), BF16)
    return pl.pallas_call(
        grad_a_kernel,
        name="grad_up_align_out",
        out_shape=(half, half),
        grid_spec=pltpu.PrefetchScalarGridSpec(
            num_scalar_prefetch=1,
            grid=(4,),
            in_specs=[
                whole((768, 1)),
                whole((rows, 768)),
                whole((rows, 768)),
                whole((rows, 768)),
                column(768),
                column(256),
                whole((rows, 768)),
            ],
            out_specs=(
                pl.BlockSpec((1, 768, 1280), lambda i, ids: (jnp.maximum(i - 2, 0), 0, 0)),
                pl.BlockSpec((1, 768, 1280), lambda i, ids: (jnp.minimum(i, 1), 0, 0)),
            ),
            scratch_shapes=[pltpu.VMEM((768, rows), BF16)] * 3,
        ),
        compiler_params=pltpu.CompilerParams(vmem_limit_bytes=VMEM_BIG),
        cost_estimate=pl.CostEstimate(
            flops=2 * rows * 768 * 5120, bytes_accessed=12_000_000, transcendentals=0
        ),
    )(ids, order, a2, a3, ctx, gub, da, gmb)


def grad_b_kernel(ids, order, gyb, hidden, keep, send, turned):
    @pl.when(pl.program_id(0) == 0)
    def _():
        turned[...] = turned_rows(order[...], gyb[...])

    made = dot(turned[...], hidden[...]).astype(BF16).reshape(4, 192, 384)
    keep[0, :, 0] = made[0:2]
    send[0, :, 0] = made[2:4]


def grad_b(ids, order, gyb, hidden):
    rows = gyb.shape[0]
    half = jax.ShapeDtypeStruct((2, 2, 4, 192, 384), BF16)
    index = lambda i: (i >> 2) + (((i >> 1) & 1) << 1) + ((i & 1) << 2)
    spec = pl.BlockSpec((1, 2, 1, 192, 384), lambda i, ids: (i // 4, 0, i % 4, 0, 0))
    return pl.pallas_call(
        grad_b_kernel,
        name="grad_down",
        out_shape=(half, half),
        grid_spec=pltpu.PrefetchScalarGridSpec(
            num_scalar_prefetch=1,
            grid=(8,),
            in_specs=[
                pl.BlockSpec((768, 1), lambda i, ids: (0, 0)),
                pl.BlockSpec((rows, 768), lambda i, ids: (0, 0)),
                pl.BlockSpec((rows, 384), lambda i, ids: (0, ids[0] ^ index(i))),
            ],
            out_specs=(spec, spec),
            scratch_shapes=[pltpu.VMEM((768, rows), BF16)],
        ),
        compiler_params=pltpu.CompilerParams(vmem_limit_bytes=VMEM_BIG),
        cost_estimate=pl.CostEstimate(
            flops=2 * rows * 768 * 3072, bytes_accessed=8_000_000, transcendentals=0
        ),
    )(ids, order, gyb, hidden)


def grad_c_kernel(ids, order, a1, g_joined, keep_x, send_x, keep_y, send_y, turned):
    step = pl.program_id(0)

    @pl.when(step == 0)
    def _():
        turned[...] = turned_rows(order[...], a1[...])

    own = spare_columns(g_joined, ids[1] ^ relative(step), g_joined.shape[1] // 4, 640)
    made = dot(turned[...], own).astype(BF16)

    def write(out_x, out_y):
        out_x[0] = made[0:384]
        out_y[:, 0] = made[384:768].reshape(2, 192, 640)

    pl.when(step < 2)(lambda: write(send_x, send_y))
    pl.when(step >= 2)(lambda: write(keep_x, keep_y))


def grad_c(ids, order, a1, g_joined):
    rows = a1.shape[0]
    half_x = jax.ShapeDtypeStruct((2, 384, 640), BF16)
    half_y = jax.ShapeDtypeStruct((2, 2, 192, 640), BF16)
    later = lambda i: jnp.maximum(i - 2, 0)
    sooner = lambda i: jnp.minimum(i, 1)
    return pl.pallas_call(
        grad_c_kernel,
        name="grad_qkv",
        out_shape=(half_x, half_x, half_y, half_y),
        grid_spec=pltpu.PrefetchScalarGridSpec(
            num_scalar_prefetch=1,
            grid=(4,),
            in_specs=[
                pl.BlockSpec((768, 1), lambda i, ids: (0, 0)),
                pl.BlockSpec((rows, 768), lambda i, ids: (0, 0)),
                pl.BlockSpec((rows, 2304), lambda i, ids: (0, 0)),
            ],
            out_specs=(
                pl.BlockSpec((1, 384, 640), lambda i, ids: (later(i), 0, 0)),
                pl.BlockSpec((1, 384, 640), lambda i, ids: (sooner(i), 0, 0)),
                pl.BlockSpec((2, 1, 192, 640), lambda i, ids: (0, later(i), 0, 0)),
                pl.BlockSpec((2, 1, 192, 640), lambda i, ids: (0, sooner(i), 0, 0)),
            ),
            scratch_shapes=[pltpu.VMEM((768, rows), BF16)],
        ),
        compiler_params=pltpu.CompilerParams(vmem_limit_bytes=VMEM_BIG),
        cost_estimate=pl.CostEstimate(
            flops=2 * rows * 768 * 2560, bytes_accessed=8_000_000, transcendentals=0
        ),
    )(ids, order, a1, g_joined)


def flip(value, axis, bit, peers, groups):
    pairs = []
    for b in range(peers):
        for g in range(groups):
            other = (b ^ bit, g) if axis == "batch" else (b, g ^ bit)
            pairs.append((b * groups + g, other[0] * groups + other[1]))
    return lax.ppermute(value, AXES, pairs)


STEPS_X = (("grp", 1), ("grp", 2), ("batch", 1), ("batch", 2), ("batch", 4))
STEPS_Y = (("grp", 1), ("batch", 1), ("grp", 2), ("batch", 2), ("batch", 4))


def reduce_blocks(keep, send, steps, peers, groups):
    for axis, bit in steps[:-1]:
        came = flip(send, axis, bit, peers, groups)
        half = keep.shape[0] // 2
        keep, send = keep[:half] + came[:half], keep[half:] + came[half:]
    came = flip(send, *steps[-1], peers, groups)
    return keep[0].astype(F32) + came[0].astype(F32)


def tiled_blocks(matrix, row_parts, column_parts):
    r, c = matrix.shape
    shaped = matrix.reshape(row_parts, r // row_parts, column_parts, c // column_parts)
    return jnp.transpose(shaped, (0, 2, 1, 3)).reshape(
        row_parts * column_parts, r // row_parts, c // column_parts
    )


def scattered(matrix, peers, groups):
    return lax.psum_scatter(
        tiled_blocks(matrix, peers, groups), AXES, scatter_dimension=0, tiled=True
    )[0]


def call(kernel, name, out_shape, scratch, flops, nbytes, *args):
    return pl.pallas_call(
        kernel,
        name=name,
        out_shape=out_shape,
        scratch_shapes=scratch,
        compiler_params=pltpu.CompilerParams(vmem_limit_bytes=VMEM_BIG),
        cost_estimate=pl.CostEstimate(flops=flops, bytes_accessed=nbytes, transcendentals=0),
    )(*args)


def exchange(packed, peers):
    shaped = packed.reshape(peers, packed.shape[0] // peers, packed.shape[1])
    return lax.all_to_all(shaped, "batch", split_axis=0, concat_axis=0, tiled=True).reshape(
        packed.shape
    )


def per_device(
    tokens, dest, seg_ids, cot_out, cot_align,
    ln1_gain, ln1_bias, w_qkv, q_bias, v_bias, w_out, out_bias,
    ln2_gain, ln2_bias, w_up, up_bias, w_down, down_bias,
    ln3_gain, ln3_bias, w_align, align_bias,
):
    rows, width = tokens.shape
    align = cot_align.shape[1]
    wide = w_up.shape[1]
    slots = seg_ids.shape[1]
    peers, groups = lax.axis_size("batch"), lax.axis_size("grp")
    capacity = slots // peers
    dest_row = dest.reshape(1, rows)
    seg_col = seg_ids.reshape(slots, 1)
    line = lambda v: v.reshape(1, v.shape[0])
    shape = jax.ShapeDtypeStruct
    windows_count = slots // CLIPMAX

    packed = call(
        functools.partial(pack_kernel, peers, capacity), "pack_tokens",
        shape((slots, width), BF16), [], 2 * slots * rows * width, 1_500_000,
        dest_row, tokens,
    )
    packed = exchange(packed, peers)

    ctx, qkv, a1, lse = call(
        attention_kernel, "attention",
        (shape((slots, width), BF16), shape((slots, 3 * width), BF16), shape((slots, width), BF16), shape((slots, 128), F32)),
        [pltpu.VMEM((windows_count, CLIPMAX, 3 * CLIPMAX), F32)],
        2 * slots * width * 3 * width + 4 * slots * slots * width, 9_000_000,
        packed, seg_ids, seg_col, line(ln1_gain), line(ln1_bias), w_qkv, line(q_bias), line(v_bias),
    )
    ctx = exchange(ctx, peers)

    low = lambda c: shape((rows, c), BF16)
    y, al, g_packed, g_mid, a2, a3, ctx_rows, hidden, gub, gyb, gmb, small_rows = call(
        functools.partial(rows_kernel, peers, capacity), "rows",
        (low(width), low(align), shape((slots, width), BF16), shape((rows, width), F32), low(width), low(width), low(width),
         low(wide), low(wide), low(width), low(width), shape((16, width), F32)),
        [pltpu.VMEM((rows, wide), F32), pltpu.VMEM((rows, width), F32), pltpu.VMEM((rows, width), F32),
         pltpu.VMEM((rows, 128), F32), pltpu.VMEM((rows, width), F32)],
        8 * rows * width * (width + 2 * wide + align), 22_000_000,
        ctx, tokens, dest, dest_row, cot_out, cot_align,
        w_out, line(out_bias), line(ln2_gain), line(ln2_bias), w_up, line(up_bias), w_down, line(down_bias),
        line(ln3_gain), line(ln3_bias), w_align, line(align_bias),
    )
    g_arrived = exchange(g_packed, peers)

    fast = peers == 8 and groups == 4 and (width, wide, align) == (768, 3072, 1024)
    if fast:
        b, g = lax.axis_index("batch"), lax.axis_index("grp")
        ids = jnp.stack([b, g]).astype(jnp.int32)
        place = jnp.arange(8)
        turn = (place >> 2) + (((place >> 1) & 1) << 1) + ((place & 1) << 2)
        rel_b = b ^ turn
        order_a = (rel_b[:, None] * 96 + jnp.arange(96)[None, :]).reshape(768, 1)
        order_c = (
            rel_b[None, :, None] * 96 + jnp.arange(2)[:, None, None] * 48 + jnp.arange(48)
        ).reshape(768, 1)
        rel_g = g ^ jnp.array([0, 2, 1, 3])
        order_b = (rel_g[:, None] * 192 + jnp.arange(192)[None, :]).reshape(768, 1)
        keep_a, send_a = grad_a(ids, order_a, a2, a3, ctx_rows, gub, cot_align, gmb)
        sum_a = reduce_blocks(
            keep_a.reshape(16, 96, 1280), send_a.reshape(16, 96, 1280), STEPS_X, peers, groups
        )
        keep_b, send_b = grad_b(ids, order_b, gyb, hidden)
        sum_b = reduce_blocks(
            keep_b.reshape(16, 192, 384), send_b.reshape(16, 192, 384), STEPS_Y, peers, groups
        )
        sum_up, sum_align, sum_out = sum_a[:, :768], sum_a[:, 768:1024], sum_a[:, 1024:1216]
        sum_down = sum_b.T
    else:
        left = lambda a, c: lax.dot_general(a, c, (((0,), (0,)), ((), ())), preferred_element_type=F32)
        sum_up, sum_align, sum_out, sum_down = (
            scattered(left(a2, gub), peers, groups),
            scattered(left(a3, cot_align), peers, groups),
            scattered(left(ctx_rows, gmb), peers, groups),
            scattered(left(hidden, gyb), peers, groups),
        )

    g_joined, g_rows, small_slots = call(
        attention_back_kernel, "attention_back",
        (shape((slots, 3 * width), BF16), shape((slots, width), BF16), shape((8, width), F32)),
        [pltpu.VMEM((windows_count, 3 * CLIPMAX, CLIPMAX), F32), pltpu.VMEM((128, slots), F32), pltpu.VMEM((slots, 128), F32),
         pltpu.VMEM((slots, 128), F32), pltpu.VMEM((slots, 128), F32), pltpu.VMEM((slots, width), F32)],
        2 * slots * width * 3 * width + 12 * slots * slots * width, 12_000_000,
        packed, g_arrived, qkv, a1, lse, seg_ids, seg_col, line(ln1_gain), w_qkv,
    )
    g_back = exchange(g_rows, peers)
    if fast:
        keep_x, send_x, keep_y, send_y = grad_c(ids, order_c, a1, g_joined)
        sum_x = reduce_blocks(
            keep_x.reshape(16, 48, 640), send_x.reshape(16, 48, 640), STEPS_X, peers, groups
        )
        sum_y = reduce_blocks(
            keep_y.reshape(16, 48, 640), send_y.reshape(16, 48, 640), STEPS_Y, peers, groups
        )
        sum_qkv = jnp.concatenate([sum_x, sum_y], axis=0)[:, :576]
    else:
        sum_qkv = scattered(left(a1, g_joined), peers, groups)

    grad_tokens = call(
        functools.partial(last_kernel, peers, capacity), "grad_tokens",
        low(width), [], 2 * slots * rows * width, 2_000_000,
        dest, g_mid, g_back,
    )
    total = jnp.concatenate([small_rows, small_slots], axis=0)
    if fast:
        for axis, bit in STEPS_X:
            total = total + flip(total, axis, bit, peers, groups)
    else:
        total = lax.psum(total, AXES)
    sum_up_bias = total[6:10].reshape(4 * width)[:wide]
    sum_align_bias = total[10:12].reshape(2 * width)[:align]
    return (
        y, al, grad_tokens,
        total[16], total[17], sum_qkv, total[18], total[19],
        sum_out, total[5], total[3], total[4],
        sum_up, sum_up_bias, sum_down, total[2],
        total[0], total[1], sum_align, sum_align_bias,
    )


def solution(mesh):
    row, one = P(AXES, None), P()
    matrix = P("batch", "grp")
    return jax.shard_map(
        per_device,
        mesh=mesh,
        in_specs=(row,) * 5 + (one,) * 17,
        out_specs=(
            row, row, row, one, one, matrix, one, one, matrix, one,
            one, one, matrix, one, matrix, one, one, one, matrix, one,
        ),
        check_vma=False,
    )
```

```python
import functools

import jax
import jax.numpy as jnp
from jax import lax
from jax.experimental import pallas as pl
from jax.experimental.pallas import tpu as pltpu
from jax.sharding import PartitionSpec as P

H = 12
CLIPMAX = 128
EPS = 1e-06
MASKED = -1e30
DEAD = 16.0
AXES = ("batch", "grp")
SMEM = pl.BlockSpec(memory_space=pltpu.SMEM)
VMEM = pl.BlockSpec(memory_space=pltpu.VMEM)
HBM = pl.BlockSpec(memory_space=pltpu.HBM)
F32 = jnp.float32
BF16 = jnp.bfloat16


def dot(a, b):
    return jnp.dot(a, b, preferred_element_type=F32)


def dot_nt(a, b):
    return lax.dot_general(a, b, (((1,), (1,)), ((), ())), preferred_element_type=F32)


def dot_tn(a, b):
    return lax.dot_general(a, b, (((0,), (0,)), ((), ())), preferred_element_type=F32)


def iota(shape, axis):
    return lax.broadcasted_iota(jnp.int32, shape, axis)


def row_loop(total, step, body):
    def one(i, carry):
        body(pl.ds(pl.multiple_of(i * step, step), step))
        return carry

    lax.fori_loop(0, total // step, one, 0)


def norm_parts(v):
    centered = v - jnp.mean(v, axis=-1, keepdims=True)
    rstd = lax.rsqrt(jnp.mean(centered * centered, axis=-1, keepdims=True) + EPS)
    return centered * rstd, rstd


def norm_back(g_out, gain, hat, rstd):
    t = g_out * gain
    return rstd * (
        t - jnp.mean(t, axis=-1, keepdims=True) - hat * jnp.mean(t * hat, axis=-1, keepdims=True)
    )


def slot_column(dest_col, me, peers, capacity):
    rows = dest_col.shape[0]
    onehot = (dest_col == iota((rows, peers), 1)).astype(F32)
    before = (iota((rows, rows), 0) > iota((rows, rows), 1)).astype(BF16)
    earlier = dot(before, onehot.astype(BF16))
    offset = jnp.sum(earlier * onehot, axis=1, keepdims=True).astype(jnp.int32)
    return (dest_col ^ me) * capacity + offset


def slot_row(dest_row, me, peers, capacity):
    rows = dest_row.shape[1]
    onehot = (dest_row == iota((peers, rows), 0)).astype(F32)
    before = (iota((rows, rows), 0) < iota((rows, rows), 1)).astype(BF16)
    earlier = dot(onehot.astype(BF16), before)
    offset = jnp.sum(earlier * onehot, axis=0, keepdims=True).astype(jnp.int32)
    return (dest_row ^ me) * capacity + offset


def placing(dest_row, me, peers, capacity):
    shape = (peers * capacity, dest_row.shape[1])
    return iota(shape, 0) == slot_row(dest_row, me, peers, capacity)


def fetching(dest_col, me, peers, capacity):
    shape = (dest_col.shape[0], peers * capacity)
    return (iota(shape, 1) == slot_column(dest_col, me, peers, capacity)).astype(BF16)


def own_index(ids, blocks):
    return ids[0] if blocks > 1 else 0


def block_rows(ids, k, refs):
    size = refs[0].shape[0]
    if len(refs) == 1:
        return pl.ds(0, size)
    return pl.ds(pl.multiple_of((ids[0] ^ k) * size, size), size)


def pack_kernel(peers, capacity, ids, dest_row, tokens, *outs):
    place = placing(dest_row[...], own_index(ids, len(outs)), peers, capacity)
    held = jnp.sum(place.astype(F32), axis=1, keepdims=True)
    rows = jnp.where(held > 0.5, dot(place.astype(BF16), tokens[...]), DEAD).astype(BF16)
    size = outs[0].shape[0]
    for k, out in enumerate(outs):
        out[...] = rows[k * size : (k + 1) * size]


def windows(slots):
    block = CLIPMAX
    return [
        (n * block, max(0, (n - 1) * block), min(slots, (n + 2) * block))
        for n in range(slots // block)
    ]


def write_bias(packed, seg_row, seg_col, bias):
    block = CLIPMAX
    live = packed[:, 0:1].astype(F32) < DEAD * 0.5
    for n, (start, low, high) in enumerate(windows(packed.shape[0])):
        shape, keys = (high - low, block), slice(low, high)
        same = seg_col[keys, :] == seg_row[:, start : start + block]
        own = (low + iota(shape, 0)) == (start + iota(shape, 1))
        made = jnp.where(same & (live[keys, :] | own), 0.0, MASKED)
        bias[n, 0 : high - low, 0:block] = made
        bias[n, 0 : high - low, block:] = made


def stacked(rows):
    first = iota(rows.shape, 1) < 64
    zero = jnp.zeros_like(rows)
    return jnp.concatenate([jnp.where(first, rows, zero), jnp.where(first, zero, rows)], axis=0)


def unstacked(turned):
    half = turned.shape[1] // 2
    upper = iota((128, half), 0) < 64
    return jnp.transpose(jnp.where(upper, turned[:, :half], turned[:, half:]))


def attention_kernel(blocks, ids, *refs):
    arrived, refs = refs[:blocks], refs[blocks:]
    (seg_row, seg_col, gain, shift, w_hbm, q_bias, v_bias,
     ctx, qkv_out, natural_out, a1, lse,
     bias, turned_v, w_qkv, qkv, packed, in_sems, w_sem, out_sems) = refs
    slots, width = packed.shape
    block = CLIPMAX
    fetches = []
    for k, ref in enumerate(arrived):
        to = packed.at[block_rows(ids, k, arrived), :]
        fetches.append(pltpu.make_async_copy(ref, to, in_sems.at[k]))
        fetches[-1].start()
    weights = pltpu.make_async_copy(w_hbm, w_qkv, w_sem)
    weights.start()
    for fetch in fetches:
        fetch.wait()
    keep = pltpu.make_async_copy(packed, natural_out, out_sems.at[0])
    keep.start()
    write_bias(packed, seg_row, seg_col, bias)
    gain_f, shift_f = gain[...].astype(F32), shift[...].astype(F32)

    def norm_rows(r):
        x = packed[r, :].astype(F32)
        x = jnp.where(x[:, 0:1] < DEAD * 0.5, x, 0.0)
        hat, _ = norm_parts(x)
        a1[r, :] = (hat * gain_f + shift_f).astype(BF16)

    row_loop(slots, 32, norm_rows)
    weights.wait()

    piece = 256
    for part, part_bias in ((0, q_bias), (1, None), (2, v_bias)):
        for c in range(width // piece):
            cols = slice(part * width + c * piece, part * width + (c + 1) * piece)
            made = dot(a1[...], w_qkv[:, cols])
            if part_bias is not None:
                made = made + part_bias[:, c * piece : (c + 1) * piece].astype(F32)
            qkv[:, cols] = made.astype(BF16)
    keep_qkv = pltpu.make_async_copy(qkv, qkv_out, out_sems.at[1])
    keep_qkv.start()

    scale = jnp.asarray(64**-0.5, BF16)

    def pair(hp, carry):
        def lanes(part):
            return pl.ds(pl.multiple_of(part * width + hp * 128, 128), 128)

        turned_v[...] = jnp.transpose(qkv[:, lanes(2)].astype(F32)).astype(BF16)
        scores = []
        for n, (start, low, high) in enumerate(windows(slots)):
            q = stacked(qkv[start : start + block, lanes(0)] * scale)
            scores.append(dot_nt(qkv[low:high, lanes(1)], q) + bias[n, 0 : high - low, :])
        for n, (start, low, high) in enumerate(windows(slots)):
            s = scores[n]
            top = jnp.max(s, axis=0, keepdims=True)
            e = jnp.exp(s - top)
            total = jnp.sum(e, axis=0, keepdims=True)
            lse[hp, n : n + 1, :] = top + jnp.log(total)
            found = dot(turned_v[:, low:high], e.astype(BF16)) * (1.0 / total)
            ctx[start : start + block, lanes(0)] = unstacked(found).astype(BF16)
        return carry

    lax.fori_loop(0, width // 128, pair, 0)
    keep.wait()
    keep_qkv.wait()


def attention_back_kernel(shared, traffic, ids, *refs):
    (g_ctx, packed, qkv, lse, a1, seg_row, seg_col, gain, w_hbm), refs = refs[:9], refs[9:]
    (g_rows, g_joined, small), refs = refs[:3], refs[3:]
    if shared:
        (send, turned), refs = refs[:2], refs[2:]
    bias, turned_k, gk, gv, acc, sums, w_qkv, w_sem = refs[:8]
    slots, width = packed.shape
    block = CLIPMAX
    weights = pltpu.make_async_copy(w_hbm, w_qkv, w_sem)
    weights.start()
    traffic.need(1, 6)
    write_bias(packed, seg_row, seg_col, bias)
    traffic.need(2, 3, 4)
    scale = jnp.asarray(64**-0.5, BF16)

    def pair(hp, carry):
        def lanes(part):
            return pl.ds(pl.multiple_of(part * width + hp * 128, 128), 128)

        if shared:
            a1_turned = refs[8]
            a1_turned[lanes(0), :] = jnp.transpose(a1[:, lanes(0)].astype(F32)).astype(BF16)
        turned_k[...] = jnp.transpose(qkv[:, lanes(1)].astype(F32)).astype(BF16)
        gk[...] = jnp.zeros_like(gk)
        gv[...] = jnp.zeros_like(gv)
        first = []
        for n, (start, low, high) in enumerate(windows(slots)):
            here = slice(start, start + block)
            q = stacked(qkv[here, lanes(0)] * scale)
            g = stacked(g_ctx[here, lanes(0)])
            s = dot_nt(qkv[low:high, lanes(1)], q) + bias[n, 0 : high - low, :]
            first.append((q, g, s, dot_nt(qkv[low:high, lanes(2)], g)))
        for n, (start, low, high) in enumerate(windows(slots)):
            here = slice(start, start + block)
            q, g, s, gp = first[n]
            p = jnp.exp(s - lse[hp, n : n + 1, :])
            inner = jnp.sum(gp * p, axis=0, keepdims=True)
            gs = (p * (gp - inner)).astype(BF16)
            gv[low:high, :] += dot(p.astype(BF16), g)
            gk[low:high, :] += dot(gs, q)
            gq = dot(turned_k[:, low:high], gs) * (64**-0.5)
            g_joined[here, lanes(0)] = unstacked(gq).astype(BF16)
        g_joined[:, lanes(1)] = gk[...].astype(BF16)
        g_joined[:, lanes(2)] = gv[...].astype(BF16)
        return carry

    lax.fori_loop(0, width // 128, pair, 0)

    weights.wait()
    acc[...] = dot_nt(g_joined[...], w_qkv[...])
    ones = jnp.ones((8, slots), BF16)
    small[2:3, :] = dot(ones, g_joined[:, 0:width])[0:1]
    small[3:4, :] = dot(ones, g_joined[:, 2 * width :])[0:1]
    small[4:8, :] = jnp.zeros_like(small[4:8, :])
    sums[...] = jnp.zeros_like(sums)
    gain_f = gain[...].astype(F32)

    def back_rows(r):
        x = packed[r, :].astype(F32)
        x = jnp.where(x[:, 0:1] < DEAD * 0.5, x, 0.0)
        hat, rstd = norm_parts(x)
        g_out = acc[r, :]
        sums[0] += folded(g_out * hat)
        sums[1] += folded(g_out)
        g_rows[r, :] = norm_back(g_out, gain_f, hat, rstd).astype(BF16)

    row_loop(slots, 32, back_rows)
    small[0:1, :] = jnp.sum(sums[0], axis=0, keepdims=True)
    small[1:2, :] = jnp.sum(sums[1], axis=0, keepdims=True)
    if shared:
        set_blocks(refs[8], turned, ids, 2, 8, 2)
        joined_products(sender(send, joined_place, JOINED_BASE, (JOINED_ROWS,) * 2), 1, ids, turned, g_joined)
        write_small(small, send, 32 * JOINED_ROWS)


def folded(rows):
    total = rows[0:8]
    for i in range(8, rows.shape[0], 8):
        total = total + rows[i : i + 8]
    return total


def gelu_parts(u):
    bell = jnp.exp(-0.5 * u * u)
    t = 1.0 / (1.0 + 0.305 * jnp.abs(u))
    poly = 0.03669796139001846
    for c in (
        -0.15298233926296234, 0.18570539355278015, -0.03796539083123207, 0.12101536989212036,
        0.10342279821634293, 0.12246651202440262, 0.12163975089788437,
    ):
        poly = poly * t + c
    tail = bell * (poly * t)
    below = jnp.where(u < 0.0, tail, 1.0 - tail)
    return below, below + u * (bell * 0.3989422804014327)


def rows_kernel(peers, capacity, shared, traffic, ids, *refs):
    (whole, tokens, dest_col, dest_row, cot_out, cot_align, out_hbm, out_bias, gain2, shift2, up_hbm, up_bias, down_hbm, down_bias,
     gain3, shift3, align_hbm, align_bias), refs = refs[:18], refs[18:]
    (y_out, al_out, g_packed, g_mid, hidden, gub, a2, a3, ctx, gyb, gmb, small), refs = refs[:12], refs[12:]
    if shared:
        (send_1, send_2, turned_d, turned_3, turned_2, turned_1, small_e), refs = refs[:7], refs[7:]
    (mid, acc, hat2, rstd2, slope, u_a, u_b, h_a, h_b, sums, w_out, w_up, w_down, w_align, sems), refs = refs[:15], refs[15:]
    rows, width = tokens.shape
    wide = hidden.shape[1]
    piece = u_a.shape[1]
    loads = [
        pltpu.make_async_copy(source, to, sems.at[k])
        for k, (source, to) in enumerate(
            ((out_hbm, w_out), (up_hbm, w_up), (down_hbm, w_down), (align_hbm, w_align))
        )
    ]
    for load in loads:
        load.start()

    fetch = fetching(dest_col[...], 0, peers, capacity)
    ctx[...] = dot(fetch, whole[...]).astype(BF16)
    loads[0].wait()
    acc[...] = dot(ctx[...], w_out[...])

    def to_mid(r):
        m = tokens[r, :].astype(F32) + acc[r, :] + out_bias[...].astype(F32)
        hat, rstd = norm_parts(m)
        hat2[r, :] = hat
        rstd2[r, :] = jnp.broadcast_to(rstd, (rstd.shape[0], 128))
        a2[r, :] = (hat * gain2[...].astype(F32) + shift2[...].astype(F32)).astype(BF16)
        acc[r, :] = m + down_bias[...].astype(F32)

    row_loop(rows, 32, to_mid)

    def columns(i):
        return pl.ds(pl.multiple_of(i * piece, piece), piece)

    def up(i):
        return dot(a2[...], w_up[:, columns(i)]) + up_bias[:, columns(i)].astype(F32)

    def bend(i, u_ref, h_ref):
        u = u_ref[...]
        below, bent = gelu_parts(u)
        slope[:, columns(i)] = bent
        made = (u * below).astype(BF16)
        hidden[:, columns(i)] = made
        h_ref[...] = made

    last = wide // piece - 1
    h_b[...] = jnp.zeros_like(h_b)
    loads[1].wait()
    u_a[...] = up(0)
    loads[2].wait()

    def two(j, carry):
        u_b[...] = up(2 * j + 1)
        acc[...] += dot(h_b[...], w_down[columns(jnp.maximum(2 * j - 1, 0)), :])
        bend(2 * j, u_a, h_a)
        u_a[...] = up(jnp.minimum(2 * j + 2, last))
        acc[...] += dot(h_a[...], w_down[columns(2 * j), :])
        bend(2 * j + 1, u_b, h_b)
        return carry

    lax.fori_loop(0, (last + 1) // 2, two, 0)
    acc[...] += dot(h_b[...], w_down[columns(last), :])
    traffic.ready(4)

    def to_a3(r):
        y = acc[r, :]
        y_out[r, :] = y.astype(BF16)
        hat, _ = norm_parts(y)
        a3[r, :] = (hat * gain3[...].astype(F32) + shift3[...].astype(F32)).astype(BF16)

    row_loop(rows, 32, to_a3)
    loads[3].wait()
    al_out[...] = (dot(a3[...], w_align[...]) + align_bias[...].astype(F32)).astype(BF16)
    traffic.ready(0, 1)
    mid[...] = dot_nt(cot_align[...], w_align[...])
    sums[...] = jnp.zeros_like(sums)

    def back3(r):
        hat, rstd = norm_parts(acc[r, :])
        g_out = mid[r, :]
        gy = cot_out[r, :].astype(F32) + norm_back(g_out, gain3[...].astype(F32), hat, rstd)
        g_mid[r, :] = gy
        gyb[r, :] = gy.astype(BF16)
        sums[0] += folded(g_out * hat)
        sums[1] += folded(g_out)

    row_loop(rows, 32, back3)
    small[...] = jnp.zeros_like(small)
    small[0:1, :] = jnp.sum(sums[0], axis=0, keepdims=True)
    small[1:2, :] = jnp.sum(sums[1], axis=0, keepdims=True)
    ones = jnp.ones((8, rows), BF16)
    small[2:3, :] = dot(ones, gyb[...])[0:1]
    align = dot(ones, cot_align[...])[0:1]
    small[3:4, :] = align[:, :width]
    small[4:5, 0 : align.shape[1] - width] = align[:, width:]

    acc[...] = jnp.zeros_like(acc)
    for c in range(wide // 512):
        cols = slice(c * 512, (c + 1) * 512)
        low = (slope[:, cols] * dot_nt(gyb[...], w_down[cols, :])).astype(BF16)
        gub[:, cols] = low
        acc[...] += dot_nt(low, w_up[:, cols])
    traffic.ready(5)
    sums[...] = jnp.zeros_like(sums)

    def back2(r):
        hat, g_out = hat2[r, :], acc[r, :]
        gm = g_mid[r, :] + norm_back(g_out, gain2[...].astype(F32), hat, rstd2[r, 0:1])
        g_mid[r, :] = gm
        gmb[r, :] = gm.astype(BF16)
        sums[0] += folded(g_out * hat)
        sums[1] += folded(g_out)

    row_loop(rows, 32, back2)
    traffic.ready(3, 10)
    g_ctx = dot_nt(gmb[...], w_out[...]).astype(BF16)
    place = placing(dest_row[...], 0, peers, capacity).astype(BF16)
    g_packed[...] = dot(place, g_ctx).astype(BF16)
    traffic.ready(2)
    small[8:9, :] = jnp.sum(sums[0], axis=0, keepdims=True)
    small[9:10, :] = jnp.sum(sums[1], axis=0, keepdims=True)
    small[10:11, :] = dot(ones, gmb[...])[0:1]
    g_up = dot(ones, gub[...])[0:1]
    for c in range(wide // width):
        small[11 + c : 12 + c, :] = g_up[:, c * width : (c + 1) * width]
    if shared:
        (natural,) = refs
        turn(gyb, natural, turned_d, ids, 10, 4)
        traffic.ready(14)
        put = sender(send_1, early_place, (0,), EARLY_PARTS)
        first_products(put, 1, ids, turned_d, hidden)
        small_e[...] = rows_of_small(small[...])
        write_small(small, send_1, SENT_1)
        traffic.ready(12, 18)
        turn(a2, natural, turned_2, ids, 2, 8)
        turn(ctx, natural, turned_1, ids, 2, 8)
        turn(a3, natural, turned_3, ids, 2, 8)
        traffic.ready(15, 16, 17)
        put = sender(send_2, early_place, (None, 0, SENT_BASE), EARLY_PARTS)
        second_products(put, 1, ids, turned_3, turned_2, turned_1, cot_align, gub, gmb)


def last_kernel(peers, capacity, ids, arrived, dest_col, g_mid, out):
    fetch = fetching(dest_col[...], 0, peers, capacity)
    out[...] = (g_mid[...] + dot(fetch, arrived[...])).astype(BF16)


EARLY_PARTS, JOINED_ROWS = (576, 480, 480), 240
SENT_1, SENT_2, SENT_BASE, JOINED_BASE = 16 * 576, 16 * 960, 16 * 480, (0, 16 * 240)


def set_blocks(natural, out, ids, first, count, parts):
    size = natural.shape[0] // count // parts
    for j in range(count):
        for part in range(parts):
            to = part * count * size + ids[first + j] * size
            at = (j * parts + part) * size
            out[pl.ds(pl.multiple_of(to, size), size), :] = natural[at : at + size, :]


def turn(source, natural, out, ids, first, count):
    for c in range(source.shape[1] // 128):
        at = slice(c * 128, (c + 1) * 128)
        natural[at, :] = jnp.transpose(source[:, at].astype(F32)).astype(BF16)
    set_blocks(natural, out, ids, first, count, 1)


def spare_columns(ref, index, step, load):
    tile = pl.multiple_of((index * step) // 128 * 128, 128)
    part = ref[:, pl.ds(tile, load)].astype(F32)
    return jnp.where((index * step) % 128 == 64, pltpu.roll(part, load - 64, 1), part).astype(BF16)


def batch_relative(i):
    return (i >> 2) + (((i >> 1) & 1) << 1) + ((i & 1) << 2)


def joined_place(part, x, i):
    return (x * 8 + i) if part == 0 else (i >> 2) * 8 + x * 4 + (i & 3)


def early_place(part, x, i):
    y, low, high = i >> 2, (i >> 1) & 1, i & 1
    return (x * 8 + low * 4 + y * 2 + high, y * 8 + x * 4 + low * 2 + high, low * 8 + y * 4 + x * 2 + high)[part]


def sender(send, place, bases, sizes):
    def put(part, x, i, at, value):
        at = bases[part] + place(part, x, i) * sizes[part] + at
        send[at : at + value.shape[0], :] = value.astype(BF16)

    return put


def keeper(came, place, bases, sizes, outs):
    def put(part, x, i, at, value):
        where, count = place(part, x, i), value.shape[0]
        start = bases[part] + where * sizes[part] + at
        there = came[start : start + count, :].astype(F32)
        start = (where & 7) * sizes[part] + at
        outs[part][where >> 3][start : start + count, :] = (value + there).astype(BF16)

    return put


def split_small(value):
    high = value.astype(BF16)
    return high, (value - high.astype(F32)).astype(BF16)


def write_small(small, out, base):
    count = small.shape[0]
    for c in range(6):
        high, rest = split_small(small[:, c * 128 : (c + 1) * 128])
        out[base + c * count : base + (c + 1) * count, :] = high
        out[base + (6 + c) * count : base + (7 + c) * count, :] = rest


def both_small(small, came):
    high, rest = split_small(small)
    count = small.shape[0]
    there = came[:count].astype(F32) + came[count:].astype(F32)
    return (high.astype(F32) + rest.astype(F32)) + there


def rows_of_small(small):
    return jnp.concatenate([small[:, c * 128 : (c + 1) * 128] for c in range(6)], axis=0)


def own_columns(ids, core, x, step):
    return pl.ds(pl.multiple_of((ids[1] ^ (core + 2 * x)) * step, 128), step)


def first_products(put, core, ids, turned_d, hidden):
    for i in range(8):
        at = pl.ds(pl.multiple_of((ids[0] ^ batch_relative(i)) * 384, 128), 384)
        made = dot(turned_d[core * 384 : core * 384 + 384, :], hidden[:, at])
        for x in range(2):
            for c in range(3):
                put(0, x, i, c * 192, made[x * 192 : x * 192 + 192, c * 128 : c * 128 + 128])


def second_products(put, core, ids, turned_3, turned_2, turned_1, da, gub, gmb):
    for x in range(2):
        for c in range(3):
            at = pl.ds(pl.multiple_of((ids[1] ^ (core + 2 * x)) * 768 + c * 256, 128), 256)
            made = dot(turned_2[...], gub[:, at])
            for i in range(8):
                for half in range(2):
                    rows = made[i * 96 : i * 96 + 96, half * 128 : half * 128 + 128]
                    slab = 2 * c + half
                    put(1 + slab // 5, x, i, slab % 5 * 96, rows)
        align = dot(turned_3[...], da[:, own_columns(ids, core, x, 256)])
        out = dot(turned_1[...], spare_columns(gmb, ids[1] ^ (core + 2 * x), 192, 256))
        for i in range(8):
            for half in range(2):
                part = slice(half * 128, half * 128 + 128)
                put(2, x, i, 96 + half * 96, align[i * 96 : i * 96 + 96, part])
                put(2, x, i, 288 + half * 96, out[i * 96 : i * 96 + 96, part])


def joined_products(put, core, ids, turned, g_joined):
    for x in range(2):
        own = spare_columns(g_joined, ids[1] ^ (core + 2 * x), 576, 640)
        for c, slabs in ((0, 2), (2, 2), (4, 1)):
            made = dot(turned[...], own[:, c * 128 : (c + slabs) * 128])
            for part in range(2):
                for i in range(8):
                    at = part * 384 + i * 48
                    for k in range(slabs):
                        put(part, x, i, (c + k) * 48, made[at : at + 48, k * 128 : k * 128 + 128])


def first_keep(ids, turned_d, hidden, came, small, keep, send, total):
    put = keeper(came, early_place, (0,), EARLY_PARTS, ((keep, send),))
    first_products(put, 0, ids, turned_d, hidden)
    pass_small(small, came, SENT_1, total, send, 8 * EARLY_PARTS[0])


def second_keep(ids, turned_3, turned_2, turned_1, da, gub, gmb, came, keep_1, send_1, keep_2, send_2):
    outs = (None, (keep_1, send_1), (keep_2, send_2))
    put = keeper(came, early_place, (None, 0, SENT_BASE), EARLY_PARTS, outs)
    second_products(put, 0, ids, turned_3, turned_2, turned_1, da, gub, gmb)


def joined_keep(ids, turned, g_joined, came, small, keep_x, send_x, keep_y, send_y, total):
    outs = ((keep_x, send_x), (keep_y, send_y))
    put = keeper(came, joined_place, JOINED_BASE, (JOINED_ROWS,) * 2, outs)
    joined_products(put, 0, ids, turned, g_joined)
    pass_small_of(rows_of_small(small[...]), came, 32 * JOINED_ROWS, total, send_x, 8 * JOINED_ROWS)


def pass_small(small, came, from_row, total, send, to_row):
    pass_small_of(small[...], came, from_row, total, send, to_row)


def pass_small_of(small, came, from_row, total, send, to_row):
    count = small.shape[0]
    both = both_small(small, came[from_row : from_row + 2 * count, :])
    total[...] = both
    if send is not None:
        high, rest = split_small(both)
        send[to_row : to_row + count, :] = high
        send[to_row + count : to_row + 2 * count, :] = rest


def added(keep, came, at, count):
    rows = slice(at, at + count)
    return keep[rows, :].astype(F32) + came[rows, :].astype(F32)


def step_parts(ids, *refs):
    keeps, cames, small = refs[0:3], refs[3:6], refs[6]
    outs, sends, total = refs[7:10], refs[10:13], refs[13]
    for keep, came, out, send in zip(keeps, cames, outs, sends):
        half = keep.shape[0] // 2
        out[...] = added(keep, came, 0, half).astype(BF16)
        send[0:half, :] = added(keep, came, half, half).astype(BF16)
    half = keeps[0].shape[0] // 2
    pass_small(small, cames[0], 2 * half, total, sends[0], half)


def step_parts_last(ids, *refs):
    keeps, cames, small = refs[0:3], refs[3:6], refs[6]
    outs, send, total = refs[7:10], refs[10], refs[11]
    at = 0
    for keep, came, out in zip(keeps, cames, outs):
        half = keep.shape[0] // 2
        out[...] = added(keep, came, 0, half).astype(BF16)
        send[at : at + half, :] = added(keep, came, half, half).astype(BF16)
        at += half
    pass_small(small, cames[0], keeps[0].shape[0], total, send, at)


def step_apart(ids, keep_x, came_x, keep_y, came_y, *refs):
    small, out_x, send_x, out_y, send_y, total = refs
    half = keep_x.shape[0] // 2
    for keep, came, out, send in ((keep_x, came_x, out_x, send_x), (keep_y, came_y, out_y, send_y)):
        out[...] = added(keep, came, 0, half).astype(BF16)
        send[0:half, :] = added(keep, came, half, half).astype(BF16)
    pass_small(small, came_x, 2 * half, total, send_x, half)


def step_meet(ids, keep_x, came_x, keep_y, came_y, *refs):
    small, out, send, total = refs
    half = keep_x.shape[0] // 2
    for part, (keep, came) in enumerate(((keep_x, came_x), (keep_y, came_y))):
        at = slice(part * half, (part + 1) * half)
        out[at, :] = added(keep, came, 0, half).astype(BF16)
        send[at, :] = added(keep, came, half, half).astype(BF16)
    pass_small(small, came_x, 2 * half, total, send, 2 * half)


def step_joint(ids, keep, came, *refs):
    small, out, send, total = refs
    half = keep.shape[0] // 4
    for part in range(2):
        at = slice(part * half, (part + 1) * half)
        out[at, :] = added(keep, came, part * 2 * half, half).astype(BF16)
        send[at, :] = added(keep, came, part * 2 * half + half, half).astype(BF16)
    pass_small(small, came, 4 * half, total, send, 2 * half)


def small_columns(small, out):
    count = out.shape[0]
    for c in range(6):
        out[:, c * 128 : (c + 1) * 128] = small[c * count : (c + 1) * count]


def early_end(ids, keep_0, keep_1, keep_2, came, small, down, align, up, out, total):
    def block(keep, base, at, count):
        return keep[at : at + count, :].astype(F32) + came[base + at : base + at + count, :].astype(F32)

    for c in range(3):
        down[c * 128 : (c + 1) * 128, :] = jnp.transpose(block(keep_0, 0, c * 192, 192))
    for c in range(5):
        up[:, c * 128 : (c + 1) * 128] = block(keep_1, 576, c * 96, 96)
    up[:, 640:768] = block(keep_2, 1056, 0, 96)
    for c in range(2):
        align[:, c * 128 : (c + 1) * 128] = block(keep_2, 1056, 96 + c * 96, 96)
    out[:, 0:128] = block(keep_2, 1056, 288, 96)
    out[:, 128:192] = block(keep_2, 1056, 384, 96)[:, 0:64]
    count = small.shape[0]
    both = both_small(small[...], came[1536 : 1536 + 2 * count, :])
    small_columns(both, total)


def joined_end(ids, keep, came, small, out, total):
    for part in range(2):
        rows = slice(part * 48, part * 48 + 48)
        for c in range(4):
            out[rows, c * 128 : (c + 1) * 128] = added(keep, came, part * 240 + c * 48, 48)
        out[rows, 512:576] = added(keep, came, part * 240 + 192, 48)[:, 0:64]
    count = small.shape[0]
    both = both_small(small[...], came[480 : 480 + 2 * count, :])
    small_columns(both, total)


def flip(value, axis, bit, peers, groups):
    pairs = []
    for b in range(peers):
        for g in range(groups):
            other = (b ^ bit, g) if axis == "batch" else (b, g ^ bit)
            pairs.append((b * groups + g, other[0] * groups + other[1]))
    return lax.ppermute(value, AXES, pairs)


def tie(value, *others):
    return lax.optimization_barrier((value,) + others)[0]


def tiled_blocks(matrix, row_parts, column_parts):
    r, c = matrix.shape
    shaped = matrix.reshape(row_parts, r // row_parts, column_parts, c // column_parts)
    return jnp.transpose(shaped, (0, 2, 1, 3)).reshape(
        row_parts * column_parts, r // row_parts, c // column_parts
    )


def scattered(left, right, peers, groups):
    matrix = lax.dot_general(left, right, (((0,), (0,)), ((), ())), preferred_element_type=F32)
    return lax.psum_scatter(
        tiled_blocks(matrix, peers, groups), AXES, scatter_dimension=0, tiled=True
    )[0]


class Traffic:
    def __init__(self, loads, flushes):
        self.loads, self.flushes, self.left = loads, flushes, {}

    def need(self, *which):
        for k in which:
            copy = self.loads.pop(k, None)
            if copy is not None:
                copy.wait()

    def ready(self, *which):
        for k in which:
            if k in self.flushes:
                self.left[k] = self.flushes.pop(k)
                self.left[k].start()

    def finish(self):
        self.need(*list(self.loads))
        self.ready(*list(self.flushes))
        for copy in self.left.values():
            copy.wait()


def call(kernel, name, grant, out_shape, scratch, ids, *args, far=(), kept=(), load=(), flush=(), lazy=False, cost=0.001):
    n_in, n_out, n_scratch = len(args), len(out_shape), len(scratch)
    in_hbm, out_hbm = set(far) | set(load), {-1 - k for k in far} | set(flush)
    outs = [pltpu.HBM(o.shape, o.dtype) if k in kept or k in out_hbm else o for k, o in enumerate(out_shape)]
    own = [pltpu.VMEM(args[k].shape, args[k].dtype) for k in load] + [pltpu.VMEM(out_shape[k].shape, out_shape[k].dtype) for k in flush]
    if own:
        own.append(pltpu.SemaphoreType.DMA((len(own),)))

    def body(ids, *refs):
        ins, made, rest = list(refs[:n_in]), list(refs[n_in : n_in + n_out]), refs[n_in + n_out :]
        buffers = rest[n_scratch:]
        loads, flushes = {}, {}
        for i, k in enumerate(load):
            loads[k] = pltpu.make_async_copy(ins[k], buffers[i], buffers[-1].at[i])
            loads[k].start()
            ins[k] = buffers[i]
        for i, k in enumerate(flush, len(load)):
            flushes[k] = pltpu.make_async_copy(buffers[i], made[k], buffers[-1].at[i])
            made[k] = buffers[i]
        traffic = Traffic(loads, flushes)
        if lazy:
            kernel(traffic, ids, *ins, *made, *rest[:n_scratch])
        else:
            traffic.need(*load)
            kernel(ids, *ins, *made, *rest[:n_scratch])
        traffic.finish()

    return pl.pallas_call(
        body,
        name=name,
        out_shape=outs,
        in_specs=[SMEM] + [HBM if k in in_hbm else VMEM for k in range(n_in)],
        out_specs=[HBM if k in out_hbm else VMEM for k in range(n_out)],
        scratch_shapes=list(scratch) + own,
        compiler_params=pltpu.CompilerParams(vmem_limit_bytes=grant * 1_000_000),
        cost_estimate=pl.CostEstimate(flops=int(cost * 10**9), bytes_accessed=1, transcendentals=0),
    )(ids, *(pltpu.with_memory_space_constraint(a, pltpu.HBM) if k in in_hbm else a for k, a in enumerate(args)))


def exchange(blocks, peers, groups):
    if len(blocks) == 1:
        shaped = blocks[0].reshape(peers, blocks[0].shape[0] // peers, blocks[0].shape[1])
        moved = lax.all_to_all(shaped, "batch", split_axis=0, concat_axis=0, tiled=True)
        return [moved.reshape(blocks[0].shape)]
    came = {k: flip(blocks[k], "batch", k, peers, groups) for k in range(1, peers)}
    return [blocks[0]] + [came[k] for k in range(1, peers)]


def per_device(
    tokens, dest, seg_ids, cot_out, cot_align,
    ln1_gain, ln1_bias, w_qkv, q_bias, v_bias, w_out, out_bias,
    ln2_gain, ln2_bias, w_up, up_bias, w_down, down_bias,
    ln3_gain, ln3_bias, w_align, align_bias,
):
    rows, width = tokens.shape
    align = cot_align.shape[1]
    wide = w_up.shape[1]
    slots = seg_ids.shape[1]
    peers, groups = lax.axis_size("batch"), lax.axis_size("grp")
    capacity = slots // peers
    fast = peers == 8 and groups == 4 and (width, wide, align) == (768, 3072, 1024)
    blocks = 8 if fast else 1
    dest_row = dest.reshape(1, rows)
    seg_col = seg_ids.reshape(slots, 1)
    line = lambda v: v.reshape(1, v.shape[0])
    shape = jax.ShapeDtypeStruct
    vmem = pltpu.VMEM
    dma = pltpu.SemaphoreType.DMA
    count = slots // CLIPMAX
    low = lambda c: shape((rows, c), BF16)
    flat = lambda n: shape((n, 128), BF16)
    move = lambda value, axis, bit: flip(value, axis, bit, peers, groups)
    b, g = lax.axis_index("batch"), lax.axis_index("grp")
    place_b = b ^ jnp.arange(8)
    place_b = (place_b >> 2) + (((place_b >> 1) & 1) << 1) + ((place_b & 1) << 2)
    place_g = g ^ jnp.arange(4)
    place_g = (place_g >> 1) + ((place_g & 1) << 1)
    ids = jnp.concatenate([jnp.stack([b, g]), place_b, place_g]).astype(jnp.int32)

    packed = call(
        functools.partial(pack_kernel, peers, capacity), "pack_tokens", 56,
        [shape((slots // blocks, width), BF16)] * blocks, [],
        ids, dest_row, tokens,
    )
    packed = exchange(packed, peers, groups)

    in_slots = shape((slots, width), BF16)
    ctx, qkv, natural, a1, lse = call(
        functools.partial(attention_kernel, blocks), "attention", 56,
        [in_slots, shape((slots, 3 * width), BF16), in_slots, in_slots, shape((width // 128, count, 2 * CLIPMAX), F32)],
        [vmem((count, 3 * CLIPMAX, 2 * CLIPMAX), F32), vmem((128, slots), BF16), vmem((width, 3 * width), BF16),
         vmem((slots, 3 * width), BF16), vmem((slots, width), BF16), dma((blocks,)), dma, dma((2,))],
        ids, *packed, seg_ids, seg_col, line(ln1_gain), line(ln1_bias), w_qkv, line(q_bias), line(v_bias),
        far=tuple(range(blocks)) + (blocks + 4, -2, -3), kept=(3, 4),
    )
    (ctx,) = exchange([ctx], peers, groups)

    full = shape((rows, width), F32)
    joined, extra = JOINED_ROWS, 12 * 16
    chain = lambda n: [flat(n * EARLY_PARTS[0] + extra)] + [flat(n * r) for r in EARLY_PARTS[1:]]
    held = lambda n: [flat(n * r) for r in EARLY_PARTS]
    small_early = shape((96, 128), F32)
    turned = shape((width, rows), BF16)
    y, al, g_packed, g_mid, hidden, gub, a2, a3, ctx_rows, gyb, gmb, small_0, *sent = call(
        functools.partial(rows_kernel, peers, capacity, fast), "rows", 46,
        [low(width), low(align), in_slots, full, low(wide), low(wide), low(width), low(width), low(width), low(width), low(width),
         shape((16, width), F32)] + ([flat(SENT_1 + extra), flat(SENT_2), turned, turned, turned, turned, small_early] if fast else []),
        [vmem((rows, width), F32), vmem((rows, width), F32), vmem((rows, width), F32), vmem((rows, 128), F32), vmem((rows, wide), F32),
         vmem((rows, 512), F32), vmem((rows, 512), F32), vmem((rows, 512), BF16), vmem((rows, 512), BF16),
         vmem((2, 8, width), F32), vmem(w_out.shape, BF16), vmem(w_up.shape, BF16), vmem(w_down.shape, BF16),
         vmem(w_align.shape, BF16), dma((4,))] + ([vmem((width, rows), BF16)] if fast else []),
        ids, ctx, tokens, dest, dest_row, cot_out, cot_align,
        w_out, line(out_bias), line(ln2_gain), line(ln2_bias), w_up, line(up_bias), w_down, line(down_bias),
        line(ln3_gain), line(ln3_bias), w_align, line(align_bias),
        far=(6, 10, 12, 16), flush=(0, 1, 2, 3, 4, 5, 10) + ((12, 13, 14, 15, 16, 17, 18) if fast else ()), kept=(6, 7, 8, 9, 11), lazy=True,
    )
    (g_arrived,) = exchange([g_packed], peers, groups)

    if fast:
        send_1, send_2, turned_d, turned_3, turned_2, turned_1, small_e = sent
        came_2 = move(send_2, "grp", 1)
        came_1 = move(send_1, "grp", 1)
        routes = (
            (("grp", 2), ("batch", 2), ("batch", 1)),
            (("batch", 1), ("grp", 2), ("batch", 2)),
            (("batch", 2), ("batch", 1), ("grp", 2)),
        )
        go = lambda sends, k: [move(send, *route[k]) for send, route in zip(sends, routes)]
        k1, s1, k2, s2 = call(
            second_keep, "second_keep", 24, [held(8)[1], held(8)[1], held(8)[2], held(8)[2]], [],
            ids, turned_3, turned_2, turned_1, cot_align, gub, gmb, came_2,
            load=(0, 1, 2, 3, 4, 5), flush=(0, 2),
        )
        k0, s0, small_e = call(
            first_keep, "first_keep", 20, [held(8)[0], chain(8)[0], small_early], [],
            ids, turned_d, hidden, tie(came_1, s1), small_e,
            load=(0, 1), flush=(0,),
        )
        keeps, sends = [k0, k1, k2], [s0, s1, s2]
        cames = go(sends, 0)
        g_arrived = tie(g_arrived, s0)

    more = 12 * 8
    outs = [in_slots, shape((slots, 3 * width), BF16), shape((8, width), F32)]
    turned = shape((width, slots), BF16)
    made = call(
        functools.partial(attention_back_kernel, fast), "attention_back", 28,
        outs + ([flat(32 * joined + more), turned] if fast else []),
        [vmem((count, 3 * CLIPMAX, 2 * CLIPMAX), F32), vmem((128, slots), BF16), vmem((slots, 128), F32), vmem((slots, 128), F32),
         vmem((slots, width), F32), vmem((2, 8, width), F32), vmem((width, 3 * width), BF16), dma]
        + ([vmem((width, slots), BF16)] if fast else []),
        ids, g_arrived, natural, qkv, lse, a1, seg_ids, seg_col, line(ln1_gain), w_qkv,
        far=(8,), load=(1, 6, 2, 3, 4), flush=(0, 4) if fast else (0,), lazy=True,
    )
    g_rows, g_joined, small_2 = made[:3]
    (g_back,) = exchange([g_rows], peers, groups)

    if fast:
        send, turned_c = made[3:]
        came = move(send, "grp", 1)
        small_shape = shape((48, 128), F32)

        def early_step(name, n, keeps, cames, small_e, before, cost, **more_of):
            made = call(
                step_parts, name, 14, held(n) + chain(n) + [small_early], [],
                ids, *keeps, tie(cames[0], before), *cames[1:], small_e, cost=cost, **more_of,
            )
            return made[0:3], made[3:6], made[6]

        keeps, sends, small_e = early_step("early_step_1", 4, keeps, cames, small_e, send, 15, load=(0, 1, 2, 6), flush=(0, 1, 2))
        cames = go(sends, 1)
        kx3, sx3, ky3, sy3, small_j = call(
            joined_keep, "joined_keep", 12, [flat(8 * joined), flat(8 * joined + more), flat(8 * joined), flat(8 * joined), small_shape], [],
            ids, turned_c, g_joined, tie(came, sends[0]), small_2,
        )
        cx3, cy3 = move(sx3, "grp", 2), move(sy3, "batch", 1)
        keeps, sends, small_e = early_step("early_step_2", 2, keeps, cames, small_e, sx3, 0.001, load=(0, 1, 2))
        cames = go(sends, 2)
        kx3, sx3, ky3, sy3, small_j = call(
            step_apart, "joined_apart", 10, [flat(4 * joined), flat(4 * joined + more), flat(4 * joined), flat(4 * joined), small_shape], [],
            ids, kx3, tie(cx3, sends[0]), ky3, cy3, small_j,
        )
        cx3, cy3 = move(sx3, "batch", 1), move(sy3, "grp", 2)
        *keeps, send, small_e = call(
            step_parts_last, "early_step_3", 10, held(1) + [flat(1536 + extra), small_early], [],
            ids, *keeps, tie(cames[0], sx3), *cames[1:], small_e,
        )
        last = move(send, "batch", 4)
        k3, s3, small_j = call(
            step_meet, "joined_meet", 10, [flat(4 * joined), flat(4 * joined + more), small_shape], [],
            ids, kx3, tie(cx3, send), ky3, cy3, small_j,
        )
        c3 = move(s3, "batch", 2)
        k3, s3, small_j = call(
            step_joint, "joined_joint", 10, [flat(2 * joined), flat(2 * joined + more), small_shape], [],
            ids, k3, c3, small_j,
        )
        c3 = move(s3, "batch", 4)
        sum_down, sum_align, sum_up, sum_out, small_e = call(
            early_end, "early_end", 10,
            [shape((384, 192), F32), shape((96, 256), F32), shape((96, 768), F32), shape((96, 192), F32), shape((16, width), F32)], [],
            ids, *keeps, tie(last, s3), small_e,
        )
        g_back = tie(g_back, s3)
        sum_qkv, small_j = call(
            joined_end, "joined_end", 10, [shape((96, 576), F32), shape((8, width), F32)], [],
            ids, k3, tie(c3, sum_out), small_j,
        )
        small_0, small_2 = small_e, small_j
    else:
        sum_up, sum_align, sum_out, sum_down, sum_qkv = (
            scattered(a2, gub, peers, groups),
            scattered(a3, cot_align, peers, groups),
            scattered(ctx_rows, gmb, peers, groups),
            scattered(hidden, gyb, peers, groups),
            scattered(a1, g_joined, peers, groups),
        )
        small_0, small_2 = lax.psum((small_0, small_2), AXES)

    (grad_tokens,) = call(
        functools.partial(last_kernel, peers, capacity), "grad_tokens", 8, [low(width)], [],
        ids, g_back, dest, g_mid,
    )
    sum_align_bias = small_0[3:5].reshape(2 * width)[:align]
    sum_up_bias = small_0[11:15].reshape(4 * width)[:wide]
    return (
        y, al, grad_tokens,
        small_2[0], small_2[1], sum_qkv, small_2[2], small_2[3],
        sum_out, small_0[10], small_0[8], small_0[9],
        sum_up, sum_up_bias, sum_down, small_0[2],
        small_0[0], small_0[1], sum_align, sum_align_bias,
    )


def solution(mesh):
    row, one = P(AXES, None), P()
    matrix = P("batch", "grp")
    return jax.shard_map(
        per_device,
        mesh=mesh,
        in_specs=(row,) * 5 + (one,) * 17,
        out_specs=(
            row, row, row, one, one, matrix, one, one, matrix, one,
            one, one, matrix, one, matrix, one, one, one, matrix, one,
        ),
        check_vma=False,
    )
```

```python
import functools

import jax
import jax.numpy as jnp
from jax import lax
from jax.experimental import pallas as pl
from jax.experimental.pallas import tpu as pltpu
from jax.sharding import PartitionSpec as P

H = 12
CLIPMAX = 128
EPS = 1e-06
MASKED = -1e30
DEAD = 16.0
AXES = ("batch", "grp")
SMEM = pl.BlockSpec(memory_space=pltpu.SMEM)
VMEM = pl.BlockSpec(memory_space=pltpu.VMEM)
HBM = pl.BlockSpec(memory_space=pltpu.HBM)
F32 = jnp.float32
BF16 = jnp.bfloat16


def dot(a, b):
    return jnp.dot(a, b, preferred_element_type=F32)


def dot_nt(a, b):
    return lax.dot_general(a, b, (((1,), (1,)), ((), ())), preferred_element_type=F32)


def dot_tn(a, b):
    return lax.dot_general(a, b, (((0,), (0,)), ((), ())), preferred_element_type=F32)


def iota(shape, axis):
    return lax.broadcasted_iota(jnp.int32, shape, axis)


def row_loop(total, step, body):
    def one(i, carry):
        body(pl.ds(pl.multiple_of(i * step, step), step))
        return carry

    lax.fori_loop(0, total // step, one, 0)


def norm_parts(v):
    centered = v - jnp.mean(v, axis=-1, keepdims=True)
    rstd = lax.rsqrt(jnp.mean(centered * centered, axis=-1, keepdims=True) + EPS)
    return centered * rstd, rstd


def norm_back(g_out, gain, hat, rstd):
    t = g_out * gain
    return rstd * (
        t - jnp.mean(t, axis=-1, keepdims=True) - hat * jnp.mean(t * hat, axis=-1, keepdims=True)
    )


def slot_column(dest_col, me, peers, capacity):
    rows = dest_col.shape[0]
    onehot = (dest_col == iota((rows, peers), 1)).astype(F32)
    before = (iota((rows, rows), 0) > iota((rows, rows), 1)).astype(BF16)
    earlier = dot(before, onehot.astype(BF16))
    offset = jnp.sum(earlier * onehot, axis=1, keepdims=True).astype(jnp.int32)
    return (dest_col ^ me) * capacity + offset


def slot_row(dest_row, me, peers, capacity):
    rows = dest_row.shape[1]
    onehot = (dest_row == iota((peers, rows), 0)).astype(F32)
    before = (iota((rows, rows), 0) < iota((rows, rows), 1)).astype(BF16)
    earlier = dot(onehot.astype(BF16), before)
    offset = jnp.sum(earlier * onehot, axis=0, keepdims=True).astype(jnp.int32)
    return (dest_row ^ me) * capacity + offset


def placing(dest_row, me, peers, capacity):
    shape = (peers * capacity, dest_row.shape[1])
    return iota(shape, 0) == slot_row(dest_row, me, peers, capacity)


def fetching(dest_col, me, peers, capacity):
    shape = (dest_col.shape[0], peers * capacity)
    return (iota(shape, 1) == slot_column(dest_col, me, peers, capacity)).astype(BF16)


def own_index(ids, blocks):
    return ids[0] if blocks > 1 else 0


ORDER = (0, 1, 2, 3, 4, 5, 6, 7)


def block_rows(ids, k, refs):
    size = refs[0].shape[0]
    if len(refs) == 1:
        return pl.ds(0, size)
    return pl.ds(pl.multiple_of((ids[0] ^ ORDER[k]) * size, size), size)


def pack_kernel(peers, capacity, ids, dest_row, tokens, *outs):
    place = placing(dest_row[...], own_index(ids, len(outs)), peers, capacity)
    held = jnp.sum(place.astype(F32), axis=1, keepdims=True)
    rows = jnp.where(held > 0.5, dot(place.astype(BF16), tokens[...]), DEAD).astype(BF16)
    size = outs[0].shape[0]
    for out, k in zip(outs, ORDER):
        out[...] = rows[k * size : (k + 1) * size]


def windows(slots):
    block = CLIPMAX
    return [
        (n * block, max(0, (n - 1) * block), min(slots, (n + 2) * block))
        for n in range(slots // block)
    ]


def write_bias(packed, seg_row, seg_col, bias):
    block = CLIPMAX
    live = packed[:, 0:1].astype(F32) < DEAD * 0.5
    for n, (start, low, high) in enumerate(windows(packed.shape[0])):
        shape, keys = (high - low, block), slice(low, high)
        same = seg_col[keys, :] == seg_row[:, start : start + block]
        own = (low + iota(shape, 0)) == (start + iota(shape, 1))
        made = jnp.where(same & (live[keys, :] | own), 0.0, MASKED)
        bias[n, 0 : high - low, 0:block] = made
        bias[n, 0 : high - low, block:] = made


def stacked(rows):
    first = iota(rows.shape, 1) < 64
    zero = jnp.zeros_like(rows)
    return jnp.concatenate([jnp.where(first, rows, zero), jnp.where(first, zero, rows)], axis=0)


def unstacked(turned):
    half = turned.shape[1] // 2
    upper = iota((128, half), 0) < 64
    return jnp.transpose(jnp.where(upper, turned[:, :half], turned[:, half:]))


def attention_kernel(blocks, ids, *refs):
    arrived, refs = refs[:blocks], refs[blocks:]
    (seg_row, seg_col, gain, shift, w_hbm, q_bias, v_bias,
     ctx, qkv_out, natural_out, a1, lse,
     bias, turned_v, w_qkv, qkv, packed, in_sems, w_sem, out_sems) = refs
    slots, width = packed.shape
    block = CLIPMAX
    fetches = []
    for k, ref in enumerate(arrived):
        to = packed.at[block_rows(ids, k, arrived), :]
        fetches.append(pltpu.make_async_copy(ref, to, in_sems.at[k]))
        fetches[-1].start()
    weights = pltpu.make_async_copy(w_hbm, w_qkv, w_sem)
    weights.start()
    for fetch in fetches:
        fetch.wait()
    keep = pltpu.make_async_copy(packed, natural_out, out_sems.at[0])
    keep.start()
    write_bias(packed, seg_row, seg_col, bias)
    gain_f, shift_f = gain[...].astype(F32), shift[...].astype(F32)

    def norm_rows(r):
        x = packed[r, :].astype(F32)
        x = jnp.where(x[:, 0:1] < DEAD * 0.5, x, 0.0)
        hat, _ = norm_parts(x)
        a1[r, :] = (hat * gain_f + shift_f).astype(BF16)

    row_loop(slots, 32, norm_rows)
    weights.wait()

    piece = 256
    for part, part_bias in ((0, q_bias), (1, None), (2, v_bias)):
        for c in range(width // piece):
            cols = slice(part * width + c * piece, part * width + (c + 1) * piece)
            made = dot(a1[...], w_qkv[:, cols])
            if part_bias is not None:
                made = made + part_bias[:, c * piece : (c + 1) * piece].astype(F32)
            qkv[:, cols] = made.astype(BF16)
    keep_qkv = pltpu.make_async_copy(qkv, qkv_out, out_sems.at[1])
    keep_qkv.start()

    scale = jnp.asarray(64**-0.5, BF16)

    def pair(hp, carry):
        def lanes(part):
            return pl.ds(pl.multiple_of(part * width + hp * 128, 128), 128)

        turned_v[...] = jnp.transpose(qkv[:, lanes(2)].astype(F32)).astype(BF16)
        scores = []
        for n, (start, low, high) in enumerate(windows(slots)):
            q = stacked(qkv[start : start + block, lanes(0)] * scale)
            scores.append(dot_nt(qkv[low:high, lanes(1)], q) + bias[n, 0 : high - low, :])
        for n, (start, low, high) in enumerate(windows(slots)):
            s = scores[n]
            top = jnp.max(s, axis=0, keepdims=True)
            e = jnp.exp(s - top)
            total = jnp.sum(e, axis=0, keepdims=True)
            lse[hp, n : n + 1, :] = top + jnp.log(total)
            found = dot(turned_v[:, low:high], e.astype(BF16)) * (1.0 / total)
            ctx[start : start + block, lanes(0)] = unstacked(found).astype(BF16)
        return carry

    lax.fori_loop(0, width // 128, pair, 0)
    keep.wait()
    keep_qkv.wait()


def attention_back_kernel(shared, traffic, ids, *refs):
    (g_ctx, packed, qkv, lse, a1, seg_row, seg_col, gain, w_hbm), refs = refs[:9], refs[9:]
    (g_rows, g_joined, small), refs = refs[:3], refs[3:]
    if shared:
        (send, turned), refs = refs[:2], refs[2:]
    bias, turned_k, gk, gv, acc, sums, w_qkv, w_sem = refs[:8]
    slots, width = packed.shape
    block = CLIPMAX
    weights = pltpu.make_async_copy(w_hbm, w_qkv, w_sem)
    weights.start()
    traffic.need(1, 6)
    write_bias(packed, seg_row, seg_col, bias)
    traffic.need(2, 3, 4)
    scale = jnp.asarray(64**-0.5, BF16)

    def pair(hp, carry):
        def lanes(part):
            return pl.ds(pl.multiple_of(part * width + hp * 128, 128), 128)

        if shared:
            a1_turned = refs[8]
            a1_turned[lanes(0), :] = jnp.transpose(a1[:, lanes(0)].astype(F32)).astype(BF16)
        turned_k[...] = jnp.transpose(qkv[:, lanes(1)].astype(F32)).astype(BF16)
        gk[...] = jnp.zeros_like(gk)
        gv[...] = jnp.zeros_like(gv)
        first = []
        for n, (start, low, high) in enumerate(windows(slots)):
            here = slice(start, start + block)
            q = stacked(qkv[here, lanes(0)] * scale)
            g = stacked(g_ctx[here, lanes(0)])
            s = dot_nt(qkv[low:high, lanes(1)], q) + bias[n, 0 : high - low, :]
            first.append((q, g, s, dot_nt(qkv[low:high, lanes(2)], g)))
        for n, (start, low, high) in enumerate(windows(slots)):
            here = slice(start, start + block)
            q, g, s, gp = first[n]
            p = jnp.exp(s - lse[hp, n : n + 1, :])
            inner = jnp.sum(gp * p, axis=0, keepdims=True)
            gs = (p * (gp - inner)).astype(BF16)
            gv[low:high, :] += dot(p.astype(BF16), g)
            gk[low:high, :] += dot(gs, q)
            gq = dot(turned_k[:, low:high], gs) * (64**-0.5)
            g_joined[here, lanes(0)] = unstacked(gq).astype(BF16)
        g_joined[:, lanes(1)] = gk[...].astype(BF16)
        g_joined[:, lanes(2)] = gv[...].astype(BF16)
        return carry

    lax.fori_loop(0, width // 128, pair, 0)

    weights.wait()
    acc[...] = dot_nt(g_joined[...], w_qkv[...])
    ones = jnp.ones((8, slots), BF16)
    small[2:3, :] = dot(ones, g_joined[:, 0:width])[0:1]
    small[3:4, :] = dot(ones, g_joined[:, 2 * width :])[0:1]
    small[4:8, :] = jnp.zeros_like(small[4:8, :])
    sums[...] = jnp.zeros_like(sums)
    gain_f = gain[...].astype(F32)

    def back_rows(r):
        x = packed[r, :].astype(F32)
        x = jnp.where(x[:, 0:1] < DEAD * 0.5, x, 0.0)
        hat, rstd = norm_parts(x)
        g_out = acc[r, :]
        sums[0] += folded(g_out * hat)
        sums[1] += folded(g_out)
        g_rows[r, :] = norm_back(g_out, gain_f, hat, rstd).astype(BF16)

    row_loop(slots, 32, back_rows)
    small[0:1, :] = jnp.sum(sums[0], axis=0, keepdims=True)
    small[1:2, :] = jnp.sum(sums[1], axis=0, keepdims=True)
    if shared:
        set_blocks(refs[8], turned, 0, ids, 2, 8, JOINED_SPLIT)
        joined_products(sender(send, joined_place, JOINED_BASE, JOINED_PARTS), 1, ids, turned, g_joined)
        write_small(small, send, 16 * sum(JOINED_PARTS))


def folded(rows):
    total = rows[0:8]
    for i in range(8, rows.shape[0], 8):
        total = total + rows[i : i + 8]
    return total


def gelu_parts(u):
    bell = jnp.exp(-0.5 * u * u)
    t = 1.0 / (1.0 + 0.305 * jnp.abs(u))
    poly = 0.03669796139001846
    for c in (
        -0.15298233926296234, 0.18570539355278015, -0.03796539083123207, 0.12101536989212036,
        0.10342279821634293, 0.12246651202440262, 0.12163975089788437,
    ):
        poly = poly * t + c
    tail = bell * (poly * t)
    below = jnp.where(u < 0.0, tail, 1.0 - tail)
    return below, below + u * (bell * 0.3989422804014327)


def rows_kernel(peers, capacity, shared, traffic, ids, *refs):
    (whole, tokens, dest_col, dest_row, cot_out, cot_align, out_hbm, out_bias, gain2, shift2, up_hbm, up_bias, down_hbm, down_bias,
     gain3, shift3, align_hbm, align_bias), refs = refs[:18], refs[18:]
    (y_out, al_out, g_packed, g_mid, hidden, gub, a2, a3, ctx, gyb, gmb, small), refs = refs[:12], refs[12:]
    if shared:
        (send, own), refs = refs[:2], refs[2:]
    (mid, acc, hat2, rstd2, slope, u_a, u_b, h_a, h_b, sums, w_out, w_up, w_down, w_align, sems), refs = refs[:15], refs[15:]
    rows, width = tokens.shape
    wide = hidden.shape[1]
    piece = u_a.shape[1]
    loads = [
        pltpu.make_async_copy(source, to, sems.at[k])
        for k, (source, to) in enumerate(
            ((out_hbm, w_out), (up_hbm, w_up), (down_hbm, w_down), (align_hbm, w_align))
        )
    ]
    for load in loads:
        load.start()

    fetch = fetching(dest_col[...], 0, peers, capacity)
    ctx[...] = dot(fetch, whole[...]).astype(BF16)
    loads[0].wait()
    acc[...] = dot(ctx[...], w_out[...])

    def to_mid(r):
        m = tokens[r, :].astype(F32) + acc[r, :] + out_bias[...].astype(F32)
        hat, rstd = norm_parts(m)
        hat2[r, :] = hat
        rstd2[r, :] = jnp.broadcast_to(rstd, (rstd.shape[0], 128))
        a2[r, :] = (hat * gain2[...].astype(F32) + shift2[...].astype(F32)).astype(BF16)
        acc[r, :] = m + down_bias[...].astype(F32)

    row_loop(rows, 32, to_mid)

    def columns(i):
        return pl.ds(pl.multiple_of(i * piece, piece), piece)

    def up(i):
        return dot(a2[...], w_up[:, columns(i)]) + up_bias[:, columns(i)].astype(F32)

    def bend(i, u_ref, h_ref):
        u = u_ref[...]
        below, bent = gelu_parts(u)
        slope[:, columns(i)] = bent
        made = (u * below).astype(BF16)
        hidden[:, columns(i)] = made
        h_ref[...] = made

    last = wide // piece - 1
    h_b[...] = jnp.zeros_like(h_b)
    loads[1].wait()
    u_a[...] = up(0)
    loads[2].wait()

    def two(j, carry):
        u_b[...] = up(2 * j + 1)
        acc[...] += dot(h_b[...], w_down[columns(jnp.maximum(2 * j - 1, 0)), :])
        bend(2 * j, u_a, h_a)
        u_a[...] = up(jnp.minimum(2 * j + 2, last))
        acc[...] += dot(h_a[...], w_down[columns(2 * j), :])
        bend(2 * j + 1, u_b, h_b)
        return carry

    lax.fori_loop(0, (last + 1) // 2, two, 0)
    acc[...] += dot(h_b[...], w_down[columns(last), :])
    traffic.ready(4)

    def to_a3(r):
        y = acc[r, :]
        y_out[r, :] = y.astype(BF16)
        hat, _ = norm_parts(y)
        a3[r, :] = (hat * gain3[...].astype(F32) + shift3[...].astype(F32)).astype(BF16)

    row_loop(rows, 32, to_a3)
    loads[3].wait()
    al_out[...] = (dot(a3[...], w_align[...]) + align_bias[...].astype(F32)).astype(BF16)
    traffic.ready(0, 1)
    mid[...] = dot_nt(cot_align[...], w_align[...])
    sums[...] = jnp.zeros_like(sums)

    def back3(r):
        hat, rstd = norm_parts(acc[r, :])
        g_out = mid[r, :]
        gy = cot_out[r, :].astype(F32) + norm_back(g_out, gain3[...].astype(F32), hat, rstd)
        g_mid[r, :] = gy
        gyb[r, :] = gy.astype(BF16)
        sums[0] += folded(g_out * hat)
        sums[1] += folded(g_out)

    row_loop(rows, 32, back3)
    small[...] = jnp.zeros_like(small)
    small[0:1, :] = jnp.sum(sums[0], axis=0, keepdims=True)
    small[1:2, :] = jnp.sum(sums[1], axis=0, keepdims=True)
    ones = jnp.ones((8, rows), BF16)
    small[2:3, :] = dot(ones, gyb[...])[0:1]
    align = dot(ones, cot_align[...])[0:1]
    small[3:4, :] = align[:, :width]
    small[4:5, 0 : align.shape[1] - width] = align[:, width:]

    acc[...] = jnp.zeros_like(acc)
    for c in range(wide // 512):
        cols = slice(c * 512, (c + 1) * 512)
        low = (slope[:, cols] * dot_nt(gyb[...], w_down[cols, :])).astype(BF16)
        gub[:, cols] = low
        acc[...] += dot_nt(low, w_up[:, cols])
    traffic.ready(5)
    sums[...] = jnp.zeros_like(sums)

    def back2(r):
        hat, g_out = hat2[r, :], acc[r, :]
        gm = g_mid[r, :] + norm_back(g_out, gain2[...].astype(F32), hat, rstd2[r, 0:1])
        g_mid[r, :] = gm
        gmb[r, :] = gm.astype(BF16)
        sums[0] += folded(g_out * hat)
        sums[1] += folded(g_out)

    row_loop(rows, 32, back2)
    traffic.ready(3, 10)
    g_ctx = dot_nt(gmb[...], w_out[...]).astype(BF16)
    place = placing(dest_row[...], 0, peers, capacity).astype(BF16)
    g_packed[...] = dot(place, g_ctx).astype(BF16)
    traffic.ready(2)
    small[8:9, :] = jnp.sum(sums[0], axis=0, keepdims=True)
    small[9:10, :] = jnp.sum(sums[1], axis=0, keepdims=True)
    small[10:11, :] = dot(ones, gmb[...])[0:1]
    g_up = dot(ones, gub[...])[0:1]
    for c in range(wide // width):
        small[11 + c : 12 + c, :] = g_up[:, c * width : (c + 1) * width]
    if shared:
        natural, turned_d = refs
        turn(gyb, natural, turned_d, 0, ids, 10, 4)
        own[OWN_D : OWN_D + 384, :] = turned_d[0:384, :]
        send[AT_D : AT_D + 384, :] = turned_d[384:768, :]
        for core, out, align_at, out_at in ((0, own, OWN_ALIGN, OWN_OUT), (1, send, AT_ALIGN, AT_OUT)):
            for x in range(2):
                at = slice(align_at + x * 256, align_at + x * 256 + 256)
                out[at, :] = cot_align[:, own_columns(ids, core, x, 256)]
                at = slice(out_at + x * 256, out_at + x * 256 + 256)
                out[at, :] = spare_columns(gmb, ids[1] ^ (core + 2 * x), 192, 256)
        turn(a3, natural, send, AT_3, ids, 2, 8)
        turn(ctx, natural, send, AT_1, ids, 2, 8)
        turn(a2, natural, send, AT_2, ids, 2, 8)
        for core, out, up_at in ((0, own, OWN_UP), (1, send, AT_UP)):
            for x in range(2):
                for c in range(3):
                    at = pl.ds(pl.multiple_of((ids[1] ^ (core + 2 * x)) * 768 + c * 256, 128), 256)
                    to = up_at + (x * 3 + c) * 256
                    out[to : to + 256, :] = gub[:, at]
        for c in range(3):
            high, rest = split_small(small[:, c * 256 : (c + 1) * 256])
            send[AT_SMALL + c * 16 : AT_SMALL + c * 16 + 16, :] = high
            send[AT_SMALL + 48 + c * 16 : AT_SMALL + 64 + c * 16, :] = rest


def last_kernel(peers, capacity, ids, arrived, dest_col, g_mid, out):
    fetch = fetching(dest_col[...], 0, peers, capacity)
    out[...] = (g_mid[...] + dot(fetch, arrived[...])).astype(BF16)


EARLY_PARTS, JOINED_PARTS, JOINED_SPLIT = (576, 576, 384), (240, 240), (48, 48)
JOINED_BASE = (0, 16 * 240)
AT_2, AT_3, AT_1, AT_D, AT_UP, AT_ALIGN, AT_OUT, AT_SMALL, SENT = 0, 768, 1536, 2304, 2688, 4224, 4736, 5248, 5344
OWN_D, OWN_UP, OWN_ALIGN, OWN_OUT, OWN = 0, 384, 1920, 2432, 2944


def set_blocks(natural, out, base, ids, first, count, sizes):
    at = 0
    for j in range(count):
        start = base
        for size in sizes:
            to = start + ids[first + j] * size
            out[pl.ds(pl.multiple_of(to, 16), size), :] = natural[at : at + size, :]
            at, start = at + size, start + count * size


def turn_into(source, natural):
    for c in range(source.shape[1] // 128):
        at = slice(c * 128, (c + 1) * 128)
        natural[at, :] = jnp.transpose(source[:, at].astype(F32)).astype(BF16)


def turn(source, natural, out, base, ids, first, count):
    turn_into(source, natural)
    set_blocks(natural, out, base, ids, first, count, (source.shape[1] // count,))


def spare_columns(ref, index, step, load):
    tile = pl.multiple_of((index * step) // 128 * 128, 128)
    part = ref[:, pl.ds(tile, load)].astype(F32)
    return jnp.where((index * step) % 128 == 64, pltpu.roll(part, load - 64, 1), part).astype(BF16)


def batch_relative(i):
    return (i >> 2) + (((i >> 1) & 1) << 1) + ((i & 1) << 2)


def joined_place(part, x, i):
    return (x * 8 + i) if part == 0 else (i >> 2) * 8 + x * 4 + (i & 3)


def early_place(part, x, i):
    y, low, high = i >> 2, (i >> 1) & 1, i & 1
    return (x * 8 + low * 4 + y * 2 + high, y * 8 + x * 4 + high * 2 + low, low * 8 + y * 4 + x * 2 + high)[part]


def sender(send, place, bases, sizes):
    def put(part, x, i, at, value):
        at = bases[part] + place(part, x, i) * sizes[part] + at
        send[at : at + value.shape[0], :] = value.astype(BF16)

    return put


def keeper(came, place, bases, sizes, outs):
    def put(part, x, i, at, value):
        where, count = place(part, x, i), value.shape[0]
        start = bases[part] + where * sizes[part] + at
        there = came[start : start + count, :].astype(F32)
        start = (where & 7) * sizes[part] + at
        outs[part][where >> 3][start : start + count, :] = (value + there).astype(BF16)

    return put


def split_small(value):
    high = value.astype(BF16)
    return high, (value - high.astype(F32)).astype(BF16)


def write_small(small, out, base):
    count = small.shape[0]
    for c in range(6):
        high, rest = split_small(small[:, c * 128 : (c + 1) * 128])
        out[base + c * count : base + (c + 1) * count, :] = high
        out[base + (6 + c) * count : base + (7 + c) * count, :] = rest


def both_small(small, came):
    high, rest = split_small(small)
    count = small.shape[0]
    there = came[:count].astype(F32) + came[count:].astype(F32)
    return (high.astype(F32) + rest.astype(F32)) + there


def rows_of_small(small):
    return jnp.concatenate([small[:, c * 128 : (c + 1) * 128] for c in range(6)], axis=0)


def own_columns(ids, core, x, step):
    return pl.ds(pl.multiple_of((ids[1] ^ (core + 2 * x)) * step, 128), step)


def joined_products(put, core, ids, turned, g_joined):
    for x in range(2):
        own = spare_columns(g_joined, ids[1] ^ (core + 2 * x), 576, 640)
        for c, slabs in ((0, 2), (2, 2), (4, 1)):
            made = dot(turned[...], own[:, c * 128 : (c + slabs) * 128])
            for part, size in enumerate(JOINED_SPLIT):
                for i in range(8):
                    at = part * 8 * JOINED_SPLIT[0] + i * size
                    for k in range(slabs):
                        put(part, x, i, (c + k) * size, made[at : at + size, k * 128 : k * 128 + 128])


def writer(outs):
    def put(part, x, i, at, value):
        where, count = early_place(part, x, i), value.shape[0]
        start = (where & 7) * EARLY_PARTS[part] + at
        outs[part][where >> 3][start : start + count, :] = value.astype(BF16)

    return put


def fetch_rows(pieces, sems):
    copies = []
    for k, (source, at, buffer) in enumerate(pieces):
        source = source if at is None else source.at[pl.ds(at, buffer.shape[0]), :]
        copies.append(pltpu.make_async_copy(source, buffer, sems.at[k]))
        copies[-1].start()
    return copies


def first_grads(
    traffic, ids, hidden_hbm, came_hidden_hbm, sent, own, came, keep_1, send_1, keep_2, send_2,
    turned_o, turned_c, ends_o, ends_c, down_o, down_c, hidden, came_hidden, sems,
):
    copies = fetch_rows(
        ((sent, AT_3, turned_o), (came, AT_3, turned_c), (own, OWN_ALIGN, ends_o), (came, AT_ALIGN, ends_c),
         (own, OWN_D, down_o), (came, AT_D, down_c), (hidden_hbm, None, hidden), (came_hidden_hbm, None, came_hidden)),
        sems,
    )
    put = writer((None, (keep_1, send_1), (keep_2, send_2)))
    for copy in copies[:4]:
        copy.wait()
    for x in range(2):
        for k, shift in ((0, 0), (1, 192)):
            turned = slice(k * 768, k * 768 + 768)
            at = slice(k * 512 + x * 256, k * 512 + x * 256 + 256)
            made = dot(turned_o[turned, :], ends_o[at, :])
            made += dot(turned_c[turned, :], ends_c[at, :])
            for i in range(8):
                for half in range(2):
                    put(2, x, i, shift + half * 96, made[i * 96 : i * 96 + 96, half * 128 : half * 128 + 128])
    traffic.ready(2, 3)
    for copy in copies[4:]:
        copy.wait()
    for i in (4, 5, 6, 7, 0, 1, 2, 3):
        at = pl.ds(pl.multiple_of((ids[0] ^ batch_relative(i)) * 384, 128), 384)
        made = dot(down_o[...], hidden[:, at])
        made += dot(down_c[...], came_hidden[:, at])
        for x in range(2):
            for c in range(3):
                put(1, x, i, c * 192, made[x * 192 : x * 192 + 192, c * 128 : c * 128 + 128])
        if i == 7:
            traffic.ready(1)


def second_grads(
    traffic, ids, sent, own, came, keep, send, total,
    turned_o, turned_c, up_o, up_c, small_o, small_c, sems,
):
    copies = fetch_rows(
        ((sent, AT_2, turned_o), (came, AT_2, turned_c), (own, OWN_UP, up_o), (came, AT_UP, up_c),
         (sent, AT_SMALL, small_o), (came, AT_SMALL, small_c)),
        sems,
    )
    put = writer(((keep, send),))
    for copy in copies:
        copy.wait()
    to = 8 * EARLY_PARTS[0]
    for c in range(6):
        lanes = slice(c % 2 * 128, c % 2 * 128 + 128)
        both = None
        for ref in (small_o, small_c):
            at = c // 2 * 16
            value = ref[at : at + 16, lanes].astype(F32) + ref[at + 48 : at + 64, lanes].astype(F32)
            both = value if both is None else both + value
        total[c * 16 : c * 16 + 16, :] = both
        high, rest = split_small(both)
        send[to + c * 16 : to + c * 16 + 16, :] = high
        send[to + 96 + c * 16 : to + 112 + c * 16, :] = rest
    for x in (1, 0):
        for c in range(3):
            at = slice((x * 3 + c) * 256, (x * 3 + c) * 256 + 256)
            made = dot(turned_o[...], up_o[at, :])
            made += dot(turned_c[...], up_c[at, :])
            for i in range(8):
                for half in range(2):
                    rows = made[i * 96 : i * 96 + 96, half * 128 : half * 128 + 128]
                    put(0, x, i, (2 * c + half) * 96, rows)
        if x == 1:
            traffic.ready(1)


def joined_keep(ids, turned, g_joined, came, small, keep_x, send_x, keep_y, send_y, total):
    outs = ((keep_x, send_x), (keep_y, send_y))
    put = keeper(came, joined_place, JOINED_BASE, JOINED_PARTS, outs)
    joined_products(put, 0, ids, turned, g_joined)
    pass_small_of(rows_of_small(small[...]), came, 16 * sum(JOINED_PARTS), total, send_x, 8 * JOINED_PARTS[0])


def pass_small(small, came, from_row, total, send, to_row):
    pass_small_of(small[...], came, from_row, total, send, to_row)


def pass_small_of(small, came, from_row, total, send, to_row):
    count = small.shape[0]
    both = both_small(small, came[from_row : from_row + 2 * count, :])
    total[...] = both
    if send is not None:
        high, rest = split_small(both)
        send[to_row : to_row + count, :] = high
        send[to_row + count : to_row + 2 * count, :] = rest


def joined_half(keep, came, at, count):
    rows = slice(at, at + count)
    return keep[rows, :] + came[rows, :]


def added(keep, came, at, count):
    rows = slice(at, at + count)
    return keep[rows, :].astype(F32) + came[rows, :].astype(F32)


def step_parts(traffic, ids, *refs):
    keeps, cames, small = refs[0:3], refs[3:6], refs[6]
    outs, sends, total = refs[7:10], refs[10:13], refs[13]
    for k, (keep, came, out, send) in enumerate(zip(keeps, cames, outs, sends)):
        half = keep.shape[0] // 2
        traffic.need(k, 3 + k)
        send[0:half, :] = joined_half(keep, came, half, half)
        if k == 0:
            traffic.need(6)
            pass_small(small, came, 2 * half, total, send, half)
        traffic.ready(3 + k)
        out[...] = joined_half(keep, came, 0, half)
        traffic.ready(k)


def step_parts_last(ids, *refs):
    keeps, cames, small = refs[0:3], refs[3:6], refs[6]
    outs, sends, total = refs[7:10], refs[10:12], refs[12]
    for k, to, at in ((0, 0, 0), (1, 1, 0), (2, 0, EARLY_PARTS[0])):
        half = keeps[k].shape[0] // 2
        outs[k][...] = joined_half(keeps[k], cames[k], 0, half)
        sends[to][at : at + half, :] = joined_half(keeps[k], cames[k], half, half)
    pass_small(small, cames[0], keeps[0].shape[0], total, sends[0], EARLY_PARTS[0] + EARLY_PARTS[2])


def step_apart(ids, keep_x, came_x, keep_y, came_y, small, out_x, send_x, out_y, send_y, total):
    for keep, came, out, send in ((keep_x, came_x, out_x, send_x), (keep_y, came_y, out_y, send_y)):
        half = keep.shape[0] // 2
        out[...] = joined_half(keep, came, 0, half)
        send[0:half, :] = joined_half(keep, came, half, half)
    pass_small(small, came_x, keep_x.shape[0], total, send_x, keep_x.shape[0] // 2)


def step_meet(ids, keep_x, came_x, keep_y, came_y, small, out, send, total):
    at = 0
    for keep, came in ((keep_x, came_x), (keep_y, came_y)):
        half = keep.shape[0] // 2
        out[at : at + half, :] = joined_half(keep, came, 0, half)
        send[at : at + half, :] = joined_half(keep, came, half, half)
        at += half
    pass_small(small, came_x, keep_x.shape[0], total, send, at)


def step_joint(ids, keep, came, small, out, send, total):
    at = 0
    for half in JOINED_PARTS:
        out[at : at + half, :] = joined_half(keep, came, 2 * at, half)
        send[at : at + half, :] = joined_half(keep, came, 2 * at + half, half)
        at += half
    pass_small(small, came, 2 * at, total, send, at)


def small_columns(small, out):
    count = out.shape[0]
    for c in range(6):
        out[:, c * 128 : (c + 1) * 128] = small[c * count : (c + 1) * count]


def early_end(ids, keep_0, keep_1, keep_2, came, came_1, small, down, align, up, out, total):
    def block(at, count):
        return keep_2[at : at + count, :].astype(F32) + came[576 + at : 576 + at + count, :].astype(F32)

    for c in range(3):
        down[c * 128 : (c + 1) * 128, :] = jnp.transpose(added(keep_1, came_1, c * 192, 192))
    for c in range(6):
        up[:, c * 128 : (c + 1) * 128] = added(keep_0, came, c * 96, 96)
    for c in range(2):
        align[:, c * 128 : (c + 1) * 128] = block(c * 96, 96)
    out[:, 0:128] = block(192, 96)
    out[:, 128:192] = block(288, 96)[:, 0:64]
    count = small.shape[0]
    both = both_small(small[...], came[960 : 960 + 2 * count, :])
    small_columns(both, total)


def joined_end(ids, keep, came, small, out, total):
    start, at = 0, 0
    for part, size in enumerate(JOINED_SPLIT):
        rows = slice(start, start + size)
        for c in range(4):
            out[rows, c * 128 : (c + 1) * 128] = added(keep, came, at + c * size, size)
        out[rows, 512:576] = added(keep, came, at + 4 * size, size)[:, 0:64]
        start, at = start + size, at + 5 * size
    count = small.shape[0]
    both = both_small(small[...], came[at : at + 2 * count, :])
    small_columns(both, total)


def flip(value, axis, bit, peers, groups):
    pairs = []
    for b in range(peers):
        for g in range(groups):
            other = (b ^ bit, g) if axis == "batch" else (b, g ^ bit)
            pairs.append((b * groups + g, other[0] * groups + other[1]))
    return lax.ppermute(value, AXES, pairs)


def tie(value, *others):
    return lax.optimization_barrier((value,) + others)[0]


def tiled_blocks(matrix, row_parts, column_parts):
    r, c = matrix.shape
    shaped = matrix.reshape(row_parts, r // row_parts, column_parts, c // column_parts)
    return jnp.transpose(shaped, (0, 2, 1, 3)).reshape(
        row_parts * column_parts, r // row_parts, c // column_parts
    )


def scattered(left, right, peers, groups):
    matrix = lax.dot_general(left, right, (((0,), (0,)), ((), ())), preferred_element_type=F32)
    return lax.psum_scatter(
        tiled_blocks(matrix, peers, groups), AXES, scatter_dimension=0, tiled=True
    )[0]


class Traffic:
    def __init__(self, loads, flushes):
        self.loads, self.flushes, self.left = loads, flushes, {}

    def need(self, *which):
        for k in which:
            copy = self.loads.pop(k, None)
            if copy is not None:
                copy.wait()

    def ready(self, *which):
        for k in which:
            if k in self.flushes:
                self.left[k] = self.flushes.pop(k)
                self.left[k].start()

    def finish(self):
        self.need(*list(self.loads))
        self.ready(*list(self.flushes))
        for copy in self.left.values():
            copy.wait()


def call(kernel, name, grant, out_shape, scratch, ids, *args, far=(), kept=(), load=(), flush=(), lazy=False, cost=0.001):
    n_in, n_out, n_scratch = len(args), len(out_shape), len(scratch)
    in_hbm, out_hbm = set(far) | set(load), {-1 - k for k in far} | set(flush)
    outs = [pltpu.HBM(o.shape, o.dtype) if k in kept or k in out_hbm else o for k, o in enumerate(out_shape)]
    own = [pltpu.VMEM(args[k].shape, args[k].dtype) for k in load] + [pltpu.VMEM(out_shape[k].shape, out_shape[k].dtype) for k in flush]
    if own:
        own.append(pltpu.SemaphoreType.DMA((len(own),)))

    def body(ids, *refs):
        ins, made, rest = list(refs[:n_in]), list(refs[n_in : n_in + n_out]), refs[n_in + n_out :]
        buffers = rest[n_scratch:]
        loads, flushes = {}, {}
        for i, k in enumerate(load):
            loads[k] = pltpu.make_async_copy(ins[k], buffers[i], buffers[-1].at[i])
            loads[k].start()
            ins[k] = buffers[i]
        for i, k in enumerate(flush, len(load)):
            flushes[k] = pltpu.make_async_copy(buffers[i], made[k], buffers[-1].at[i])
            made[k] = buffers[i]
        traffic = Traffic(loads, flushes)
        if lazy:
            kernel(traffic, ids, *ins, *made, *rest[:n_scratch])
        else:
            traffic.need(*load)
            kernel(ids, *ins, *made, *rest[:n_scratch])
        traffic.finish()

    return pl.pallas_call(
        body,
        name=name,
        out_shape=outs,
        in_specs=[SMEM] + [HBM if k in in_hbm else VMEM for k in range(n_in)],
        out_specs=[HBM if k in out_hbm else VMEM for k in range(n_out)],
        scratch_shapes=list(scratch) + own,
        compiler_params=pltpu.CompilerParams(vmem_limit_bytes=grant * 1_000_000),
        cost_estimate=pl.CostEstimate(flops=int(cost * 10**9), bytes_accessed=1, transcendentals=0),
    )(ids, *(pltpu.with_memory_space_constraint(a, pltpu.HBM) if k in in_hbm else a for k, a in enumerate(args)))


def exchange(blocks, peers, groups):
    if len(blocks) == 1:
        shaped = blocks[0].reshape(peers, blocks[0].shape[0] // peers, blocks[0].shape[1])
        moved = lax.all_to_all(shaped, "batch", split_axis=0, concat_axis=0, tiled=True)
        return [moved.reshape(blocks[0].shape)]
    return [blocks[0]] + [flip(block, "batch", k, peers, groups) for k, block in zip(ORDER[1:], blocks[1:])]


def per_device(
    tokens, dest, seg_ids, cot_out, cot_align,
    ln1_gain, ln1_bias, w_qkv, q_bias, v_bias, w_out, out_bias,
    ln2_gain, ln2_bias, w_up, up_bias, w_down, down_bias,
    ln3_gain, ln3_bias, w_align, align_bias,
):
    rows, width = tokens.shape
    align = cot_align.shape[1]
    wide = w_up.shape[1]
    slots = seg_ids.shape[1]
    peers, groups = lax.axis_size("batch"), lax.axis_size("grp")
    capacity = slots // peers
    fast = peers == 8 and groups == 4 and (width, wide, align) == (768, 3072, 1024)
    blocks = 8 if fast else 1
    dest_row = dest.reshape(1, rows)
    seg_col = seg_ids.reshape(slots, 1)
    line = lambda v: v.reshape(1, v.shape[0])
    shape = jax.ShapeDtypeStruct
    vmem = pltpu.VMEM
    dma = pltpu.SemaphoreType.DMA
    count = slots // CLIPMAX
    low = lambda c: shape((rows, c), BF16)
    flat = lambda n: shape((n, 128), BF16)
    move = lambda value, axis, bit: flip(value, axis, bit, peers, groups)
    b, g = lax.axis_index("batch"), lax.axis_index("grp")
    place_b = b ^ jnp.arange(8)
    place_b = (place_b >> 2) + (((place_b >> 1) & 1) << 1) + ((place_b & 1) << 2)
    place_g = g ^ jnp.arange(4)
    place_g = (place_g >> 1) + ((place_g & 1) << 1)
    ids = jnp.concatenate([jnp.stack([b, g]), place_b, place_g]).astype(jnp.int32)

    packed = call(
        functools.partial(pack_kernel, peers, capacity), "pack_tokens", 56,
        [shape((slots // blocks, width), BF16)] * blocks, [],
        ids, dest_row, tokens,
    )
    packed = exchange(packed, peers, groups)

    in_slots = shape((slots, width), BF16)
    ctx, qkv, natural, a1, lse = call(
        functools.partial(attention_kernel, blocks), "attention", 56,
        [in_slots, shape((slots, 3 * width), BF16), in_slots, in_slots, shape((width // 128, count, 2 * CLIPMAX), F32)],
        [vmem((count, 3 * CLIPMAX, 2 * CLIPMAX), F32), vmem((128, slots), BF16), vmem((width, 3 * width), BF16),
         vmem((slots, 3 * width), BF16), vmem((slots, width), BF16), dma((blocks,)), dma, dma((2,))],
        ids, *packed, seg_ids, seg_col, line(ln1_gain), line(ln1_bias), w_qkv, line(q_bias), line(v_bias),
        far=tuple(range(blocks)) + (blocks + 4, -2, -3), kept=(3, 4),
    )
    (ctx,) = exchange([ctx], peers, groups)

    full = shape((rows, width), F32)
    extra = 12 * 16
    parts = lambda n: [flat(n * JOINED_PARTS[0]), flat(n * JOINED_PARTS[0] + more), flat(n * JOINED_PARTS[1]), flat(n * JOINED_PARTS[1])]
    both = sum(JOINED_PARTS)
    more = 12 * 8
    chain = lambda n: [flat(n * EARLY_PARTS[0] + extra)] + [flat(n * r) for r in EARLY_PARTS[1:]]
    held = lambda n: [flat(n * r) for r in EARLY_PARTS]
    small_early = shape((96, 128), F32)
    turned = shape((width, rows), BF16)
    y, al, g_packed, g_mid, hidden, gub, a2, a3, ctx_rows, gyb, gmb, small_0, *sent = call(
        functools.partial(rows_kernel, peers, capacity, fast), "rows", 46,
        [low(width), low(align), in_slots, full, low(wide), low(wide), low(width), low(width), low(width), low(width), low(width),
         shape((16, width), F32)] + ([shape((SENT, 256), BF16), shape((OWN, 256), BF16)] if fast else []),
        [vmem((rows, width), F32), vmem((rows, width), F32), vmem((rows, width), F32), vmem((rows, 128), F32), vmem((rows, wide), F32),
         vmem((rows, 512), F32), vmem((rows, 512), F32), vmem((rows, 512), BF16), vmem((rows, 512), BF16),
         vmem((2, 8, width), F32), vmem(w_out.shape, BF16), vmem(w_up.shape, BF16), vmem(w_down.shape, BF16),
         vmem(w_align.shape, BF16), dma((4,))] + ([vmem((width, rows), BF16)] * 2 if fast else []),
        ids, ctx, tokens, dest, dest_row, cot_out, cot_align,
        w_out, line(out_bias), line(ln2_gain), line(ln2_bias), w_up, line(up_bias), w_down, line(down_bias),
        line(ln3_gain), line(ln3_bias), w_align, line(align_bias),
        far=(6, 10, 12, 16), flush=(0, 1, 2, 3, 4) + ((12, 13) if fast else ()), kept=(5, 6, 7, 8, 9, 10, 11), lazy=True,
    )
    (g_arrived,) = exchange([g_packed], peers, groups)

    if fast:
        sent, own = sent
        came = move(sent, "grp", 1)
        came_hidden = move(hidden, "grp", 1)
        routes = (
            (("grp", 2), ("batch", 2), ("batch", 1)),
            (("batch", 1), ("grp", 2), ("batch", 4)),
            (("batch", 2), ("batch", 1), ("grp", 2)),
        )
        go = lambda sends, k: [move(send, *route[k]) for send, route in zip(sends, routes)]
        square = lambda n: vmem((n, rows), BF16)
        k0, s0, small_e = call(
            second_grads, "second_grads", 16, [held(8)[0], chain(8)[0], small_early],
            [square(768), square(768), square(1536), square(1536), square(96), square(96), dma((6,))],
            ids, sent, own, came,
            far=(0, 1, 2), flush=(0, 1), kept=(2,), lazy=True,
        )
        k1, s1, k2, s2 = call(
            first_grads, "first_grads", 20, [held(8)[1], held(8)[1], held(8)[2], held(8)[2]],
            [square(1536), square(1536), square(1024), square(1024), square(384), square(384),
             vmem((rows, wide), BF16), vmem((rows, wide), BF16), dma((8,))],
            ids, hidden, came_hidden, sent, own, tie(came, s0),
            far=(0, 1, 2, 3, 4), flush=(0, 1, 2, 3), lazy=True,
        )
        keeps, sends = [k0, k1, k2], [s0, s1, s2]
        cames = go(sends, 0)
        g_arrived = tie(g_arrived, s1)

    outs = [in_slots, shape((slots, 3 * width), BF16), shape((8, width), F32)]
    turned = shape((width, slots), BF16)
    made = call(
        functools.partial(attention_back_kernel, fast), "attention_back", 28,
        outs + ([flat(16 * both + more), turned] if fast else []),
        [vmem((count, 3 * CLIPMAX, 2 * CLIPMAX), F32), vmem((128, slots), BF16), vmem((slots, 128), F32), vmem((slots, 128), F32),
         vmem((slots, width), F32), vmem((2, 8, width), F32), vmem((width, 3 * width), BF16), dma]
        + ([vmem((width, slots), BF16)] if fast else []),
        ids, g_arrived, natural, qkv, lse, a1, seg_ids, seg_col, line(ln1_gain), w_qkv,
        far=(8,), load=(1, 6, 2, 3, 4), flush=(0, 1, 4) if fast else (0,), lazy=True,
    )
    g_rows, g_joined, small_2 = made[:3]
    (g_back,) = exchange([g_rows], peers, groups)

    if fast:
        send, turned_c = made[3:]
        came = move(send, "grp", 1)
        small_shape = shape((48, 128), F32)

        def early_step(name, n, keeps, cames, small_e, before, cost, **more_of):
            made = call(
                step_parts, name, 14, held(n) + chain(n) + [small_early], [],
                ids, *keeps, tie(cames[0], before), *cames[1:], small_e, cost=cost, lazy=True, **more_of,
            )
            return made[0:3], made[3:6], made[6]

        keeps, sends, small_e = early_step("early_step_1", 4, keeps, cames, small_e, send, 15, load=(0, 3, 6, 1, 4, 2, 5), flush=(0, 1, 2, 3, 4, 5))
        cames = go(sends, 1)
        kx3, sx3, ky3, sy3, small_j = call(
            joined_keep, "joined_keep", 12, parts(8) + [small_shape], [],
            ids, turned_c, g_joined, tie(came, sends[0]), small_2, load=(0, 1),
        )
        cx3, cy3 = move(sx3, "grp", 2), move(sy3, "batch", 1)
        keeps, sends, small_e = early_step("early_step_2", 2, keeps, cames, small_e, sx3, 3.0, load=(0, 1, 2))
        cames = go(sends, 2)
        kx3, sx3, ky3, sy3, small_j = call(
            step_apart, "joined_apart", 10, parts(4) + [small_shape], [],
            ids, kx3, tie(cx3, sends[0]), ky3, cy3, small_j,
        )
        cx3, cy3 = move(sx3, "batch", 1), move(sy3, "grp", 2)
        *keeps, send, send_1, small_e = call(
            step_parts_last, "early_step_3", 10, held(1) + [flat(960 + extra), held(1)[1], small_early], [],
            ids, *keeps, tie(cames[0], sx3), *cames[1:], small_e, cost=1.0,
        )
        last = move(send, "batch", 4)
        last_1 = move(send_1, "batch", 2)
        g_back = tie(g_back, send)
        k3, s3, small_j = call(
            step_meet, "joined_meet", 10, [flat(2 * both), flat(2 * both + more), small_shape], [],
            ids, kx3, tie(cx3, send), ky3, cy3, small_j,
        )
        c3 = move(s3, "batch", 2)
        k3, s3, small_j = call(
            step_joint, "joined_joint", 10, [flat(both), flat(both + more), small_shape], [],
            ids, k3, c3, small_j,
        )
        c3 = move(s3, "batch", 4)
        sum_down, sum_align, sum_up, sum_out, small_e = call(
            early_end, "early_end", 10,
            [shape((384, 192), F32), shape((96, 256), F32), shape((96, 768), F32), shape((96, 192), F32), shape((16, width), F32)], [],
            ids, *keeps, tie(last, s3), last_1, small_e,
        )
        sum_qkv, small_j = call(
            joined_end, "joined_end", 10, [shape((96, 576), F32), shape((8, width), F32)], [],
            ids, k3, tie(c3, sum_out), small_j,
        )
        small_0, small_2 = small_e, small_j
    else:
        sum_up, sum_align, sum_out, sum_down, sum_qkv = (
            scattered(a2, gub, peers, groups),
            scattered(a3, cot_align, peers, groups),
            scattered(ctx_rows, gmb, peers, groups),
            scattered(hidden, gyb, peers, groups),
            scattered(a1, g_joined, peers, groups),
        )
        small_0, small_2 = lax.psum((small_0, small_2), AXES)

    (grad_tokens,) = call(
        functools.partial(last_kernel, peers, capacity), "grad_tokens", 8, [low(width)], [],
        ids, g_back, dest, g_mid,
    )
    sum_align_bias = small_0[3:5].reshape(2 * width)[:align]
    sum_up_bias = small_0[11:15].reshape(4 * width)[:wide]
    return (
        y, al, grad_tokens,
        small_2[0], small_2[1], sum_qkv, small_2[2], small_2[3],
        sum_out, small_0[10], small_0[8], small_0[9],
        sum_up, sum_up_bias, sum_down, small_0[2],
        small_0[0], small_0[1], sum_align, sum_align_bias,
    )


def solution(mesh):
    row, one = P(AXES, None), P()
    matrix = P("batch", "grp")
    return jax.shard_map(
        per_device,
        mesh=mesh,
        in_specs=(row,) * 5 + (one,) * 17,
        out_specs=(
            row, row, row, one, one, matrix, one, one, matrix, one,
            one, one, matrix, one, matrix, one, one, one, matrix, one,
        ),
        check_vma=False,
    )
```

```python
import functools

import jax
import jax.numpy as jnp
from jax import lax
from jax.experimental import pallas as pl
from jax.experimental.pallas import tpu as pltpu
from jax.sharding import PartitionSpec as P

H = 12
CLIPMAX = 128
EPS = 1e-06
MASKED = -1e30
DEAD = 16.0
AXES = ("batch", "grp")
SMEM = pl.BlockSpec(memory_space=pltpu.SMEM)
VMEM = pl.BlockSpec(memory_space=pltpu.VMEM)
HBM = pl.BlockSpec(memory_space=pltpu.HBM)
F32 = jnp.float32
BF16 = jnp.bfloat16


def dot(a, b):
    return jnp.dot(a, b, preferred_element_type=F32)


def dot_nt(a, b):
    return lax.dot_general(a, b, (((1,), (1,)), ((), ())), preferred_element_type=F32)


def dot_tn(a, b):
    return lax.dot_general(a, b, (((0,), (0,)), ((), ())), preferred_element_type=F32)


def iota(shape, axis):
    return lax.broadcasted_iota(jnp.int32, shape, axis)


def row_loop(total, step, body):
    def one(i, carry):
        body(pl.ds(pl.multiple_of(i * step, step), step))
        return carry

    lax.fori_loop(0, total // step, one, 0)


def norm_parts(v):
    centered = v - jnp.mean(v, axis=-1, keepdims=True)
    rstd = lax.rsqrt(jnp.mean(centered * centered, axis=-1, keepdims=True) + EPS)
    return centered * rstd, rstd


def norm_back(g_out, gain, hat, rstd):
    t = g_out * gain
    return rstd * (
        t - jnp.mean(t, axis=-1, keepdims=True) - hat * jnp.mean(t * hat, axis=-1, keepdims=True)
    )


def slot_column(dest_col, me, peers, capacity):
    rows = dest_col.shape[0]
    onehot = (dest_col == iota((rows, peers), 1)).astype(F32)
    before = (iota((rows, rows), 0) > iota((rows, rows), 1)).astype(BF16)
    earlier = dot(before, onehot.astype(BF16))
    offset = jnp.sum(earlier * onehot, axis=1, keepdims=True).astype(jnp.int32)
    return (dest_col ^ me) * capacity + offset


def placing_row(dest_row, me, peers, capacity):
    rows = dest_row.shape[1]
    onehot = (dest_row == iota((peers, rows), 0)).astype(F32)
    before = (iota((rows, rows), 0) < iota((rows, rows), 1)).astype(BF16)
    earlier = dot(onehot.astype(BF16), before)
    offset = jnp.sum(earlier * onehot, axis=0, keepdims=True).astype(jnp.int32)
    return iota((peers * capacity, rows), 0) == (dest_row ^ me) * capacity + offset


def placing(dest_col, me, peers, capacity):
    rows = dest_col.shape[0]
    slot = slot_column(dest_col, me, peers, capacity).astype(F32)
    slot = jnp.transpose(jnp.broadcast_to(slot, (rows, 128)))[0:1, :].astype(jnp.int32)
    return iota((peers * capacity, rows), 0) == slot


def fetching(dest_col, me, peers, capacity):
    shape = (dest_col.shape[0], peers * capacity)
    return (iota(shape, 1) == slot_column(dest_col, me, peers, capacity)).astype(BF16)


def own_index(ids, blocks):
    return ids[0] if blocks > 1 else 0


ORDER = (0, 1, 2, 3, 4, 5, 6, 7)


def block_rows(ids, k, refs):
    size = refs[0].shape[0]
    if len(refs) == 1:
        return pl.ds(0, size)
    return pl.ds(pl.multiple_of((ids[0] ^ ORDER[k]) * size, size), size)


def pack_kernel(peers, capacity, ids, dest_row, tokens, *outs):
    place = placing_row(dest_row[...], own_index(ids, len(outs)), peers, capacity)
    held = jnp.sum(place.astype(F32), axis=1, keepdims=True)
    rows = jnp.where(held > 0.5, dot(place.astype(BF16), tokens[...]), DEAD).astype(BF16)
    size = outs[0].shape[0]
    for out, k in zip(outs, ORDER):
        out[...] = rows[k * size : (k + 1) * size]


def windows(slots):
    block = CLIPMAX
    return [
        (n * block, max(0, (n - 1) * block), min(slots, (n + 2) * block))
        for n in range(slots // block)
    ]


def write_bias(packed, seg_row, seg_col, bias):
    block = CLIPMAX
    live = packed[:, 0:1].astype(F32) < DEAD * 0.5
    for n, (start, low, high) in enumerate(windows(packed.shape[0])):
        shape, keys = (high - low, block), slice(low, high)
        same = seg_col[keys, :] == seg_row[:, start : start + block]
        own = (low + iota(shape, 0)) == (start + iota(shape, 1))
        made = jnp.where(same & (live[keys, :] | own), 0.0, MASKED)
        bias[n, 0 : high - low, 0:block] = made
        bias[n, 0 : high - low, block:] = made


def stacked(rows):
    first = iota(rows.shape, 1) < 64
    zero = jnp.zeros_like(rows)
    return jnp.concatenate([jnp.where(first, rows, zero), jnp.where(first, zero, rows)], axis=0)


def unstacked(turned):
    half = turned.shape[1] // 2
    upper = iota((128, half), 0) < 64
    return jnp.transpose(jnp.where(upper, turned[:, :half], turned[:, half:]))


def attention_kernel(blocks, traffic, ids, *refs):
    arrived, refs = refs[:blocks], refs[blocks:]
    (seg_row, seg_col, gain, shift, w_hbm, q_bias, v_bias), refs = refs[:7], refs[7:]
    outs, refs = refs[:blocks], refs[blocks:]
    (qkv_out, natural_out, a1, lse,
     bias, turned_v, w_qkv, qkv, packed, ctx, in_sems, w_sem, out_sems) = refs
    slots, width = packed.shape
    block = CLIPMAX
    fetches = []
    for k, ref in enumerate(arrived):
        to = packed.at[block_rows(ids, k, arrived), :]
        fetches.append(pltpu.make_async_copy(ref, to, in_sems.at[k]))
        fetches[-1].start()
    weights = pltpu.make_async_copy(w_hbm, w_qkv, w_sem)
    weights.start()
    for fetch in fetches:
        fetch.wait()
    keep = pltpu.make_async_copy(packed, natural_out, out_sems.at[0])
    keep.start()
    traffic.need(blocks, blocks + 1)
    write_bias(packed, seg_row, seg_col, bias)
    gain_f, shift_f = gain[...].astype(F32), shift[...].astype(F32)

    def norm_rows(r):
        x = packed[r, :].astype(F32)
        x = jnp.where(x[:, 0:1] < DEAD * 0.5, x, 0.0)
        hat, _ = norm_parts(x)
        a1[r, :] = (hat * gain_f + shift_f).astype(BF16)

    row_loop(slots, 32, norm_rows)
    traffic.ready(blocks + 2)
    weights.wait()

    piece = 256
    for part, part_bias in ((0, q_bias), (1, None), (2, v_bias)):
        for c in range(width // piece):
            cols = slice(part * width + c * piece, part * width + (c + 1) * piece)
            made = dot(a1[...], w_qkv[:, cols])
            if part_bias is not None:
                made = made + part_bias[:, c * piece : (c + 1) * piece].astype(F32)
            qkv[:, cols] = made.astype(BF16)
    keep_qkv = pltpu.make_async_copy(qkv, qkv_out, out_sems.at[1])
    keep_qkv.start()

    scale = jnp.asarray(64**-0.5, BF16)

    def pair(hp, carry):
        def lanes(part):
            return pl.ds(pl.multiple_of(part * width + hp * 128, 128), 128)

        turned_v[...] = jnp.transpose(qkv[:, lanes(2)].astype(F32)).astype(BF16)
        scores = []
        for n, (start, low, high) in enumerate(windows(slots)):
            q = stacked(qkv[start : start + block, lanes(0)] * scale)
            scores.append(dot_nt(qkv[low:high, lanes(1)], q) + bias[n, 0 : high - low, :])
        for n, (start, low, high) in enumerate(windows(slots)):
            s = scores[n]
            top = jnp.max(s, axis=0, keepdims=True)
            e = jnp.exp(s - top)
            total = jnp.sum(e, axis=0, keepdims=True)
            lse[hp, n : n + 1, :] = top + jnp.log(total)
            found = dot(turned_v[:, low:high], e.astype(BF16)) * (1.0 / total)
            ctx[start : start + block, lanes(0)] = unstacked(found).astype(BF16)
        return carry

    lax.fori_loop(0, width // 128, pair, 0)
    sends = []
    for k, ref in enumerate(outs):
        sends.append(pltpu.make_async_copy(ctx.at[block_rows(ids, k, outs), :], ref, in_sems.at[k]))
        sends[-1].start()
    keep.wait()
    keep_qkv.wait()
    for copy in sends:
        copy.wait()


def attention_back_kernel(shared, traffic, ids, *refs):
    (g_ctx, packed, qkv, lse, a1, seg_row, seg_col, gain, w_hbm), refs = refs[:9], refs[9:]
    (g_rows, g_joined, small), refs = refs[:3], refs[3:]
    if shared:
        (send, turned), refs = refs[:2], refs[2:]
    bias, turned_k, gk, gv, acc, sums, w_qkv, w_sem = refs[:8]
    slots, width = packed.shape
    block = CLIPMAX
    weights = pltpu.make_async_copy(w_hbm, w_qkv, w_sem)
    weights.start()
    traffic.need(1, 6)
    write_bias(packed, seg_row, seg_col, bias)
    traffic.need(2, 3, 4)
    scale = jnp.asarray(64**-0.5, BF16)

    def pair(hp, carry):
        def lanes(part):
            return pl.ds(pl.multiple_of(part * width + hp * 128, 128), 128)

        if shared:
            a1_turned = refs[8]
            a1_turned[lanes(0), :] = jnp.transpose(a1[:, lanes(0)].astype(F32)).astype(BF16)
        turned_k[...] = jnp.transpose(qkv[:, lanes(1)].astype(F32)).astype(BF16)
        gk[...] = jnp.zeros_like(gk)
        gv[...] = jnp.zeros_like(gv)
        first = []
        for n, (start, low, high) in enumerate(windows(slots)):
            here = slice(start, start + block)
            q = stacked(qkv[here, lanes(0)] * scale)
            g = stacked(g_ctx[here, lanes(0)])
            s = dot_nt(qkv[low:high, lanes(1)], q) + bias[n, 0 : high - low, :]
            first.append((q, g, s, dot_nt(qkv[low:high, lanes(2)], g)))
        for n, (start, low, high) in enumerate(windows(slots)):
            here = slice(start, start + block)
            q, g, s, gp = first[n]
            p = jnp.exp(s - lse[hp, n : n + 1, :])
            inner = jnp.sum(gp * p, axis=0, keepdims=True)
            gs = (p * (gp - inner)).astype(BF16)
            gv[low:high, :] += dot(p.astype(BF16), g)
            gk[low:high, :] += dot(gs, q)
            gq = dot(turned_k[:, low:high], gs) * (64**-0.5)
            g_joined[here, lanes(0)] = unstacked(gq).astype(BF16)
        g_joined[:, lanes(1)] = gk[...].astype(BF16)
        g_joined[:, lanes(2)] = gv[...].astype(BF16)
        return carry

    lax.fori_loop(0, width // 128, pair, 0)

    weights.wait()
    acc[...] = dot_nt(g_joined[...], w_qkv[...])
    ones = jnp.ones((8, slots), BF16)
    small[2:3, :] = dot(ones, g_joined[:, 0:width])[0:1]
    small[3:4, :] = dot(ones, g_joined[:, 2 * width :])[0:1]
    small[4:8, :] = jnp.zeros_like(small[4:8, :])
    sums[...] = jnp.zeros_like(sums)
    gain_f = gain[...].astype(F32)

    def back_rows(r):
        x = packed[r, :].astype(F32)
        x = jnp.where(x[:, 0:1] < DEAD * 0.5, x, 0.0)
        hat, rstd = norm_parts(x)
        g_out = acc[r, :]
        sums[0] += folded(g_out * hat)
        sums[1] += folded(g_out)
        g_rows[r, :] = norm_back(g_out, gain_f, hat, rstd).astype(BF16)

    row_loop(slots, 32, back_rows)
    small[0:1, :] = jnp.sum(sums[0], axis=0, keepdims=True)
    small[1:2, :] = jnp.sum(sums[1], axis=0, keepdims=True)
    if shared:
        set_blocks(refs[8], turned, 0, ids, 2, 8, JOINED_SPLIT)
        joined_products(sender(send, joined_place, JOINED_BASE, JOINED_PARTS), 1, ids, turned, g_joined)
        write_small(small, send, 16 * sum(JOINED_PARTS))


def folded(rows):
    total = rows[0:8]
    for i in range(8, rows.shape[0], 8):
        total = total + rows[i : i + 8]
    return total


def gelu_parts(u):
    bell = jnp.exp(-0.5 * u * u)
    t = 1.0 / (1.0 + 0.305 * jnp.abs(u))
    poly = 0.03669796139001846
    for c in (
        -0.15298233926296234, 0.18570539355278015, -0.03796539083123207, 0.12101536989212036,
        0.10342279821634293, 0.12246651202440262, 0.12163975089788437,
    ):
        poly = poly * t + c
    tail = bell * (poly * t)
    below = jnp.where(u < 0.0, tail, 1.0 - tail)
    return below, below + u * (bell * 0.3989422804014327)


def rows_kernel(peers, capacity, blocks, shared, traffic, ids, *refs):
    arrived, refs = refs[:blocks], refs[blocks:]
    (tokens, dest_col, cot_out, cot_align, out_hbm, out_bias, gain2, shift2, up_hbm, up_bias, down_hbm, down_bias,
     gain3, shift3, align_hbm, align_bias), refs = refs[:16], refs[16:]
    (y_out, al_out, g_packed, g_mid, hidden, gub, a2, a3, ctx, gyb, gmb, small), refs = refs[:12], refs[12:]
    if shared:
        (send, own), refs = refs[:2], refs[2:]
    (mid, acc, hat2, rstd2, slope, u_a, u_b, h_a, h_b, sums, w_out, w_up, w_down, w_align, sems, whole, in_sems), refs = refs[:17], refs[17:]
    rows, width = tokens.shape
    wide = hidden.shape[1]
    piece = u_a.shape[1]
    loads = [
        pltpu.make_async_copy(source, to, sems.at[k])
        for k, (source, to) in enumerate(
            ((out_hbm, w_out), (up_hbm, w_up), (down_hbm, w_down), (align_hbm, w_align))
        )
    ]
    size = arrived[0].shape[0]
    copies = []
    for k, ref in enumerate(arrived):
        copies.append(pltpu.make_async_copy(ref, whole.at[pl.ds(ORDER[k] * size, size), :], in_sems.at[k]))
        copies[-1].start()
    loads[0].start()
    traffic.need(blocks + 1)
    fetch = fetching(dest_col[...], own_index(ids, blocks), peers, capacity)
    for copy in copies:
        copy.wait()
    for load in loads[1:]:
        load.start()
    ctx[...] = dot(fetch, whole[...]).astype(BF16)
    traffic.need(blocks)
    loads[0].wait()
    acc[...] = dot(ctx[...], w_out[...])

    def to_mid(r):
        m = tokens[r, :].astype(F32) + acc[r, :] + out_bias[...].astype(F32)
        hat, rstd = norm_parts(m)
        hat2[r, :] = hat
        rstd2[r, :] = jnp.broadcast_to(rstd, (rstd.shape[0], 128))
        a2[r, :] = (hat * gain2[...].astype(F32) + shift2[...].astype(F32)).astype(BF16)
        acc[r, :] = m + down_bias[...].astype(F32)

    row_loop(rows, 32, to_mid)

    def columns(i):
        return pl.ds(pl.multiple_of(i * piece, piece), piece)

    def up(i):
        return dot(a2[...], w_up[:, columns(i)]) + up_bias[:, columns(i)].astype(F32)

    def bend(i, u_ref, h_ref):
        u = u_ref[...]
        below, bent = gelu_parts(u)
        slope[:, columns(i)] = bent
        made = (u * below).astype(BF16)
        hidden[:, columns(i)] = made
        h_ref[...] = made

    last = wide // piece - 1
    h_b[...] = jnp.zeros_like(h_b)
    loads[1].wait()
    u_a[...] = up(0)
    loads[2].wait()

    def two(j, carry):
        u_b[...] = up(2 * j + 1)
        acc[...] += dot(h_b[...], w_down[columns(jnp.maximum(2 * j - 1, 0)), :])
        bend(2 * j, u_a, h_a)
        u_a[...] = up(jnp.minimum(2 * j + 2, last))
        acc[...] += dot(h_a[...], w_down[columns(2 * j), :])
        bend(2 * j + 1, u_b, h_b)
        return carry

    lax.fori_loop(0, (last + 1) // 2, two, 0)
    acc[...] += dot(h_b[...], w_down[columns(last), :])
    traffic.ready(4)

    def to_a3(r):
        y = acc[r, :]
        y_out[r, :] = y.astype(BF16)
        hat, _ = norm_parts(y)
        a3[r, :] = (hat * gain3[...].astype(F32) + shift3[...].astype(F32)).astype(BF16)

    row_loop(rows, 32, to_a3)
    loads[3].wait()
    traffic.need(blocks + 2, blocks + 3)
    al_out[...] = (dot(a3[...], w_align[...]) + align_bias[...].astype(F32)).astype(BF16)
    traffic.ready(0, 1)
    mid[...] = dot_nt(cot_align[...], w_align[...])
    sums[...] = jnp.zeros_like(sums)

    def back3(r):
        hat, rstd = norm_parts(acc[r, :])
        g_out = mid[r, :]
        gy = cot_out[r, :].astype(F32) + norm_back(g_out, gain3[...].astype(F32), hat, rstd)
        g_mid[r, :] = gy
        gyb[r, :] = gy.astype(BF16)
        sums[0] += folded(g_out * hat)
        sums[1] += folded(g_out)

    row_loop(rows, 32, back3)
    small[...] = jnp.zeros_like(small)
    small[0:1, :] = jnp.sum(sums[0], axis=0, keepdims=True)
    small[1:2, :] = jnp.sum(sums[1], axis=0, keepdims=True)
    ones = jnp.ones((8, rows), BF16)
    small[2:3, :] = dot(ones, gyb[...])[0:1]
    align = dot(ones, cot_align[...])[0:1]
    small[3:4, :] = align[:, :width]
    small[4:5, 0 : align.shape[1] - width] = align[:, width:]

    acc[...] = jnp.zeros_like(acc)
    for c in range(wide // 512):
        cols = slice(c * 512, (c + 1) * 512)
        low = (slope[:, cols] * dot_nt(gyb[...], w_down[cols, :])).astype(BF16)
        gub[:, cols] = low
        acc[...] += dot_nt(low, w_up[:, cols])
    traffic.ready(5)
    sums[...] = jnp.zeros_like(sums)

    def back2(r):
        hat, g_out = hat2[r, :], acc[r, :]
        gm = g_mid[r, :] + norm_back(g_out, gain2[...].astype(F32), hat, rstd2[r, 0:1])
        g_mid[r, :] = gm
        gmb[r, :] = gm.astype(BF16)
        sums[0] += folded(g_out * hat)
        sums[1] += folded(g_out)

    row_loop(rows, 32, back2)
    traffic.ready(3, 10)
    g_ctx = dot_nt(gmb[...], w_out[...]).astype(BF16)
    place = placing(dest_col[...], 0, peers, capacity).astype(BF16)
    g_packed[...] = dot(place, g_ctx).astype(BF16)
    traffic.ready(2)
    small[8:9, :] = jnp.sum(sums[0], axis=0, keepdims=True)
    small[9:10, :] = jnp.sum(sums[1], axis=0, keepdims=True)
    small[10:11, :] = dot(ones, gmb[...])[0:1]
    g_up = dot(ones, gub[...])[0:1]
    for c in range(wide // width):
        small[11 + c : 12 + c, :] = g_up[:, c * width : (c + 1) * width]
    if shared:
        natural, turned_d = refs
        turn(gyb, natural, turned_d, 0, ids, 10, 4)
        turn(a3, natural, send, AT_3, ids, 2, 8)
        turn(ctx, natural, send, AT_1, ids, 2, 8)
        turn(a2, natural, send, AT_2, ids, 2, 8)
        own[OWN_D : OWN_D + 384, :] = turned_d[0:384, :]
        send[AT_D : AT_D + 384, :] = turned_d[384:768, :]
        for core, out, align_at, out_at in ((0, own, OWN_ALIGN, OWN_OUT), (1, send, AT_ALIGN, AT_OUT)):
            for x in range(2):
                at = slice(align_at + x * 256, align_at + x * 256 + 256)
                out[at, :] = cot_align[:, own_columns(ids, core, x, 256)]
                at = slice(out_at + x * 256, out_at + x * 256 + 256)
                out[at, :] = spare_columns(gmb, ids[1] ^ (core + 2 * x), 192, 256)
        for core, out, up_at in ((0, own, OWN_UP), (1, send, AT_UP)):
            for x in range(2):
                for c in range(3):
                    at = pl.ds(pl.multiple_of((ids[1] ^ (core + 2 * x)) * 768 + c * 256, 128), 256)
                    to = up_at + (x * 3 + c) * 256
                    out[to : to + 256, :] = gub[:, at]
        for c in range(3):
            high, rest = split_small(small[:, c * 256 : (c + 1) * 256])
            send[AT_SMALL + c * 16 : AT_SMALL + c * 16 + 16, :] = high
            send[AT_SMALL + 48 + c * 16 : AT_SMALL + 64 + c * 16, :] = rest


def last_kernel(peers, capacity, ids, arrived, dest_col, g_mid, out):
    fetch = fetching(dest_col[...], 0, peers, capacity)
    out[...] = (g_mid[...] + dot(fetch, arrived[...])).astype(BF16)


EARLY_PARTS, JOINED_PARTS, JOINED_SPLIT = (576, 480, 480), (240, 240), (48, 48)
JOINED_BASE = (0, 16 * 240)
AT_2, AT_3, AT_1, AT_D, AT_UP, AT_ALIGN, AT_OUT, AT_SMALL, SENT = 0, 768, 1536, 2304, 2688, 4224, 4736, 5248, 5344
OWN_D, OWN_UP, OWN_ALIGN, OWN_OUT, OWN = 0, 384, 1920, 2432, 2944


def set_blocks(natural, out, base, ids, first, count, sizes):
    at = 0
    for j in range(count):
        start = base
        for size in sizes:
            to = start + ids[first + j] * size
            out[pl.ds(pl.multiple_of(to, 16), size), :] = natural[at : at + size, :]
            at, start = at + size, start + count * size


def turn_into(source, natural):
    for c in range(source.shape[1] // 128):
        at = slice(c * 128, (c + 1) * 128)
        natural[at, :] = jnp.transpose(source[:, at].astype(F32)).astype(BF16)


def turn(source, natural, out, base, ids, first, count):
    turn_into(source, natural)
    set_blocks(natural, out, base, ids, first, count, (source.shape[1] // count,))


def spare_columns(ref, index, step, load):
    tile = pl.multiple_of((index * step) // 128 * 128, 128)
    part = ref[:, pl.ds(tile, load)].astype(F32)
    return jnp.where((index * step) % 128 == 64, pltpu.roll(part, load - 64, 1), part).astype(BF16)


def batch_relative(i):
    return (i >> 2) + (((i >> 1) & 1) << 1) + ((i & 1) << 2)


def joined_place(part, x, i):
    return (x * 8 + i) if part == 0 else (i >> 2) * 8 + x * 4 + (i & 3)


def early_place(part, x, i):
    y, low, high = i >> 2, (i >> 1) & 1, i & 1
    return (x * 8 + low * 4 + y * 2 + high, y * 8 + x * 4 + high * 2 + low, low * 8 + y * 4 + x * 2 + high)[part]


def sender(send, place, bases, sizes):
    def put(part, x, i, at, value):
        at = bases[part] + place(part, x, i) * sizes[part] + at
        send[at : at + value.shape[0], :] = value.astype(BF16)

    return put


def keeper(came, place, bases, sizes, outs):
    def put(part, x, i, at, value):
        where, count = place(part, x, i), value.shape[0]
        start = bases[part] + where * sizes[part] + at
        there = came[start : start + count, :].astype(F32)
        start = (where & 7) * sizes[part] + at
        outs[part][where >> 3][start : start + count, :] = (value + there).astype(BF16)

    return put


def split_small(value):
    high = value.astype(BF16)
    return high, (value - high.astype(F32)).astype(BF16)


def write_small(small, out, base):
    count = small.shape[0]
    for c in range(6):
        high, rest = split_small(small[:, c * 128 : (c + 1) * 128])
        out[base + c * count : base + (c + 1) * count, :] = high
        out[base + (6 + c) * count : base + (7 + c) * count, :] = rest


def both_small(small, came):
    high, rest = split_small(small)
    count = small.shape[0]
    there = came[:count].astype(F32) + came[count:].astype(F32)
    return (high.astype(F32) + rest.astype(F32)) + there


def rows_of_small(small):
    return jnp.concatenate([small[:, c * 128 : (c + 1) * 128] for c in range(6)], axis=0)


def own_columns(ids, core, x, step):
    return pl.ds(pl.multiple_of((ids[1] ^ (core + 2 * x)) * step, 128), step)


def joined_products(put, core, ids, turned, g_joined):
    for x in range(2):
        own = spare_columns(g_joined, ids[1] ^ (core + 2 * x), 576, 640)
        for c, slabs in ((0, 2), (2, 2), (4, 1)):
            made = dot(turned[...], own[:, c * 128 : (c + slabs) * 128])
            for part, size in enumerate(JOINED_SPLIT):
                for i in range(8):
                    at = part * 8 * JOINED_SPLIT[0] + i * size
                    for k in range(slabs):
                        put(part, x, i, (c + k) * size, made[at : at + size, k * 128 : k * 128 + 128])


def writer(outs):
    def put(part, x, i, at, value):
        where, count = early_place(part, x, i), value.shape[0]
        start = (where & 7) * EARLY_PARTS[part] + at
        outs[part][where >> 3][start : start + count, :] = value.astype(BF16)

    return put


def fetch_rows(pieces, sems):
    copies = []
    for k, (source, at, buffer) in enumerate(pieces):
        source = source if at is None else source.at[pl.ds(at, buffer.shape[0]), :]
        copies.append(pltpu.make_async_copy(source, buffer, sems.at[k]))
        copies[-1].start()
    return copies


def first_grads(
    traffic, ids, hidden_hbm, came_hidden_hbm, sent, own, came, keep_1, send_1, keep_2, send_2,
    turned_o, turned_c, ends_o, ends_c, down_o, down_c, hidden, came_hidden, sems,
):
    copies = fetch_rows(
        ((sent, AT_3, turned_o), (came, AT_3, turned_c), (own, OWN_ALIGN, ends_o), (came, AT_ALIGN, ends_c),
         (own, OWN_D, down_o), (came, AT_D, down_c), (hidden_hbm, None, hidden), (came_hidden_hbm, None, came_hidden)),
        sems,
    )
    put = writer((None, (keep_1, send_1), (keep_2, send_2)))
    for copy in copies[:4]:
        copy.wait()
    for x in range(2):
        for k in range(2):
            turned = slice(k * 768, k * 768 + 768)
            at = slice(k * 512 + x * 256, k * 512 + x * 256 + 256)
            made = dot(turned_o[turned, :], ends_o[at, :])
            made += dot(turned_c[turned, :], ends_c[at, :])
            for i in range(8):
                for half in range(2):
                    part, at = ((1, 384), (2, 192), (2, 288), (2, 384))[2 * k + half]
                    put(part, x, i, at, made[i * 96 : i * 96 + 96, half * 128 : half * 128 + 128])
    for copy in copies[4:]:
        copy.wait()
    for i in (4, 5, 6, 7, 0, 1, 2, 3):
        at = pl.ds(pl.multiple_of((ids[0] ^ batch_relative(i)) * 384, 128), 384)
        made = dot(down_o[...], hidden[:, at])
        made += dot(down_c[...], came_hidden[:, at])
        for x in range(2):
            for c, (part, to) in enumerate(((1, 0), (1, 192), (2, 0))):
                put(part, x, i, to, made[x * 192 : x * 192 + 192, c * 128 : c * 128 + 128])
        if i == 7:
            traffic.ready(1)


def second_grads(
    traffic, ids, sent, own, came, keep, send, total,
    turned_o, turned_c, up_o, up_c, small_o, small_c, sems,
):
    copies = fetch_rows(
        ((sent, AT_2, turned_o), (came, AT_2, turned_c), (own, OWN_UP, up_o), (came, AT_UP, up_c),
         (sent, AT_SMALL, small_o), (came, AT_SMALL, small_c)),
        sems,
    )
    put = writer(((keep, send),))
    for copy in copies:
        copy.wait()
    to = 8 * EARLY_PARTS[0]
    for c in range(6):
        lanes = slice(c % 2 * 128, c % 2 * 128 + 128)
        both = None
        for ref in (small_o, small_c):
            at = c // 2 * 16
            value = ref[at : at + 16, lanes].astype(F32) + ref[at + 48 : at + 64, lanes].astype(F32)
            both = value if both is None else both + value
        total[c * 16 : c * 16 + 16, :] = both
        high, rest = split_small(both)
        send[to + c * 16 : to + c * 16 + 16, :] = high
        send[to + 96 + c * 16 : to + 112 + c * 16, :] = rest
    for x in (1, 0):
        for c in range(3):
            at = slice((x * 3 + c) * 256, (x * 3 + c) * 256 + 256)
            made = dot(turned_o[...], up_o[at, :])
            made += dot(turned_c[...], up_c[at, :])
            for i in range(8):
                for half in range(2):
                    rows = made[i * 96 : i * 96 + 96, half * 128 : half * 128 + 128]
                    put(0, x, i, (2 * c + half) * 96, rows)
        if x == 1:
            traffic.ready(1)


def joined_keep(ids, turned, g_joined, came, small, keep_x, send_x, keep_y, send_y, total):
    outs = ((keep_x, send_x), (keep_y, send_y))
    put = keeper(came, joined_place, JOINED_BASE, JOINED_PARTS, outs)
    joined_products(put, 0, ids, turned, g_joined)
    pass_small_of(rows_of_small(small[...]), came, 16 * sum(JOINED_PARTS), total, send_x, 8 * JOINED_PARTS[0])


def pass_small(small, came, from_row, total, send, to_row):
    pass_small_of(small[...], came, from_row, total, send, to_row)


def pass_small_of(small, came, from_row, total, send, to_row):
    count = small.shape[0]
    both = both_small(small, came[from_row : from_row + 2 * count, :])
    total[...] = both
    if send is not None:
        high, rest = split_small(both)
        send[to_row : to_row + count, :] = high
        send[to_row + count : to_row + 2 * count, :] = rest


def joined_half(keep, came, at, count):
    rows = slice(at, at + count)
    return keep[rows, :] + came[rows, :]


def added(keep, came, at, count):
    rows = slice(at, at + count)
    return keep[rows, :].astype(F32) + came[rows, :].astype(F32)


def step_parts(count, small_with, traffic, ids, *refs):
    keeps, cames, refs = refs[:count], refs[count : 2 * count], refs[2 * count :]
    if small_with is not None:
        small, total, refs = refs[0], refs[-1], refs[1:-1]
    outs, sends = refs[:count], refs[count:]
    for k in range(count):
        half = keeps[k].shape[0] // 2
        traffic.need(k, count + k)
        sends[k][0:half, :] = joined_half(keeps[k], cames[k], half, half)
        if k == small_with:
            traffic.need(2 * count)
            pass_small(small, cames[k], 2 * half, total, sends[k], half)
        traffic.ready(count + k)
        outs[k][...] = joined_half(keeps[k], cames[k], 0, half)
        traffic.ready(k)


def step_apart(ids, keep_x, came_x, keep_y, came_y, small, out_x, send_x, out_y, send_y, total):
    for keep, came, out, send in ((keep_x, came_x, out_x, send_x), (keep_y, came_y, out_y, send_y)):
        half = keep.shape[0] // 2
        out[...] = joined_half(keep, came, 0, half)
        send[0:half, :] = joined_half(keep, came, half, half)
    pass_small(small, came_x, keep_x.shape[0], total, send_x, keep_x.shape[0] // 2)


def step_meet(ids, keep_x, came_x, keep_y, came_y, small, out, send, total):
    at = 0
    for keep, came in ((keep_x, came_x), (keep_y, came_y)):
        half = keep.shape[0] // 2
        out[at : at + half, :] = joined_half(keep, came, 0, half)
        send[at : at + half, :] = joined_half(keep, came, half, half)
        at += half
    pass_small(small, came_x, keep_x.shape[0], total, send, at)


def step_joint(ids, keep, came, small, out, send, total):
    at = 0
    for half in JOINED_PARTS:
        out[at : at + half, :] = joined_half(keep, came, 2 * at, half)
        send[at : at + half, :] = joined_half(keep, came, 2 * at + half, half)
        at += half
    pass_small(small, came, 2 * at, total, send, at)


def small_columns(small, out):
    count = out.shape[0]
    for c in range(6):
        out[:, c * 128 : (c + 1) * 128] = small[c * count : (c + 1) * count]


def early_end_a(ids, keep_1, keep_2, came_1, came_2, down, align, out):
    down[0:128, :] = jnp.transpose(added(keep_1, came_1, 0, 192))
    down[128:256, :] = jnp.transpose(added(keep_1, came_1, 192, 192))
    down[256:384, :] = jnp.transpose(added(keep_2, came_2, 0, 192))
    align[:, 0:128] = added(keep_1, came_1, 384, 96)
    align[:, 128:256] = added(keep_2, came_2, 192, 96)
    out[:, 0:128] = added(keep_2, came_2, 288, 96)
    out[:, 128:192] = added(keep_2, came_2, 384, 96)[:, 0:64]


def early_end_b(ids, keep, came, small, up, total):
    for c in range(6):
        up[:, c * 128 : (c + 1) * 128] = added(keep, came, c * 96, 96)
    count = small.shape[0]
    both = both_small(small[...], came[576 : 576 + 2 * count, :])
    small_columns(both, total)


def joined_end(ids, keep, came, small, out, total):
    start, at = 0, 0
    for part, size in enumerate(JOINED_SPLIT):
        rows = slice(start, start + size)
        for c in range(4):
            out[rows, c * 128 : (c + 1) * 128] = added(keep, came, at + c * size, size)
        out[rows, 512:576] = added(keep, came, at + 4 * size, size)[:, 0:64]
        start, at = start + size, at + 5 * size
    count = small.shape[0]
    both = both_small(small[...], came[at : at + 2 * count, :])
    small_columns(both, total)


def flip(value, axis, bit, peers, groups):
    pairs = []
    for b in range(peers):
        for g in range(groups):
            other = (b ^ bit, g) if axis == "batch" else (b, g ^ bit)
            pairs.append((b * groups + g, other[0] * groups + other[1]))
    return lax.ppermute(value, AXES, pairs)


def tie(value, *others):
    return lax.optimization_barrier((value,) + others)[0]


def tiled_blocks(matrix, row_parts, column_parts):
    r, c = matrix.shape
    shaped = matrix.reshape(row_parts, r // row_parts, column_parts, c // column_parts)
    return jnp.transpose(shaped, (0, 2, 1, 3)).reshape(
        row_parts * column_parts, r // row_parts, c // column_parts
    )


def scattered(left, right, peers, groups):
    matrix = lax.dot_general(left, right, (((0,), (0,)), ((), ())), preferred_element_type=F32)
    return lax.psum_scatter(
        tiled_blocks(matrix, peers, groups), AXES, scatter_dimension=0, tiled=True
    )[0]


class Traffic:
    def __init__(self, loads, flushes):
        self.loads, self.flushes, self.left = loads, flushes, {}

    def need(self, *which):
        for k in which:
            copy = self.loads.pop(k, None)
            if copy is not None:
                copy.wait()

    def ready(self, *which):
        for k in which:
            if k in self.flushes:
                self.left[k] = self.flushes.pop(k)
                self.left[k].start()

    def finish(self):
        self.need(*list(self.loads))
        self.ready(*list(self.flushes))
        for copy in self.left.values():
            copy.wait()


def call(kernel, name, grant, out_shape, scratch, ids, *args, far=(), kept=(), load=(), flush=(), lazy=False, cost=0.001):
    n_in, n_out, n_scratch = len(args), len(out_shape), len(scratch)
    in_hbm, out_hbm = set(far) | set(load), {-1 - k for k in far} | set(flush)
    outs = [pltpu.HBM(o.shape, o.dtype) if k in kept or k in out_hbm else o for k, o in enumerate(out_shape)]
    own = [pltpu.VMEM(args[k].shape, args[k].dtype) for k in load] + [pltpu.VMEM(out_shape[k].shape, out_shape[k].dtype) for k in flush]
    if own:
        own.append(pltpu.SemaphoreType.DMA((len(own),)))

    def body(ids, *refs):
        ins, made, rest = list(refs[:n_in]), list(refs[n_in : n_in + n_out]), refs[n_in + n_out :]
        buffers = rest[n_scratch:]
        loads, flushes = {}, {}
        for i, k in enumerate(load):
            loads[k] = pltpu.make_async_copy(ins[k], buffers[i], buffers[-1].at[i])
            loads[k].start()
            ins[k] = buffers[i]
        for i, k in enumerate(flush, len(load)):
            flushes[k] = pltpu.make_async_copy(buffers[i], made[k], buffers[-1].at[i])
            made[k] = buffers[i]
        traffic = Traffic(loads, flushes)
        if lazy:
            kernel(traffic, ids, *ins, *made, *rest[:n_scratch])
        else:
            traffic.need(*load)
            kernel(ids, *ins, *made, *rest[:n_scratch])
        traffic.finish()

    return pl.pallas_call(
        body,
        name=name,
        out_shape=outs,
        in_specs=[SMEM] + [HBM if k in in_hbm else VMEM for k in range(n_in)],
        out_specs=[HBM if k in out_hbm else VMEM for k in range(n_out)],
        scratch_shapes=list(scratch) + own,
        compiler_params=pltpu.CompilerParams(vmem_limit_bytes=grant * 1_000_000),
        cost_estimate=pl.CostEstimate(flops=int(cost * 10**9), bytes_accessed=1, transcendentals=0),
    )(ids, *(pltpu.with_memory_space_constraint(a, pltpu.HBM) if k in in_hbm else a for k, a in enumerate(args)))


def exchange(blocks, peers, groups):
    if len(blocks) == 1:
        shaped = blocks[0].reshape(peers, blocks[0].shape[0] // peers, blocks[0].shape[1])
        moved = lax.all_to_all(shaped, "batch", split_axis=0, concat_axis=0, tiled=True)
        return [moved.reshape(blocks[0].shape)]
    return [blocks[0]] + [flip(block, "batch", k, peers, groups) for k, block in zip(ORDER[1:], blocks[1:])]


def per_device(
    tokens, dest, seg_ids, cot_out, cot_align,
    ln1_gain, ln1_bias, w_qkv, q_bias, v_bias, w_out, out_bias,
    ln2_gain, ln2_bias, w_up, up_bias, w_down, down_bias,
    ln3_gain, ln3_bias, w_align, align_bias,
):
    rows, width = tokens.shape
    align = cot_align.shape[1]
    wide = w_up.shape[1]
    slots = seg_ids.shape[1]
    peers, groups = lax.axis_size("batch"), lax.axis_size("grp")
    capacity = slots // peers
    fast = peers == 8 and groups == 4 and (width, wide, align) == (768, 3072, 1024)
    blocks = 8 if fast else 1
    seg_col = seg_ids.reshape(slots, 1)
    line = lambda v: v.reshape(1, v.shape[0])
    shape = jax.ShapeDtypeStruct
    vmem = pltpu.VMEM
    dma = pltpu.SemaphoreType.DMA
    count = slots // CLIPMAX
    low = lambda c: shape((rows, c), BF16)
    flat = lambda n: shape((n, 128), BF16)
    move = lambda value, axis, bit: flip(value, axis, bit, peers, groups)
    b, g = lax.axis_index("batch"), lax.axis_index("grp")
    place_b = b ^ jnp.arange(8)
    place_b = (place_b >> 2) + (((place_b >> 1) & 1) << 1) + ((place_b & 1) << 2)
    place_g = g ^ jnp.arange(4)
    place_g = (place_g >> 1) + ((place_g & 1) << 1)
    ids = jnp.concatenate([jnp.stack([b, g]), place_b, place_g]).astype(jnp.int32)

    packed = call(
        functools.partial(pack_kernel, peers, capacity), "pack_tokens", 56,
        [shape((slots // blocks, width), BF16)] * blocks, [],
        ids, dest.reshape(1, rows), tokens, kept=tuple(range(blocks)), load=(1,),
    )
    packed = exchange(packed, peers, groups)

    in_slots = shape((slots, width), BF16)
    apart = [shape((slots // blocks, width), BF16)] * blocks
    made = call(
        functools.partial(attention_kernel, blocks), "attention", 56,
        apart + [shape((slots, 3 * width), BF16), in_slots, in_slots, shape((width // 128, count, 2 * CLIPMAX), F32)],
        [vmem((count, 3 * CLIPMAX, 2 * CLIPMAX), F32), vmem((128, slots), BF16), vmem((width, 3 * width), BF16),
         vmem((slots, 3 * width), BF16), vmem((slots, width), BF16), vmem((slots, width), BF16), dma((blocks,)), dma, dma((2,))],
        ids, *packed, seg_ids, seg_col, line(ln1_gain), line(ln1_bias), w_qkv, line(q_bias), line(v_bias),
        far=tuple(range(blocks)) + (blocks + 4,) + tuple(-1 - k for k in range(blocks + 2)),
        load=(blocks, blocks + 1), flush=(blocks + 2,), kept=(blocks + 3,), lazy=True,
    )
    ctx, (qkv, natural, a1, lse) = exchange(made[:blocks], peers, groups), made[blocks:]

    full = shape((rows, width), F32)
    extra = 12 * 16
    parts = lambda n: [flat(n * JOINED_PARTS[0]), flat(n * JOINED_PARTS[0] + more), flat(n * JOINED_PARTS[1]), flat(n * JOINED_PARTS[1])]
    both = sum(JOINED_PARTS)
    more = 12 * 8
    chain = lambda n: [flat(n * EARLY_PARTS[0] + extra)] + [flat(n * r) for r in EARLY_PARTS[1:]]
    held = lambda n: [flat(n * r) for r in EARLY_PARTS]
    small_early = shape((96, 128), F32)
    turned = shape((width, rows), BF16)
    y, al, g_packed, g_mid, hidden, gub, a2, a3, ctx_rows, gyb, gmb, small_0, *sent = call(
        functools.partial(rows_kernel, peers, capacity, blocks, fast), "rows", 46,
        [low(width), low(align), in_slots, full, low(wide), low(wide), low(width), low(width), low(width), low(width), low(width),
         shape((16, width), F32)] + ([shape((SENT, 256), BF16), shape((OWN, 256), BF16)] if fast else []),
        [vmem((rows, width), F32), vmem((rows, width), F32), vmem((rows, width), F32), vmem((rows, 128), F32), vmem((rows, wide), F32),
         vmem((rows, 512), F32), vmem((rows, 512), F32), vmem((rows, 512), BF16), vmem((rows, 512), BF16),
         vmem((2, 8, width), F32), vmem(w_out.shape, BF16), vmem(w_up.shape, BF16), vmem(w_down.shape, BF16),
         vmem(w_align.shape, BF16), dma((4,)), vmem((slots, width), BF16), dma((blocks,))] + ([vmem((width, rows), BF16)] * 2 if fast else []),
        ids, *ctx, tokens, dest, cot_out, cot_align,
        w_out, line(out_bias), line(ln2_gain), line(ln2_bias), w_up, line(up_bias), w_down, line(down_bias),
        line(ln3_gain), line(ln3_bias), w_align, line(align_bias),
        far=tuple(range(blocks)) + tuple(blocks + k for k in (4, 8, 10, 14)), load=(), flush=(0, 1, 2, 3, 4) + ((12, 13) if fast else ()), kept=(5, 6, 7, 8, 9, 10, 11), lazy=True,
    )
    (g_arrived,) = exchange([g_packed], peers, groups)

    if fast:
        sent, own = sent
        came = move(sent, "grp", 1)
        came_hidden = move(hidden, "grp", 1)
        routes = (
            (("grp", 2), ("batch", 2), ("batch", 1), ("batch", 4)),
            (("batch", 1), ("grp", 2), ("batch", 4), ("batch", 2)),
            (("batch", 2), ("batch", 1), ("grp", 2), ("batch", 4)),
        )
        go = lambda sends, k, which=(0, 1, 2): [move(send, *routes[p][k]) for send, p in zip(sends, which)]
        square = lambda n: vmem((n, rows), BF16)
        k0, s0, small_e = call(
            second_grads, "second_grads", 16, [held(8)[0], chain(8)[0], small_early],
            [square(768), square(768), square(1536), square(1536), square(96), square(96), dma((6,))],
            ids, sent, own, came,
            far=(0, 1, 2), flush=(0, 1), kept=(2,), lazy=True,
        )
        k1, s1, k2, s2 = call(
            first_grads, "first_grads", 20, [held(8)[1], held(8)[1], held(8)[2], held(8)[2]],
            [square(1536), square(1536), square(1024), square(1024), square(384), square(384),
             vmem((rows, wide), BF16), vmem((rows, wide), BF16), dma((8,))],
            ids, hidden, came_hidden, sent, own, tie(came, s0),
            far=(0, 1, 2, 3, 4), flush=(0, 1, 2, 3), lazy=True,
        )
        keeps, sends = [k0, k1, k2], [s0, s1, s2]
        cames = go(sends, 0)
        g_arrived = tie(g_arrived, s1)

    outs = [in_slots, shape((slots, 3 * width), BF16), shape((8, width), F32)]
    turned = shape((width, slots), BF16)
    made = call(
        functools.partial(attention_back_kernel, fast), "attention_back", 28,
        outs + ([flat(16 * both + more), turned] if fast else []),
        [vmem((count, 3 * CLIPMAX, 2 * CLIPMAX), F32), vmem((128, slots), BF16), vmem((slots, 128), F32), vmem((slots, 128), F32),
         vmem((slots, width), F32), vmem((2, 8, width), F32), vmem((width, 3 * width), BF16), dma]
        + ([vmem((width, slots), BF16)] if fast else []),
        ids, g_arrived, natural, qkv, lse, a1, seg_ids, seg_col, line(ln1_gain), w_qkv,
        far=(8,), load=(1, 6, 2, 3, 4), flush=(0, 1, 4) if fast else (0,), lazy=True,
    )
    g_rows, g_joined, small_2 = made[:3]
    (g_back,) = exchange([g_rows], peers, groups)

    if fast:
        send, turned_c = made[3:]
        came = move(send, "grp", 1)
        small_shape = shape((48, 128), F32)

        def early_step(name, which, n, keeps, cames, small_e, before, cost, **more_of):
            count = len(which)
            first = which[0] == 0
            made = call(
                functools.partial(step_parts, count, 0 if first else None), name, 14,
                [held(n)[p] for p in which] + [chain(n)[p] for p in which] + ([small_early] if first else []), [],
                ids, *keeps, tie(cames[0], before), *cames[1:], *((small_e,) if first else ()), cost=cost, lazy=True, **more_of,
            )
            return list(made[:count]), list(made[count : 2 * count]), (made[-1] if first else small_e)

        both_, one_ = (1, 2), (0,)
        C1, CK, C2A, C2B, CA, C3A, C3B, CEA = 15,.001,3,.001,.001,4,.001,3
        keeps, sends, small_e = early_step("early_step_1", (0, 1, 2), 4, keeps, cames, small_e, send, C1, load=(0, 3, 6, 1, 4, 2, 5), flush=(0, 1, 2, 3, 4, 5))
        cames = go(sends, 1)
        kx3, sx3, ky3, sy3, small_j = call(
            joined_keep, "joined_keep", 12, parts(8) + [small_shape], [],
            ids, turned_c, g_joined, tie(came, sends[0]), small_2, load=(0, 1), cost=CK,
        )
        cx3, cy3 = move(sx3, "grp", 2), move(sy3, "batch", 1)
        keeps_a, sends_a, _ = early_step("early_step_2a", both_, 2, keeps[1:], cames[1:], None, sx3, C2A, load=(0, 1))
        cames_a = go(sends_a, 2, both_)
        keeps_b, sends_b, small_e = early_step("early_step_2b", one_, 2, keeps[:1], cames[:1], small_e, sends_a[0], C2B, load=(0,))
        cames_b = go(sends_b, 2, one_)
        kx3, sx3, ky3, sy3, small_j = call(
            step_apart, "joined_apart", 10, parts(4) + [small_shape], [],
            ids, kx3, tie(cx3, sends_b[0]), ky3, cy3, small_j, cost=CA,
        )
        cx3, cy3 = move(sx3, "batch", 1), move(sy3, "grp", 2)
        keeps_a, sends_a, _ = early_step("early_step_3a", both_, 1, keeps_a, cames_a, None, sx3, C3A)
        cames_a = go(sends_a, 3, both_)
        keeps_b, sends_b, small_e = early_step("early_step_3b", one_, 1, keeps_b, cames_b, small_e, sends_a[0], C3B)
        cames_b = go(sends_b, 3, one_)
        g_back = tie(g_back, sends_b[0])
        k3, s3, small_j = call(
            step_meet, "joined_meet", 10, [flat(2 * both), flat(2 * both + more), small_shape], [],
            ids, kx3, tie(cx3, sends_b[0]), ky3, cy3, small_j,
        )
        c3 = move(s3, "batch", 2)
        sum_down, sum_align, sum_out = call(
            early_end_a, "early_end_a", 10, [shape((384, 192), F32), shape((96, 256), F32), shape((96, 192), F32)], [],
            ids, *keeps_a, tie(cames_a[0], s3), cames_a[1], cost=CEA,
        )
        sum_up, small_e = call(
            early_end_b, "early_end_b", 10, [shape((96, 768), F32), shape((16, width), F32)], [],
            ids, *keeps_b, tie(cames_b[0], sum_out), small_e, cost=CEA,
        )
        k3, s3, small_j = call(
            step_joint, "joined_joint", 10, [flat(both), flat(both + more), small_shape], [],
            ids, k3, tie(c3, sum_up), small_j,
        )
        c3 = move(s3, "batch", 4)
        sum_qkv, small_j = call(
            joined_end, "joined_end", 10, [shape((96, 576), F32), shape((8, width), F32)], [],
            ids, k3, c3, small_j,
        )
        small_0, small_2 = small_e, small_j
    else:
        sum_up, sum_align, sum_out, sum_down, sum_qkv = (
            scattered(a2, gub, peers, groups),
            scattered(a3, cot_align, peers, groups),
            scattered(ctx_rows, gmb, peers, groups),
            scattered(hidden, gyb, peers, groups),
            scattered(a1, g_joined, peers, groups),
        )
        small_0, small_2 = lax.psum((small_0, small_2), AXES)

    (grad_tokens,) = call(
        functools.partial(last_kernel, peers, capacity), "grad_tokens", 8, [low(width)], [],
        ids, g_back, dest, g_mid, load=(1, 2),
    )
    sum_align_bias = small_0[3:5].reshape(2 * width)[:align]
    sum_up_bias = small_0[11:15].reshape(4 * width)[:wide]
    return (
        y, al, grad_tokens,
        small_2[0], small_2[1], sum_qkv, small_2[2], small_2[3],
        sum_out, small_0[10], small_0[8], small_0[9],
        sum_up, sum_up_bias, sum_down, small_0[2],
        small_0[0], small_0[1], sum_align, sum_align_bias,
    )


def solution(mesh):
    row, one = P(AXES, None), P()
    matrix = P("batch", "grp")
    return jax.shard_map(
        per_device,
        mesh=mesh,
        in_specs=(row,) * 5 + (one,) * 17,
        out_specs=(
            row, row, row, one, one, matrix, one, one, matrix, one,
            one, one, matrix, one, matrix, one, one, one, matrix, one,
        ),
        check_vma=False,
    )
```

```python
import functools

import jax
import jax.numpy as jnp
from jax import lax
from jax.experimental import pallas as pl
from jax.experimental.pallas import tpu as pltpu
from jax.sharding import PartitionSpec as P

H = 12
CLIPMAX = 128
EPS = 1e-06
MASKED = -1e30
DEAD = 16.0
AXES = ("batch", "grp")
SMEM = pl.BlockSpec(memory_space=pltpu.SMEM)
VMEM = pl.BlockSpec(memory_space=pltpu.VMEM)
HBM = pl.BlockSpec(memory_space=pltpu.HBM)
F32 = jnp.float32
BF16 = jnp.bfloat16


def dot(a, b):
    return jnp.dot(a, b, preferred_element_type=F32)


def dot_nt(a, b):
    return lax.dot_general(a, b, (((1,), (1,)), ((), ())), preferred_element_type=F32)


def dot_tn(a, b):
    return lax.dot_general(a, b, (((0,), (0,)), ((), ())), preferred_element_type=F32)


def iota(shape, axis):
    return lax.broadcasted_iota(jnp.int32, shape, axis)


def row_loop(total, step, body):
    def one(i, carry):
        body(pl.ds(pl.multiple_of(i * step, step), step))
        return carry

    lax.fori_loop(0, total // step, one, 0)


def norm_parts(v):
    centered = v - jnp.mean(v, axis=-1, keepdims=True)
    rstd = lax.rsqrt(jnp.mean(centered * centered, axis=-1, keepdims=True) + EPS)
    return centered * rstd, rstd


def norm_back(g_out, gain, hat, rstd):
    t = g_out * gain
    return rstd * (
        t - jnp.mean(t, axis=-1, keepdims=True) - hat * jnp.mean(t * hat, axis=-1, keepdims=True)
    )


def slot_column(dest_col, me, peers, capacity):
    rows = dest_col.shape[0]
    onehot = (dest_col == iota((rows, peers), 1)).astype(F32)
    before = (iota((rows, rows), 0) > iota((rows, rows), 1)).astype(BF16)
    earlier = dot(before, onehot.astype(BF16))
    offset = jnp.sum(earlier * onehot, axis=1, keepdims=True).astype(jnp.int32)
    return (dest_col ^ me) * capacity + offset


def placing_row(dest_row, me, peers, capacity):
    rows = dest_row.shape[1]
    onehot = (dest_row == iota((peers, rows), 0)).astype(F32)
    before = (iota((rows, rows), 0) < iota((rows, rows), 1)).astype(BF16)
    earlier = dot(onehot.astype(BF16), before)
    offset = jnp.sum(earlier * onehot, axis=0, keepdims=True).astype(jnp.int32)
    return iota((peers * capacity, rows), 0) == (dest_row ^ me) * capacity + offset


def placing(dest_col, me, peers, capacity):
    rows = dest_col.shape[0]
    slot = slot_column(dest_col, me, peers, capacity).astype(F32)
    slot = jnp.transpose(jnp.broadcast_to(slot, (rows, 128)))[0:1, :].astype(jnp.int32)
    return iota((peers * capacity, rows), 0) == slot


def fetching(dest_col, me, peers, capacity):
    shape = (dest_col.shape[0], peers * capacity)
    return (iota(shape, 1) == slot_column(dest_col, me, peers, capacity)).astype(BF16)


def own_index(ids, blocks):
    return ids[0] if blocks > 1 else 0


ORDER = (0, 1, 2, 3, 4, 5, 6, 7)


def block_rows(ids, k, refs):
    size = refs[0].shape[0]
    if len(refs) == 1:
        return pl.ds(0, size)
    return pl.ds(pl.multiple_of((ids[0] ^ ORDER[k]) * size, size), size)


def pack_kernel(peers, capacity, ids, dest_row, tokens, *outs):
    place = placing_row(dest_row[...], own_index(ids, len(outs)), peers, capacity)
    held = jnp.sum(place.astype(F32), axis=1, keepdims=True)
    rows = jnp.where(held > 0.5, dot(place.astype(BF16), tokens[...]), DEAD).astype(BF16)
    size = outs[0].shape[0]
    for out, k in zip(outs, ORDER):
        out[...] = rows[k * size : (k + 1) * size]


def windows(slots):
    block = CLIPMAX
    return [
        (n * block, max(0, (n - 1) * block), min(slots, (n + 2) * block))
        for n in range(slots // block)
    ]


def write_bias(packed, seg_row, seg_col, bias):
    block = CLIPMAX
    live = packed[:, 0:1].astype(F32) < DEAD * 0.5
    for n, (start, low, high) in enumerate(windows(packed.shape[0])):
        shape, keys = (high - low, block), slice(low, high)
        same = seg_col[keys, :] == seg_row[:, start : start + block]
        own = (low + iota(shape, 0)) == (start + iota(shape, 1))
        made = jnp.where(same & (live[keys, :] | own), 0.0, MASKED)
        bias[n, 0 : high - low, 0:block] = made
        bias[n, 0 : high - low, block:] = made


def stacked(rows):
    first = iota(rows.shape, 1) < 64
    zero = jnp.zeros_like(rows)
    return jnp.concatenate([jnp.where(first, rows, zero), jnp.where(first, zero, rows)], axis=0)


def unstacked(turned):
    half = turned.shape[1] // 2
    upper = iota((128, half), 0) < 64
    return jnp.transpose(jnp.where(upper, turned[:, :half], turned[:, half:]))


def attention_kernel(blocks, traffic, ids, *refs):
    arrived, refs = refs[:blocks], refs[blocks:]
    (seg_row, seg_col, gain, shift, w_hbm, q_bias, v_bias), refs = refs[:7], refs[7:]
    outs, refs = refs[:blocks], refs[blocks:]
    (qkv_out, natural_out, a1, lse,
     bias, turned_v, w_qkv, qkv, packed, ctx, in_sems, w_sem, out_sems) = refs
    slots, width = packed.shape
    block = CLIPMAX
    fetches = []
    for k, ref in enumerate(arrived):
        to = packed.at[block_rows(ids, k, arrived), :]
        fetches.append(pltpu.make_async_copy(ref, to, in_sems.at[k]))
        fetches[-1].start()
    weights = pltpu.make_async_copy(w_hbm, w_qkv, w_sem)
    weights.start()
    for fetch in fetches:
        fetch.wait()
    keep = pltpu.make_async_copy(packed, natural_out, out_sems.at[0])
    keep.start()
    traffic.need(blocks, blocks + 1)
    write_bias(packed, seg_row, seg_col, bias)
    gain_f, shift_f = gain[...].astype(F32), shift[...].astype(F32)

    def norm_rows(r):
        x = packed[r, :].astype(F32)
        x = jnp.where(x[:, 0:1] < DEAD * 0.5, x, 0.0)
        hat, _ = norm_parts(x)
        a1[r, :] = (hat * gain_f + shift_f).astype(BF16)

    row_loop(slots, 32, norm_rows)
    traffic.ready(blocks + 2)
    weights.wait()

    piece = 256
    for part, part_bias in ((0, q_bias), (1, None), (2, v_bias)):
        for c in range(width // piece):
            cols = slice(part * width + c * piece, part * width + (c + 1) * piece)
            made = dot(a1[...], w_qkv[:, cols])
            if part_bias is not None:
                made = made + part_bias[:, c * piece : (c + 1) * piece].astype(F32)
            qkv[:, cols] = made.astype(BF16)
    keep_qkv = pltpu.make_async_copy(qkv, qkv_out, out_sems.at[1])
    keep_qkv.start()

    scale = jnp.asarray(64**-0.5, BF16)

    def pair(hp, carry):
        def lanes(part):
            return pl.ds(pl.multiple_of(part * width + hp * 128, 128), 128)

        turned_v[...] = jnp.transpose(qkv[:, lanes(2)].astype(F32)).astype(BF16)
        scores = []
        for n, (start, low, high) in enumerate(windows(slots)):
            q = stacked(qkv[start : start + block, lanes(0)] * scale)
            scores.append(dot_nt(qkv[low:high, lanes(1)], q) + bias[n, 0 : high - low, :])
        for n, (start, low, high) in enumerate(windows(slots)):
            s = scores[n]
            top = jnp.max(s, axis=0, keepdims=True)
            e = jnp.exp(s - top)
            total = jnp.sum(e, axis=0, keepdims=True)
            lse[hp, n : n + 1, :] = top + jnp.log(total)
            found = dot(turned_v[:, low:high], e.astype(BF16)) * (1.0 / total)
            ctx[start : start + block, lanes(0)] = unstacked(found).astype(BF16)
        return carry

    lax.fori_loop(0, width // 128, pair, 0)
    sends = []
    for k, ref in enumerate(outs):
        sends.append(pltpu.make_async_copy(ctx.at[block_rows(ids, k, outs), :], ref, in_sems.at[k]))
        sends[-1].start()
    keep.wait()
    keep_qkv.wait()
    for copy in sends:
        copy.wait()


def attention_back_kernel(shared, traffic, ids, *refs):
    (g_ctx, packed, qkv, lse, a1, seg_row, seg_col, gain, w_hbm), refs = refs[:9], refs[9:]
    (g_rows, g_joined, small), refs = refs[:3], refs[3:]
    if shared:
        (send, turned), refs = refs[:2], refs[2:]
    bias, turned_k, gk, gv, acc, sums, w_qkv, w_sem = refs[:8]
    slots, width = packed.shape
    block = CLIPMAX
    weights = pltpu.make_async_copy(w_hbm, w_qkv, w_sem)
    weights.start()
    traffic.need(1, 6)
    write_bias(packed, seg_row, seg_col, bias)
    traffic.need(2, 3, 4)
    scale = jnp.asarray(64**-0.5, BF16)

    def pair(hp, carry):
        def lanes(part):
            return pl.ds(pl.multiple_of(part * width + hp * 128, 128), 128)

        if shared:
            a1_turned = refs[8]
            a1_turned[lanes(0), :] = jnp.transpose(a1[:, lanes(0)].astype(F32)).astype(BF16)
        turned_k[...] = jnp.transpose(qkv[:, lanes(1)].astype(F32)).astype(BF16)
        gk[...] = jnp.zeros_like(gk)
        gv[...] = jnp.zeros_like(gv)
        first = []
        for n, (start, low, high) in enumerate(windows(slots)):
            here = slice(start, start + block)
            q = stacked(qkv[here, lanes(0)] * scale)
            g = stacked(g_ctx[here, lanes(0)])
            s = dot_nt(qkv[low:high, lanes(1)], q) + bias[n, 0 : high - low, :]
            first.append((q, g, s, dot_nt(qkv[low:high, lanes(2)], g)))
        for n, (start, low, high) in enumerate(windows(slots)):
            here = slice(start, start + block)
            q, g, s, gp = first[n]
            p = jnp.exp(s - lse[hp, n : n + 1, :])
            inner = jnp.sum(gp * p, axis=0, keepdims=True)
            gs = (p * (gp - inner)).astype(BF16)
            gv[low:high, :] += dot(p.astype(BF16), g)
            gk[low:high, :] += dot(gs, q)
            gq = dot(turned_k[:, low:high], gs) * (64**-0.5)
            g_joined[here, lanes(0)] = unstacked(gq).astype(BF16)
        g_joined[:, lanes(1)] = gk[...].astype(BF16)
        g_joined[:, lanes(2)] = gv[...].astype(BF16)
        return carry

    lax.fori_loop(0, width // 128, pair, 0)

    weights.wait()
    acc[...] = dot_nt(g_joined[...], w_qkv[...])
    ones = jnp.ones((8, slots), BF16)
    half = width // 2
    for k, part in ((2, 0), (3, 2)):
        made = dot(ones, g_joined[:, part * width : (part + 1) * width])[0:1]
        small[k : k + 1, :] = made[:, :half]
        small[4 + k : 5 + k, :] = made[:, half:]
    sums[...] = jnp.zeros_like(sums)
    gain_f = gain[...].astype(F32)

    def back_rows(r):
        x = packed[r, :].astype(F32)
        x = jnp.where(x[:, 0:1] < DEAD * 0.5, x, 0.0)
        hat, rstd = norm_parts(x)
        g_out = acc[r, :]
        sums[0] += folded(g_out * hat)
        sums[1] += folded(g_out)
        g_rows[r, :] = norm_back(g_out, gain_f, hat, rstd).astype(BF16)

    row_loop(slots, 32, back_rows)
    for k in range(2):
        made = jnp.sum(sums[k], axis=0, keepdims=True)
        small[k : k + 1, :] = made[:, :half]
        small[4 + k : 5 + k, :] = made[:, half:]
    if shared:
        set_blocks(refs[8], turned, 0, ids, 2, 8, JOINED_SPLIT)
        joined_products(sender(send, joined_place, JOINED_BASE, JOINED_PARTS), 1, ids, turned, g_joined)
        write_small(small, send, 16 * sum(JOINED_PARTS))


def folded(rows):
    total = rows[0:8]
    for i in range(8, rows.shape[0], 8):
        total = total + rows[i : i + 8]
    return total


def gelu_parts(u):
    bell = jnp.exp(-0.5 * u * u)
    t = 1.0 / (1.0 + 0.305 * jnp.abs(u))
    poly = 0.03669796139001846
    for c in (
        -0.15298233926296234, 0.18570539355278015, -0.03796539083123207, 0.12101536989212036,
        0.10342279821634293, 0.12246651202440262, 0.12163975089788437,
    ):
        poly = poly * t + c
    tail = bell * (poly * t)
    below = jnp.where(u < 0.0, tail, 1.0 - tail)
    return below, below + u * (bell * 0.3989422804014327)


def rows_kernel(peers, capacity, blocks, shared, traffic, ids, *refs):
    arrived, refs = refs[:blocks], refs[blocks:]
    (tokens, dest_col, cot_out, cot_align, out_hbm, out_bias, gain2, shift2, up_hbm, up_bias, down_hbm, down_bias,
     gain3, shift3, align_hbm, align_bias), refs = refs[:16], refs[16:]
    (y_out, al_out, g_packed, g_mid, hidden, gub, a2, a3, ctx, gyb, gmb, small), refs = refs[:12], refs[12:]
    if shared:
        (send, own), refs = refs[:2], refs[2:]
    (mid, acc, hat2, rstd2, slope, u_a, u_b, h_a, h_b, sums, w_out, w_up, w_down, w_align, sems, whole, in_sems), refs = refs[:17], refs[17:]
    rows, width = tokens.shape
    wide = hidden.shape[1]
    piece = u_a.shape[1]
    loads = [
        pltpu.make_async_copy(source, to, sems.at[k])
        for k, (source, to) in enumerate(
            ((out_hbm, w_out), (up_hbm, w_up), (down_hbm, w_down), (align_hbm, w_align))
        )
    ]
    size = arrived[0].shape[0]
    copies = []
    for k, ref in enumerate(arrived):
        copies.append(pltpu.make_async_copy(ref, whole.at[pl.ds(ORDER[k] * size, size), :], in_sems.at[k]))
        copies[-1].start()
    loads[0].start()
    traffic.need(blocks + 1)
    fetch = fetching(dest_col[...], own_index(ids, blocks), peers, capacity)
    for copy in copies:
        copy.wait()
    for load in loads[1:]:
        load.start()
    ctx[...] = dot(fetch, whole[...]).astype(BF16)
    traffic.need(blocks)
    loads[0].wait()
    acc[...] = dot(ctx[...], w_out[...])

    def to_mid(r):
        m = tokens[r, :].astype(F32) + acc[r, :] + out_bias[...].astype(F32)
        hat, rstd = norm_parts(m)
        hat2[r, :] = hat
        rstd2[r, :] = jnp.broadcast_to(rstd, (rstd.shape[0], 128))
        a2[r, :] = (hat * gain2[...].astype(F32) + shift2[...].astype(F32)).astype(BF16)
        acc[r, :] = m + down_bias[...].astype(F32)

    row_loop(rows, 32, to_mid)

    def columns(i):
        return pl.ds(pl.multiple_of(i * piece, piece), piece)

    def up(i):
        return dot(a2[...], w_up[:, columns(i)]) + up_bias[:, columns(i)].astype(F32)

    def bend(i, u_ref, h_ref):
        u = u_ref[...]
        below, bent = gelu_parts(u)
        slope[:, columns(i)] = bent
        made = (u * below).astype(BF16)
        hidden[:, columns(i)] = made
        h_ref[...] = made

    last = wide // piece - 1
    h_b[...] = jnp.zeros_like(h_b)
    loads[1].wait()
    u_a[...] = up(0)
    loads[2].wait()

    def two(j, carry):
        u_b[...] = up(2 * j + 1)
        acc[...] += dot(h_b[...], w_down[columns(jnp.maximum(2 * j - 1, 0)), :])
        bend(2 * j, u_a, h_a)
        u_a[...] = up(jnp.minimum(2 * j + 2, last))
        acc[...] += dot(h_a[...], w_down[columns(2 * j), :])
        bend(2 * j + 1, u_b, h_b)
        return carry

    lax.fori_loop(0, (last + 1) // 2, two, 0)
    acc[...] += dot(h_b[...], w_down[columns(last), :])
    traffic.ready(4)

    def to_a3(r):
        y = acc[r, :]
        y_out[r, :] = y.astype(BF16)
        hat, _ = norm_parts(y)
        a3[r, :] = (hat * gain3[...].astype(F32) + shift3[...].astype(F32)).astype(BF16)

    row_loop(rows, 32, to_a3)
    loads[3].wait()
    traffic.need(blocks + 2, blocks + 3)
    al_out[...] = (dot(a3[...], w_align[...]) + align_bias[...].astype(F32)).astype(BF16)
    traffic.ready(0, 1)
    mid[...] = dot_nt(cot_align[...], w_align[...])
    sums[...] = jnp.zeros_like(sums)

    def back3(r):
        hat, rstd = norm_parts(acc[r, :])
        g_out = mid[r, :]
        gy = cot_out[r, :].astype(F32) + norm_back(g_out, gain3[...].astype(F32), hat, rstd)
        g_mid[r, :] = gy
        gyb[r, :] = gy.astype(BF16)
        sums[0] += folded(g_out * hat)
        sums[1] += folded(g_out)

    row_loop(rows, 32, back3)
    small[...] = jnp.zeros_like(small)
    small[0:1, :] = jnp.sum(sums[0], axis=0, keepdims=True)
    small[1:2, :] = jnp.sum(sums[1], axis=0, keepdims=True)
    ones = jnp.ones((8, rows), BF16)
    small[2:3, :] = dot(ones, gyb[...])[0:1]
    align = dot(ones, cot_align[...])[0:1]
    small[3:4, :] = align[:, :width]
    small[4:5, 0 : align.shape[1] - width] = align[:, width:]

    acc[...] = jnp.zeros_like(acc)
    for c in range(wide // 512):
        cols = slice(c * 512, (c + 1) * 512)
        low = (slope[:, cols] * dot_nt(gyb[...], w_down[cols, :])).astype(BF16)
        gub[:, cols] = low
        acc[...] += dot_nt(low, w_up[:, cols])
    traffic.ready(5)
    sums[...] = jnp.zeros_like(sums)

    def back2(r):
        hat, g_out = hat2[r, :], acc[r, :]
        gm = g_mid[r, :] + norm_back(g_out, gain2[...].astype(F32), hat, rstd2[r, 0:1])
        g_mid[r, :] = gm
        gmb[r, :] = gm.astype(BF16)
        sums[0] += folded(g_out * hat)
        sums[1] += folded(g_out)

    row_loop(rows, 32, back2)
    traffic.ready(3, 10)
    g_ctx = dot_nt(gmb[...], w_out[...]).astype(BF16)
    place = placing(dest_col[...], 0, peers, capacity).astype(BF16)
    g_packed[...] = dot(place, g_ctx).astype(BF16)
    traffic.ready(2)
    small[8:9, :] = jnp.sum(sums[0], axis=0, keepdims=True)
    small[9:10, :] = jnp.sum(sums[1], axis=0, keepdims=True)
    small[10:11, :] = dot(ones, gmb[...])[0:1]
    g_up = dot(ones, gub[...])[0:1]
    for c in range(wide // width):
        small[11 + c : 12 + c, :] = g_up[:, c * width : (c + 1) * width]
    if shared:
        natural, turned_d = refs
        turn(gyb, natural, turned_d, 0, ids, 10, 4)
        turn(a3, natural, send, AT_3, ids, 2, 8)
        turn(ctx, natural, send, AT_1, ids, 2, 8)
        turn(a2, natural, send, AT_2, ids, 2, 8)
        own[OWN_D : OWN_D + 384, :] = turned_d[0:384, :]
        send[AT_D : AT_D + 384, :] = turned_d[384:768, :]
        for core, out, align_at, out_at in ((0, own, OWN_ALIGN, OWN_OUT), (1, send, AT_ALIGN, AT_OUT)):
            for x in range(2):
                at = slice(align_at + x * 256, align_at + x * 256 + 256)
                out[at, :] = cot_align[:, own_columns(ids, core, x, 256)]
                at = slice(out_at + x * 256, out_at + x * 256 + 256)
                out[at, :] = spare_columns(gmb, ids[1] ^ (core + 2 * x), 192, 256)
        for core, out, up_at in ((0, own, OWN_UP), (1, send, AT_UP)):
            for x in range(2):
                for c in range(3):
                    at = pl.ds(pl.multiple_of((ids[1] ^ (core + 2 * x)) * 768 + c * 256, 128), 256)
                    to = up_at + (x * 3 + c) * 256
                    out[to : to + 256, :] = gub[:, at]
        for c in range(3):
            high, rest = split_small(small[:, c * 256 : (c + 1) * 256])
            send[AT_SMALL + c * 16 : AT_SMALL + c * 16 + 16, :] = high
            send[AT_SMALL + 48 + c * 16 : AT_SMALL + 64 + c * 16, :] = rest


def last_kernel(peers, capacity, ids, arrived, dest_col, g_mid, out):
    fetch = fetching(dest_col[...], 0, peers, capacity)
    out[...] = (g_mid[...] + dot(fetch, arrived[...])).astype(BF16)


EARLY_PARTS, JOINED_PARTS, JOINED_SPLIT = (576, 480, 480), (240, 240), (48, 48)
JOINED_BASE = (0, 16 * 240)
AT_2, AT_3, AT_1, AT_D, AT_UP, AT_ALIGN, AT_OUT, AT_SMALL, SENT = 0, 768, 1536, 2304, 2688, 4224, 4736, 5248, 5344
OWN_D, OWN_UP, OWN_ALIGN, OWN_OUT, OWN = 0, 384, 1920, 2432, 2944


def set_blocks(natural, out, base, ids, first, count, sizes):
    at = 0
    for j in range(count):
        start = base
        for size in sizes:
            to = start + ids[first + j] * size
            out[pl.ds(pl.multiple_of(to, 16), size), :] = natural[at : at + size, :]
            at, start = at + size, start + count * size


def turn_into(source, natural):
    for c in range(source.shape[1] // 128):
        at = slice(c * 128, (c + 1) * 128)
        natural[at, :] = jnp.transpose(source[:, at].astype(F32)).astype(BF16)


def turn(source, natural, out, base, ids, first, count):
    turn_into(source, natural)
    set_blocks(natural, out, base, ids, first, count, (source.shape[1] // count,))


def spare_columns(ref, index, step, load):
    tile = pl.multiple_of((index * step) // 128 * 128, 128)
    part = ref[:, pl.ds(tile, load)].astype(F32)
    return jnp.where((index * step) % 128 == 64, pltpu.roll(part, load - 64, 1), part).astype(BF16)


def batch_relative(i):
    return (i >> 2) + (((i >> 1) & 1) << 1) + ((i & 1) << 2)


def joined_place(part, x, i):
    return (x * 8 + i) if part == 0 else (i >> 2) * 8 + x * 4 + (i & 3)


def early_place(part, x, i):
    y, low, high = i >> 2, (i >> 1) & 1, i & 1
    return (x * 8 + low * 4 + y * 2 + high, y * 8 + x * 4 + high * 2 + low, low * 8 + y * 4 + x * 2 + high)[part]


def sender(send, place, bases, sizes):
    def put(part, x, i, at, value):
        at = bases[part] + place(part, x, i) * sizes[part] + at
        send[at : at + value.shape[0], :] = value.astype(BF16)

    return put


def keeper(came, place, bases, sizes, outs):
    def put(part, x, i, at, value):
        where, count = place(part, x, i), value.shape[0]
        start = bases[part] + where * sizes[part] + at
        there = came[start : start + count, :].astype(F32)
        start = (where & 7) * sizes[part] + at
        outs[part][where >> 3][start : start + count, :] = (value + there).astype(BF16)

    return put


def split_small(value):
    high = value.astype(BF16)
    return high, (value - high.astype(F32)).astype(BF16)


def write_small(small, out, base):
    count, slabs = small.shape[0], small.shape[1] // 128
    for c in range(slabs):
        high, rest = split_small(small[:, c * 128 : (c + 1) * 128])
        out[base + c * count : base + (c + 1) * count, :] = high
        out[base + (slabs + c) * count : base + (slabs + 1 + c) * count, :] = rest


def both_small(small, came):
    high, rest = split_small(small)
    count = small.shape[0]
    there = came[:count].astype(F32) + came[count:].astype(F32)
    return (high.astype(F32) + rest.astype(F32)) + there


def rows_of_small(small):
    return jnp.concatenate([small[:, c * 128 : (c + 1) * 128] for c in range(small.shape[1] // 128)], axis=0)


def own_columns(ids, core, x, step):
    return pl.ds(pl.multiple_of((ids[1] ^ (core + 2 * x)) * step, 128), step)


def joined_products(put, core, ids, turned, g_joined):
    for x in range(2):
        own = spare_columns(g_joined, ids[1] ^ (core + 2 * x), 576, 640)
        for c, slabs in ((0, 2), (2, 2), (4, 1)):
            made = dot(turned[...], own[:, c * 128 : (c + slabs) * 128])
            for part, size in enumerate(JOINED_SPLIT):
                for i in range(8):
                    at = part * 8 * JOINED_SPLIT[0] + i * size
                    for k in range(slabs):
                        put(part, x, i, (c + k) * size, made[at : at + size, k * 128 : k * 128 + 128])


def writer(outs):
    def put(part, x, i, at, value):
        where, count = early_place(part, x, i), value.shape[0]
        start = (where & 7) * EARLY_PARTS[part] + at
        outs[part][where >> 3][start : start + count, :] = value.astype(BF16)

    return put


def fetch_rows(pieces, sems):
    copies = []
    for k, (source, at, buffer) in enumerate(pieces):
        source = source if at is None else source.at[pl.ds(at, buffer.shape[0]), :]
        copies.append(pltpu.make_async_copy(source, buffer, sems.at[k]))
        copies[-1].start()
    return copies


def first_grads(
    traffic, ids, hidden_hbm, came_hidden_hbm, sent, own, came, keep_1, send_1, keep_2, send_2,
    turned_o, turned_c, ends_o, ends_c, down_o, down_c, hidden, came_hidden, sems,
):
    copies = fetch_rows(
        ((sent, AT_3, turned_o), (came, AT_3, turned_c), (own, OWN_ALIGN, ends_o), (came, AT_ALIGN, ends_c),
         (own, OWN_D, down_o), (came, AT_D, down_c), (hidden_hbm, None, hidden), (came_hidden_hbm, None, came_hidden)),
        sems,
    )
    put = writer((None, (keep_1, send_1), (keep_2, send_2)))
    for copy in copies[:4]:
        copy.wait()
    for x in range(2):
        for k in range(2):
            turned = slice(k * 768, k * 768 + 768)
            at = slice(k * 512 + x * 256, k * 512 + x * 256 + 256)
            made = dot(turned_o[turned, :], ends_o[at, :])
            made += dot(turned_c[turned, :], ends_c[at, :])
            for i in range(8):
                for half in range(2):
                    part, at = ((1, 384), (2, 192), (2, 288), (2, 384))[2 * k + half]
                    put(part, x, i, at, made[i * 96 : i * 96 + 96, half * 128 : half * 128 + 128])
    for copy in copies[4:]:
        copy.wait()
    for i in (4, 5, 6, 7, 0, 1, 2, 3):
        at = pl.ds(pl.multiple_of((ids[0] ^ batch_relative(i)) * 384, 128), 384)
        made = dot(down_o[...], hidden[:, at])
        made += dot(down_c[...], came_hidden[:, at])
        for x in range(2):
            for c, (part, to) in enumerate(((1, 0), (1, 192), (2, 0))):
                put(part, x, i, to, made[x * 192 : x * 192 + 192, c * 128 : c * 128 + 128])
        if i == 7:
            traffic.ready(1)


def second_grads(
    traffic, ids, sent, own, came, keep, send, total,
    turned_o, turned_c, up_o, up_c, small_o, small_c, sems,
):
    copies = fetch_rows(
        ((sent, AT_2, turned_o), (came, AT_2, turned_c), (own, OWN_UP, up_o), (came, AT_UP, up_c),
         (sent, AT_SMALL, small_o), (came, AT_SMALL, small_c)),
        sems,
    )
    put = writer(((keep, send),))
    for copy in copies:
        copy.wait()
    to = 8 * EARLY_PARTS[0]
    for c in range(6):
        lanes = slice(c % 2 * 128, c % 2 * 128 + 128)
        both = None
        for ref in (small_o, small_c):
            at = c // 2 * 16
            value = ref[at : at + 16, lanes].astype(F32) + ref[at + 48 : at + 64, lanes].astype(F32)
            both = value if both is None else both + value
        total[c * 16 : c * 16 + 16, :] = both
        high, rest = split_small(both)
        send[to + c * 16 : to + c * 16 + 16, :] = high
        send[to + 96 + c * 16 : to + 112 + c * 16, :] = rest
    for x in (1, 0):
        for c in range(3):
            at = slice((x * 3 + c) * 256, (x * 3 + c) * 256 + 256)
            made = dot(turned_o[...], up_o[at, :])
            made += dot(turned_c[...], up_c[at, :])
            for i in range(8):
                for half in range(2):
                    rows = made[i * 96 : i * 96 + 96, half * 128 : half * 128 + 128]
                    put(0, x, i, (2 * c + half) * 96, rows)
        if x == 1:
            traffic.ready(1)


def joined_keep(ids, turned, g_joined, came, small, keep_x, send_x, keep_y, send_y, total):
    outs = ((keep_x, send_x), (keep_y, send_y))
    put = keeper(came, joined_place, JOINED_BASE, JOINED_PARTS, outs)
    joined_products(put, 0, ids, turned, g_joined)
    pass_small_of(rows_of_small(small[...]), came, 16 * sum(JOINED_PARTS), total, send_x, 8 * JOINED_PARTS[0])


def pass_small(small, came, from_row, total, send, to_row):
    pass_small_of(small[...], came, from_row, total, send, to_row)


def pass_small_of(small, came, from_row, total, send, to_row):
    count = small.shape[0]
    both = both_small(small, came[from_row : from_row + 2 * count, :])
    total[...] = both
    if send is not None:
        high, rest = split_small(both)
        send[to_row : to_row + count, :] = high
        send[to_row + count : to_row + 2 * count, :] = rest


def joined_half(keep, came, at, count):
    rows = slice(at, at + count)
    return keep[rows, :] + came[rows, :]


def added(keep, came, at, count):
    rows = slice(at, at + count)
    return keep[rows, :].astype(F32) + came[rows, :].astype(F32)


def step_parts(count, small_with, traffic, ids, *refs):
    keeps, cames, refs = refs[:count], refs[count : 2 * count], refs[2 * count :]
    if small_with is not None:
        small, total, refs = refs[0], refs[-1], refs[1:-1]
    outs, sends = refs[:count], refs[count:]
    for k in range(count):
        half = keeps[k].shape[0] // 2
        traffic.need(k, count + k)
        sends[k][0:half, :] = joined_half(keeps[k], cames[k], half, half)
        if k == small_with:
            traffic.need(2 * count)
            pass_small(small, cames[k], 2 * half, total, sends[k], half)
        traffic.ready(count + k)
        outs[k][...] = joined_half(keeps[k], cames[k], 0, half)
        traffic.ready(k)


def step_apart(ids, keep_x, came_x, keep_y, came_y, small, out_x, send_x, out_y, send_y, total):
    for keep, came, out, send in ((keep_x, came_x, out_x, send_x), (keep_y, came_y, out_y, send_y)):
        half = keep.shape[0] // 2
        out[...] = joined_half(keep, came, 0, half)
        send[0:half, :] = joined_half(keep, came, half, half)
    pass_small(small, came_x, keep_x.shape[0], total, send_x, keep_x.shape[0] // 2)


def step_meet(ids, keep_x, came_x, keep_y, came_y, small, out, send, total):
    at = 0
    for keep, came in ((keep_x, came_x), (keep_y, came_y)):
        half = keep.shape[0] // 2
        out[at : at + half, :] = joined_half(keep, came, 0, half)
        send[at : at + half, :] = joined_half(keep, came, half, half)
        at += half
    pass_small(small, came_x, keep_x.shape[0], total, send, at)


def step_joint(ids, keep, came, small, out, send, total):
    at = 0
    for half in JOINED_PARTS:
        out[at : at + half, :] = joined_half(keep, came, 2 * at, half)
        send[at : at + half, :] = joined_half(keep, came, 2 * at + half, half)
        at += half
    pass_small(small, came, 2 * at, total, send, at)


def small_columns(small, out):
    count = out.shape[0]
    for c in range(out.shape[1] // 128):
        out[:, c * 128 : (c + 1) * 128] = small[c * count : (c + 1) * count]


def early_end_a(ids, keep_1, keep_2, came_1, came_2, down, align, out):
    down[0:128, :] = jnp.transpose(added(keep_1, came_1, 0, 192))
    down[128:256, :] = jnp.transpose(added(keep_1, came_1, 192, 192))
    down[256:384, :] = jnp.transpose(added(keep_2, came_2, 0, 192))
    align[:, 0:128] = added(keep_1, came_1, 384, 96)
    align[:, 128:256] = added(keep_2, came_2, 192, 96)
    out[:, 0:128] = added(keep_2, came_2, 288, 96)
    out[:, 128:192] = added(keep_2, came_2, 384, 96)[:, 0:64]


def early_end_b(ids, keep, came, small, up, total):
    for c in range(6):
        up[:, c * 128 : (c + 1) * 128] = added(keep, came, c * 96, 96)
    count = small.shape[0]
    both = both_small(small[...], came[576 : 576 + 2 * count, :])
    small_columns(both, total)


def joined_end(ids, keep, came, small, out, total):
    start, at = 0, 0
    for part, size in enumerate(JOINED_SPLIT):
        rows = slice(start, start + size)
        for c in range(4):
            out[rows, c * 128 : (c + 1) * 128] = added(keep, came, at + c * size, size)
        out[rows, 512:576] = added(keep, came, at + 4 * size, size)[:, 0:64]
        start, at = start + size, at + 5 * size
    count = small.shape[0]
    both = both_small(small[...], came[at : at + 2 * count, :])
    small_columns(both, total)


def flip(value, axis, bit, peers, groups):
    pairs = []
    for b in range(peers):
        for g in range(groups):
            other = (b ^ bit, g) if axis == "batch" else (b, g ^ bit)
            pairs.append((b * groups + g, other[0] * groups + other[1]))
    return lax.ppermute(value, AXES, pairs)


def tie(value, *others):
    return lax.optimization_barrier((value,) + others)[0]


def tiled_blocks(matrix, row_parts, column_parts):
    r, c = matrix.shape
    shaped = matrix.reshape(row_parts, r // row_parts, column_parts, c // column_parts)
    return jnp.transpose(shaped, (0, 2, 1, 3)).reshape(
        row_parts * column_parts, r // row_parts, c // column_parts
    )


def scattered(left, right, peers, groups):
    matrix = lax.dot_general(left, right, (((0,), (0,)), ((), ())), preferred_element_type=F32)
    return lax.psum_scatter(
        tiled_blocks(matrix, peers, groups), AXES, scatter_dimension=0, tiled=True
    )[0]


class Traffic:
    def __init__(self, loads, flushes):
        self.loads, self.flushes, self.left = loads, flushes, {}

    def need(self, *which):
        for k in which:
            copy = self.loads.pop(k, None)
            if copy is not None:
                copy.wait()

    def ready(self, *which):
        for k in which:
            if k in self.flushes:
                self.left[k] = self.flushes.pop(k)
                self.left[k].start()

    def finish(self):
        self.need(*list(self.loads))
        self.ready(*list(self.flushes))
        for copy in self.left.values():
            copy.wait()


def call(kernel, name, grant, out_shape, scratch, ids, *args, far=(), kept=(), load=(), flush=(), lazy=False, cost=0.001):
    n_in, n_out, n_scratch = len(args), len(out_shape), len(scratch)
    in_hbm, out_hbm = set(far) | set(load), {-1 - k for k in far} | set(flush)
    outs = [pltpu.HBM(o.shape, o.dtype) if k in kept or k in out_hbm else o for k, o in enumerate(out_shape)]
    own = [pltpu.VMEM(args[k].shape, args[k].dtype) for k in load] + [pltpu.VMEM(out_shape[k].shape, out_shape[k].dtype) for k in flush]
    if own:
        own.append(pltpu.SemaphoreType.DMA((len(own),)))

    def body(ids, *refs):
        ins, made, rest = list(refs[:n_in]), list(refs[n_in : n_in + n_out]), refs[n_in + n_out :]
        buffers = rest[n_scratch:]
        loads, flushes = {}, {}
        for i, k in enumerate(load):
            loads[k] = pltpu.make_async_copy(ins[k], buffers[i], buffers[-1].at[i])
            loads[k].start()
            ins[k] = buffers[i]
        for i, k in enumerate(flush, len(load)):
            flushes[k] = pltpu.make_async_copy(buffers[i], made[k], buffers[-1].at[i])
            made[k] = buffers[i]
        traffic = Traffic(loads, flushes)
        if lazy:
            kernel(traffic, ids, *ins, *made, *rest[:n_scratch])
        else:
            traffic.need(*load)
            kernel(ids, *ins, *made, *rest[:n_scratch])
        traffic.finish()

    return pl.pallas_call(
        body,
        name=name,
        out_shape=outs,
        in_specs=[SMEM] + [HBM if k in in_hbm else VMEM for k in range(n_in)],
        out_specs=[HBM if k in out_hbm else VMEM for k in range(n_out)],
        scratch_shapes=list(scratch) + own,
        compiler_params=pltpu.CompilerParams(vmem_limit_bytes=grant * 1_000_000),
        cost_estimate=pl.CostEstimate(flops=int(cost * 10**9), bytes_accessed=1, transcendentals=0),
    )(ids, *(pltpu.with_memory_space_constraint(a, pltpu.HBM) if k in in_hbm else a for k, a in enumerate(args)))


def exchange(blocks, peers, groups):
    if len(blocks) == 1:
        shaped = blocks[0].reshape(peers, blocks[0].shape[0] // peers, blocks[0].shape[1])
        moved = lax.all_to_all(shaped, "batch", split_axis=0, concat_axis=0, tiled=True)
        return [moved.reshape(blocks[0].shape)]
    return [blocks[0]] + [flip(block, "batch", k, peers, groups) for k, block in zip(ORDER[1:], blocks[1:])]


def per_device(
    tokens, dest, seg_ids, cot_out, cot_align,
    ln1_gain, ln1_bias, w_qkv, q_bias, v_bias, w_out, out_bias,
    ln2_gain, ln2_bias, w_up, up_bias, w_down, down_bias,
    ln3_gain, ln3_bias, w_align, align_bias,
):
    rows, width = tokens.shape
    align = cot_align.shape[1]
    wide = w_up.shape[1]
    slots = seg_ids.shape[1]
    peers, groups = lax.axis_size("batch"), lax.axis_size("grp")
    capacity = slots // peers
    fast = peers == 8 and groups == 4 and (width, wide, align) == (768, 3072, 1024)
    blocks = 8 if fast else 1
    seg_col = seg_ids.reshape(slots, 1)
    line = lambda v: v.reshape(1, v.shape[0])
    shape = jax.ShapeDtypeStruct
    vmem = pltpu.VMEM
    dma = pltpu.SemaphoreType.DMA
    count = slots // CLIPMAX
    low = lambda c: shape((rows, c), BF16)
    flat = lambda n: shape((n, 128), BF16)
    move = lambda value, axis, bit: flip(value, axis, bit, peers, groups)
    b, g = lax.axis_index("batch"), lax.axis_index("grp")
    place_b = b ^ jnp.arange(8)
    place_b = (place_b >> 2) + (((place_b >> 1) & 1) << 1) + ((place_b & 1) << 2)
    place_g = g ^ jnp.arange(4)
    place_g = (place_g >> 1) + ((place_g & 1) << 1)
    ids = jnp.concatenate([jnp.stack([b, g]), place_b, place_g]).astype(jnp.int32)

    packed = call(
        functools.partial(pack_kernel, peers, capacity), "pack_tokens", 56,
        [shape((slots // blocks, width), BF16)] * blocks, [],
        ids, dest.reshape(1, rows), tokens, kept=tuple(range(blocks)), load=(1,),
    )
    packed = exchange(packed, peers, groups)

    in_slots = shape((slots, width), BF16)
    apart = [shape((slots // blocks, width), BF16)] * blocks
    made = call(
        functools.partial(attention_kernel, blocks), "attention", 56,
        apart + [shape((slots, 3 * width), BF16), in_slots, in_slots, shape((width // 128, count, 2 * CLIPMAX), F32)],
        [vmem((count, 3 * CLIPMAX, 2 * CLIPMAX), F32), vmem((128, slots), BF16), vmem((width, 3 * width), BF16),
         vmem((slots, 3 * width), BF16), vmem((slots, width), BF16), vmem((slots, width), BF16), dma((blocks,)), dma, dma((2,))],
        ids, *packed, seg_ids, seg_col, line(ln1_gain), line(ln1_bias), w_qkv, line(q_bias), line(v_bias),
        far=tuple(range(blocks)) + (blocks + 4,) + tuple(-1 - k for k in range(blocks + 2)),
        load=(blocks, blocks + 1), flush=(blocks + 2,), kept=(blocks + 3,), lazy=True,
    )
    ctx, (qkv, natural, a1, lse) = exchange(made[:blocks], peers, groups), made[blocks:]

    full = shape((rows, width), F32)
    extra = 12 * 16
    parts = lambda n: [flat(n * JOINED_PARTS[0]), flat(n * JOINED_PARTS[0] + more), flat(n * JOINED_PARTS[1]), flat(n * JOINED_PARTS[1])]
    both = sum(JOINED_PARTS)
    more = 6 * 8
    chain = lambda n: [flat(n * EARLY_PARTS[0] + extra)] + [flat(n * r) for r in EARLY_PARTS[1:]]
    held = lambda n: [flat(n * r) for r in EARLY_PARTS]
    small_early = shape((96, 128), F32)
    turned = shape((width, rows), BF16)
    y, al, g_packed, g_mid, hidden, gub, a2, a3, ctx_rows, gyb, gmb, small_0, *sent = call(
        functools.partial(rows_kernel, peers, capacity, blocks, fast), "rows", 46,
        [low(width), low(align), in_slots, full, low(wide), low(wide), low(width), low(width), low(width), low(width), low(width),
         shape((16, width), F32)] + ([shape((SENT, 256), BF16), shape((OWN, 256), BF16)] if fast else []),
        [vmem((rows, width), F32), vmem((rows, width), F32), vmem((rows, width), F32), vmem((rows, 128), F32), vmem((rows, wide), F32),
         vmem((rows, 512), F32), vmem((rows, 512), F32), vmem((rows, 512), BF16), vmem((rows, 512), BF16),
         vmem((2, 8, width), F32), vmem(w_out.shape, BF16), vmem(w_up.shape, BF16), vmem(w_down.shape, BF16),
         vmem(w_align.shape, BF16), dma((4,)), vmem((slots, width), BF16), dma((blocks,))] + ([vmem((width, rows), BF16)] * 2 if fast else []),
        ids, *ctx, tokens, dest, cot_out, cot_align,
        w_out, line(out_bias), line(ln2_gain), line(ln2_bias), w_up, line(up_bias), w_down, line(down_bias),
        line(ln3_gain), line(ln3_bias), w_align, line(align_bias),
        far=tuple(range(blocks)) + tuple(blocks + k for k in (4, 8, 10, 14)), load=(), flush=(0, 1, 2, 3, 4) + ((12, 13) if fast else ()), kept=(5, 6, 7, 8, 9, 10, 11), lazy=True,
    )
    (g_arrived,) = exchange([g_packed], peers, groups)

    if fast:
        sent, own = sent
        came = move(sent, "grp", 1)
        came_hidden = move(hidden, "grp", 1)
        routes = (
            (("grp", 2), ("batch", 2), ("batch", 1), ("batch", 4)),
            (("batch", 1), ("grp", 2), ("batch", 4), ("batch", 2)),
            (("batch", 2), ("batch", 1), ("grp", 2), ("batch", 4)),
        )
        go = lambda sends, k, which=(0, 1, 2): [move(send, *routes[p][k]) for send, p in zip(sends, which)]
        square = lambda n: vmem((n, rows), BF16)
        k0, s0, small_e = call(
            second_grads, "second_grads", 16, [held(8)[0], chain(8)[0], small_early],
            [square(768), square(768), square(1536), square(1536), square(96), square(96), dma((6,))],
            ids, sent, own, came,
            far=(0, 1, 2), flush=(0, 1), kept=(2,), lazy=True,
        )
        k1, s1, k2, s2 = call(
            first_grads, "first_grads", 20, [held(8)[1], held(8)[1], held(8)[2], held(8)[2]],
            [square(1536), square(1536), square(1024), square(1024), square(384), square(384),
             vmem((rows, wide), BF16), vmem((rows, wide), BF16), dma((8,))],
            ids, hidden, came_hidden, sent, own, tie(came, s0),
            far=(0, 1, 2, 3, 4), flush=(0, 1, 2, 3), lazy=True,
        )
        keeps, sends = [k0, k1, k2], [s0, s1, s2]
        cames = go(sends, 0)
        g_arrived = tie(g_arrived, s1)

    outs = [in_slots, shape((slots, 3 * width), BF16), shape((8, width // 2), F32)]
    turned = shape((width, slots), BF16)
    made = call(
        functools.partial(attention_back_kernel, fast), "attention_back", 28,
        outs + ([flat(16 * both + more), turned] if fast else []),
        [vmem((count, 3 * CLIPMAX, 2 * CLIPMAX), F32), vmem((128, slots), BF16), vmem((slots, 128), F32), vmem((slots, 128), F32),
         vmem((slots, width), F32), vmem((2, 8, width), F32), vmem((width, 3 * width), BF16), dma]
        + ([vmem((width, slots), BF16)] if fast else []),
        ids, g_arrived, natural, qkv, lse, a1, seg_ids, seg_col, line(ln1_gain), w_qkv,
        far=(8,), load=(1, 6, 2, 3, 4), flush=(0, 1, 4) if fast else (0,), lazy=True,
    )
    g_rows, g_joined, small_2 = made[:3]
    (g_back,) = exchange([g_rows], peers, groups)

    if fast:
        send, turned_c = made[3:]
        came = move(send, "grp", 1)
        small_shape = shape((24, 128), F32)

        def early_step(name, which, n, keeps, cames, small_e, before, cost, **more_of):
            count = len(which)
            first = which[0] == 0
            made = call(
                functools.partial(step_parts, count, 0 if first else None), name, 14,
                [held(n)[p] for p in which] + [chain(n)[p] for p in which] + ([small_early] if first else []), [],
                ids, *keeps, tie(cames[0], before), *cames[1:], *((small_e,) if first else ()), cost=cost, lazy=True, **more_of,
            )
            return list(made[:count]), list(made[count : 2 * count]), (made[-1] if first else small_e)

        both_, one_ = (1, 2), (0,)
        C1, CK, C2A, C2B, CA, C3A, C3B, CEA = 15,.001,3,.001,.001,4,.001,3
        keeps, sends, small_e = early_step("early_step_1", (0, 1, 2), 4, keeps, cames, small_e, send, C1, load=(0, 3, 6, 1, 4, 2, 5), flush=(0, 1, 2, 3, 4, 5))
        cames = go(sends, 1)
        kx3, sx3, ky3, sy3, small_j = call(
            joined_keep, "joined_keep", 12, parts(8) + [small_shape], [],
            ids, turned_c, g_joined, tie(came, sends[0]), small_2, load=(0, 1), cost=CK,
        )
        cx3, cy3 = move(sx3, "grp", 2), move(sy3, "batch", 1)
        keeps_a, sends_a, _ = early_step("early_step_2a", both_, 2, keeps[1:], cames[1:], None, sx3, C2A, load=(0, 1))
        cames_a = go(sends_a, 2, both_)
        keeps_b, sends_b, small_e = early_step("early_step_2b", one_, 2, keeps[:1], cames[:1], small_e, sends_a[0], C2B, load=(0,))
        cames_b = go(sends_b, 2, one_)
        kx3, sx3, ky3, sy3, small_j = call(
            step_apart, "joined_apart", 10, parts(4) + [small_shape], [],
            ids, kx3, tie(cx3, sends_b[0]), ky3, cy3, small_j, cost=CA,
        )
        cx3, cy3 = move(sx3, "batch", 1), move(sy3, "grp", 2)
        keeps_a, sends_a, _ = early_step("early_step_3a", both_, 1, keeps_a, cames_a, None, sx3, C3A)
        cames_a = go(sends_a, 3, both_)
        keeps_b, sends_b, small_e = early_step("early_step_3b", one_, 1, keeps_b, cames_b, small_e, sends_a[0], C3B)
        cames_b = go(sends_b, 3, one_)
        g_back = tie(g_back, sends_b[0])
        k3, s3, small_j = call(
            step_meet, "joined_meet", 10, [flat(2 * both), flat(2 * both + more), small_shape], [],
            ids, kx3, tie(cx3, sends_b[0]), ky3, cy3, small_j,
        )
        c3 = move(s3, "batch", 2)
        sum_down, sum_align, sum_out = call(
            early_end_a, "early_end_a", 10, [shape((384, 192), F32), shape((96, 256), F32), shape((96, 192), F32)], [],
            ids, *keeps_a, tie(cames_a[0], s3), cames_a[1], cost=CEA,
        )
        sum_up, small_e = call(
            early_end_b, "early_end_b", 10, [shape((96, 768), F32), shape((16, width), F32)], [],
            ids, *keeps_b, tie(cames_b[0], sum_out), small_e, cost=CEA,
        )
        k3, s3, small_j = call(
            step_joint, "joined_joint", 10, [flat(both), flat(both + more), small_shape], [],
            ids, k3, tie(c3, sum_up), small_j,
        )
        c3 = move(s3, "batch", 4)
        sum_qkv, small_j = call(
            joined_end, "joined_end", 10, [shape((96, 576), F32), shape((8, width // 2), F32)], [],
            ids, k3, c3, small_j,
        )
        small_0, small_2 = small_e, small_j
    else:
        sum_up, sum_align, sum_out, sum_down, sum_qkv = (
            scattered(a2, gub, peers, groups),
            scattered(a3, cot_align, peers, groups),
            scattered(ctx_rows, gmb, peers, groups),
            scattered(hidden, gyb, peers, groups),
            scattered(a1, g_joined, peers, groups),
        )
        small_0, small_2 = lax.psum((small_0, small_2), AXES)

    (grad_tokens,) = call(
        functools.partial(last_kernel, peers, capacity), "grad_tokens", 8, [low(width)], [],
        ids, g_back, dest, g_mid, load=(1, 2),
    )
    sum_align_bias = small_0[3:5].reshape(2 * width)[:align]
    sum_up_bias = small_0[11:15].reshape(4 * width)[:wide]
    late = [jnp.concatenate([small_2[k], small_2[4 + k]]) for k in range(4)]
    return (
        y, al, grad_tokens,
        late[0], late[1], sum_qkv, late[2], late[3],
        sum_out, small_0[10], small_0[8], small_0[9],
        sum_up, sum_up_bias, sum_down, small_0[2],
        small_0[0], small_0[1], sum_align, sum_align_bias,
    )


def solution(mesh):
    row, one = P(AXES, None), P()
    matrix = P("batch", "grp")
    return jax.shard_map(
        per_device,
        mesh=mesh,
        in_specs=(row,) * 5 + (one,) * 17,
        out_specs=(
            row, row, row, one, one, matrix, one, one, matrix, one,
            one, one, matrix, one, matrix, one, one, one, matrix, one,
        ),
        check_vma=False,
    )
```
